32 devices in a mesh: batch: 8 (over z, x), blk: 4 (over y, core).
Axes of the slice: x: 2, y: 2, z: 4, core: 2. Of those that a mesh axis runs over, the one named last changes fastest.
Arguments:
- inputs: bfloat16 [8, 2048, 1024], P('batch', 'blk'), may hold values from -6 to 6
- ln1_gain: float32 [1024], replicated, may hold values from 0.1 to 1.9
- ln1_bias: float32 [1024], replicated, may hold values from -1 to 1
- w_qkv: bfloat16 [1024, 3072], replicated, may hold values from -0.1875 to 0.1875
- bias_q: float32 [1024], replicated, may hold values from -1.5 to 1.5
- bias_v: float32 [1024], replicated, may hold values from -0.25 to 0.25
- w_out: bfloat16 [1024, 1024], replicated, may hold values from -2 to 2
- bias_out: float32 [1024], replicated, may hold values from -1 to 1
- ln2_gain: float32 [1024], replicated, may hold values from 0.1 to 1.9
- ln2_bias: float32 [1024], replicated, may hold values from -1 to 1
- w_up: bfloat16 [1024, 4096], replicated, may hold values from -0.1875 to 0.1875
- bias_up: float32 [4096], replicated, may hold values from -1.5 to 1.5
- w_down: bfloat16 [4096, 1024], replicated, may hold values from -0.09375 to 0.09375
- bias_down: float32 [1024], replicated, may hold values from -2.5 to 2.5
- lengths: int32 [8, 2, 3], P('batch'), may hold values from 1 to 640, as said below
- cotangent: bfloat16 [8, 2048, 1024], P('batch', 'blk'), may hold values from -6 to 6
Outputs:
- result: bfloat16 [8, 2048, 1024], P('batch', 'blk')
- grad_inputs: float32 [8, 2048, 1024], P('batch', 'blk')
- grad_ln1_gain: float32 [1024], P('batch')
- grad_ln1_bias: float32 [1024], P('batch')
- grad_w_qkv: float32 [1024, 3072], P('batch')
- grad_bias_q: float32 [1024], P('batch')
- grad_bias_v: float32 [1024], P('batch')
- grad_w_out: float32 [1024, 1024], P('batch')
- grad_bias_out: float32 [1024], P('batch')
- grad_ln2_gain: float32 [1024], P('batch')
- grad_ln2_bias: float32 [1024], P('batch')
- grad_w_up: float32 [1024, 4096], P('batch')
- grad_bias_up: float32 [4096], P('batch')
- grad_w_down: float32 [4096, 1024], P('batch')
- grad_bias_down: float32 [1024], P('batch')
The draws below stay inside these ranges and needn't reach their ends.
Inputs may be any that keep to these rules, and one draw needn't show every extreme that they name: lengths[r, u] gives utterance u of row r as (phonemes, prompt frames, target frames), packed in order from slot 0; phonemes number 1 to 128, prompt frames 1 to 256, target frames 1 to 640; slots after a row's last utterance are padding.
All inputs are finite; a program needn't handle non-finite values.
Results may differ from the reference program's by a relative error of at most 0.018.
Values may be sent and summed in bfloat16 or wider, within the bound.
No kernel may reach another device: no remote copies, remote signals or barrier semaphores. Data moves between devices by JAX's collectives and lax.ppermute only.
A program may use at most 192 MiB of HBM per device.

```python
import jax
import jax.numpy as jnp
from jax import lax

D = 1024
H = 16
HD = 64
FF = 4096
SLOTS = 2048
UTTS = 2
ROWS = 8


def draw_lengths(key, part):
    key_one, key_two, key_three, key_four = jax.random.split(jax.random.fold_in(key, 17), 4)
    phonemes = jax.random.randint(key_one, (ROWS, UTTS), 1, SLOTS // 16 + 1)
    prompts = jax.random.randint(key_two, (ROWS, UTTS), 1, SLOTS // 8 + 1)
    targets = jax.random.randint(key_three, (ROWS, UTTS), 1, 5 * SLOTS // 16 + 1)
    chosen_row = jax.random.randint(key_four, (), 0, ROWS)
    row_ids = jnp.arange(ROWS, dtype=jnp.int32)[:, None]
    utt_ids = jnp.arange(UTTS, dtype=jnp.int32)[None, :]
    targets = jnp.where((row_ids == chosen_row) & (utt_ids == 0), 5 * SLOTS // 16, targets)
    return jnp.stack([phonemes, prompts, targets], axis=2).astype(jnp.int32)


def shard_levels(stream_key, shape, cuts, low, high):
    level = 1.0
    for axis_at, shards_of in cuts:
        draws = jax.random.uniform(jax.random.fold_in(jax.random.fold_in(stream_key, 6), axis_at), (shards_of,), jnp.float32, low / len(cuts), high / len(cuts))
        level = level * jnp.repeat(jnp.exp(draws), shape[axis_at] // shards_of).reshape((-1,) + (1,) * (len(shape) - 1 - axis_at))
    return level


def gaussian(rng, shape, scale, reach, cuts=(), held_as=jnp.bfloat16):
    factor_of = shard_levels(rng, shape, cuts, -0.22, 0.18) if cuts else 1.0
    values = jax.random.normal(rng, shape, jnp.float32) * scale * factor_of
    return jnp.minimum(jnp.maximum(values, -reach), reach).astype(held_as)


def setup_inputs(seed: int = 0) -> dict:
    key_list = jax.random.split(jax.random.key(seed), 17)
    return {
        "inputs": gaussian(key_list[0], (ROWS, SLOTS, D), 1.0, 6.0, ((0, 8), (1, 4))),
        "ln1_gain": jnp.clip(1.0 + 0.18 * jax.random.normal(key_list[1], (D,), jnp.float32), 0.1, 1.9),
        "ln1_bias": gaussian(key_list[2], (D,), 0.2, 1.0, (), jnp.float32),
        "w_qkv": gaussian(key_list[3], (D, 3 * D), D ** -0.5, 0.1875),
        "bias_q": gaussian(key_list[4], (D,), 0.3, 1.5, (), jnp.float32),
        "bias_v": gaussian(key_list[5], (D,), 0.05, 0.25, (), jnp.float32),
        "w_out": gaussian(key_list[6], (D, D), (max(D // 128, 1)) ** -0.5, 2.0),
        "bias_out": gaussian(key_list[7], (D,), 0.2, 1.0, (), jnp.float32),
        "ln2_gain": jnp.clip(1.0 + 0.18 * jax.random.normal(key_list[8], (D,), jnp.float32), 0.1, 1.9),
        "ln2_bias": gaussian(key_list[9], (D,), 0.2, 1.0, (), jnp.float32),
        "w_up": gaussian(key_list[10], (D, FF), D ** -0.5, 0.1875),
        "bias_up": gaussian(key_list[11], (FF,), 0.3, 1.5, (), jnp.float32),
        "w_down": gaussian(key_list[12], (FF, D), FF ** -0.5, 0.09375),
        "bias_down": gaussian(key_list[13], (D,), 0.5, 2.5, (), jnp.float32),
        "lengths": draw_lengths(jax.random.fold_in(key_list[16], 71), 0),
        "cotangent": gaussian(key_list[15], (ROWS, SLOTS, D), 1.0, 6.0, ((0, 8), (1, 4))),
    }


epsilon = 1e-05
highest = lax.Precision.HIGHEST

@jax.custom_vjp
def low(v):
    return lax.optimization_barrier(v.astype(jnp.bfloat16)).astype(jnp.float32)

@jax.custom_vjp
def low_back(v):
    return v

def low_keep(v):
    return (low(v), None)

def low_pass(kept, grad):
    return (grad,)

def back_keep(v):
    return (v, None)

def back_low(kept, grad):
    return (low(grad),)
low.defvjp(low_keep, low_pass)
low_back.defvjp(back_keep, back_low)

def layer_norm(values, gain_vec, shift_vec):
    center = values - lax.optimization_barrier(jnp.mean(values, axis=-1, keepdims=True))
    spread = lax.optimization_barrier(jnp.mean(center * center, axis=-1, keepdims=True))
    return center * lax.rsqrt(spread + epsilon) * gain_vec + shift_vec

def piece_index(length_row, positions):
    piece_ends = jnp.cumsum(length_row.reshape(-1))
    return lax.optimization_barrier(jnp.sum((positions[:, None] >= piece_ends[None, :]).astype(jnp.int32), axis=1))

def visible(pos_query, piece_query, pos_key, piece_key, piece_count):
    both_live = (piece_query < piece_count) & (piece_key < piece_count)
    same_utt = piece_query // 3 == piece_key // 3
    seg_query = piece_query % 3
    seg_key = piece_key % 3
    in_order = (seg_key < seg_query) | (seg_key == seg_query) & ((seg_query < 2) | (pos_key <= pos_query))
    return (pos_query == pos_key) | both_live & same_utt & in_order

def layer_row(row_input, length_row, params):
    ln1_gain, ln1_bias, w_qkv, bias_q, bias_v, w_out, bias_out, ln2_gain, ln2_bias, w_up, bias_up, w_down, bias_down = params
    normed = low(layer_norm(row_input, ln1_gain, ln1_bias))
    projected = jnp.dot(normed, w_qkv, precision=highest)
    query_rows = low_back(low(projected[:, :D] + bias_q)).reshape(SLOTS, H, HD)
    key_rows = low_back(low(projected[:, D:2 * D])).reshape(SLOTS, H, HD)
    value_rows = low_back(low(projected[:, 2 * D:] + bias_v)).reshape(SLOTS, H, HD)
    positions = jnp.arange(SLOTS, dtype=jnp.int32)
    pieces = piece_index(length_row, positions)
    block_rows = min(512, SLOTS)
    score_scale = HD ** (-0.5)

    def attend(start):
        query_block = lax.dynamic_slice_in_dim(query_rows, start, block_rows, 0)
        pos_block = lax.dynamic_slice_in_dim(positions, start, block_rows, 0)
        piece_block = lax.dynamic_slice_in_dim(pieces, start, block_rows, 0)
        scores = low_back(jnp.einsum('fhd,lhd->hfl', query_block, key_rows, precision=highest) * score_scale)
        allowed = visible(pos_block[:, None], piece_block[:, None], positions[None, :], pieces[None, :], 3 * UTTS)
        scores = jnp.where(allowed[None], scores, -1e+30)
        weights = low(jax.nn.softmax(scores, axis=-1))
        return jnp.einsum('hfl,lhd->fhd', weights, value_rows, precision=highest).reshape(block_rows, D)
    starts = jnp.arange(SLOTS // block_rows, dtype=jnp.int32) * block_rows
    context = lax.map(jax.checkpoint(attend), starts).reshape(SLOTS, D)
    context = low_back(low(context))
    branch = low_back(jnp.dot(context, w_out, precision=highest) + bias_out)
    middle = row_input + branch
    normed_two = low(layer_norm(middle, ln2_gain, ln2_bias))
    hidden = low_back(jnp.dot(normed_two, w_up, precision=highest) + bias_up)
    active = low(jax.nn.gelu(hidden, approximate=False))
    return middle + low_back(jnp.dot(active, w_down, precision=highest) + bias_down)

def reference(inputs, ln1_gain, ln1_bias, w_qkv, bias_q, bias_v, w_out, bias_out, ln2_gain, ln2_bias, w_up, bias_up, w_down, bias_down, lengths, cotangent):
    params = tuple((tensor.astype(jnp.float32) for tensor in (ln1_gain, ln1_bias, w_qkv, bias_q, bias_v, w_out, bias_out, ln2_gain, ln2_bias, w_up, bias_up, w_down, bias_down)))

    def forward(whole_input, *weights):

        def one_row(packed):
            row_input, length_row = packed
            return layer_row(row_input, length_row, weights)
        return lax.map(jax.checkpoint(one_row), (whole_input, lengths))
    output, pullback = jax.vjp(forward, inputs.astype(jnp.float32), *params)
    grads = pullback(cotangent.astype(jnp.float32))
    return (output.astype(jnp.bfloat16), grads[0], grads[1], grads[2], grads[3], grads[4], grads[5], grads[6], grads[7], grads[8], grads[9], grads[10], grads[11], grads[12], grads[13])
```

```python
import functools

import jax
import jax.numpy as jnp
from jax import lax
from jax.experimental import pallas as pl
from jax.experimental.pallas import tpu as pltpu
from jax.sharding import Mesh
from jax.sharding import PartitionSpec as P

D = 1024
H = 16
HD = 64
EPS = 1e-05
NEG = -1e30
BF = jnp.bfloat16
F32 = jnp.float32


def layer_norm(values, gain_vec, shift_vec):
    center = values - jnp.mean(values, axis=-1, keepdims=True)
    spread = jnp.mean(center * center, axis=-1, keepdims=True)
    return center * lax.rsqrt(spread + EPS) * gain_vec + shift_vec


def dot(a, b):
    return jnp.dot(a, b, preferred_element_type=F32)


def dot_tn(a, b):
    return lax.dot_general(a, b, (((0,), (0,)), ((), ())), preferred_element_type=F32)


def dot_nt(a, b):
    return lax.dot_general(a, b, (((1,), (1,)), ((), ())), preferred_element_type=F32)


def half(a, h):
    a = a[:, (h // 2) * 2 * HD : (h // 2 + 1) * 2 * HD]
    lane = lax.broadcasted_iota(jnp.int32, a.shape, 1)
    zero = jnp.zeros_like(a)
    return jnp.where(lane < HD, a, zero) if h % 2 == 0 else jnp.where(lane < HD, zero, a)


def pair(a, h):
    return a[:, (h // 2) * 2 * HD : (h // 2 + 1) * 2 * HD]


def fwd_kernel(T, HG, lst, cnt, base, q_ref, k_ref, v_ref, lo_ref, hi_ref, ctx_ref, lse_ref):
    nq = q_ref.shape[0] // T
    row = lax.broadcasted_iota(jnp.int32, (T, T), 0)

    @pl.loop(0, nq)
    def _(qt):
        at = pl.ds(pl.multiple_of(qt * T, T), T)
        q = q_ref[at, :]
        qh = [half(q, h) for h in range(HG)]
        lo, hi = lo_ref[:, at], hi_ref[:, at]

        def body(n, carry):
            t = lst[qt, n]
            ks = pl.ds(pl.multiple_of(t * T, T), T)
            k, v = k_ref[ks, :], v_ref[ks, :].T
            vis = (row >= lo - base[t]) & (row < hi - base[t])
            raw = [dot_nt(pair(k, h), qh[h]) for h in range(HG)]
            out = []
            for h in range(HG):
                m, l, acc = carry[h]
                s = jnp.where(vis, raw[h], NEG)
                mn = jnp.maximum(m, jnp.max(s, axis=0, keepdims=True))
                a = jnp.exp(m - mn)
                p = jnp.exp(s - mn)
                l = a * l + jnp.sum(p, axis=0, keepdims=True)
                acc = acc * a + dot(v[h * HD : (h + 1) * HD, :], p.astype(BF))
                out.append((mn, l, acc))
            return tuple(out)

        one = (jnp.full((1, T), NEG, F32), jnp.zeros((1, T), F32), jnp.zeros((HD, T), F32))
        res = lax.fori_loop(0, cnt[qt], body, (one,) * HG)
        ctx_ref[at, :] = jnp.concatenate([r[2] / r[1] for r in res], axis=0).T.astype(BF)
        lse_ref[:, at] = jnp.concatenate([r[0] + jnp.log(r[1]) for r in res], axis=0)


def bwd_kernel(T, HG, lst, cnt, base, q_ref, k_ref, v_ref, ctx_ref, do_ref, lse_ref, lo_ref, hi_ref, out_ref, dqt, dl):
    n_tiles = q_ref.shape[0] // T
    W = HG * HD
    row = lax.broadcasted_iota(jnp.int32, (T, T), 0)
    lane = lax.broadcasted_iota(jnp.int32, (T, 2 * HD), 1)
    dqt[...] = jnp.zeros_like(dqt)

    @pl.loop(0, n_tiles)
    def _(t):
        at = pl.ds(pl.multiple_of(t * T, T), T)
        prod = (do_ref[at, :].astype(F32) * ctx_ref[at, :].astype(F32)).T
        dl[:, at] = jnp.concatenate([jnp.sum(prod[h * HD : (h + 1) * HD], axis=0, keepdims=True) for h in range(HG)], axis=0)

    @pl.loop(0, n_tiles)
    def _(kt):
        ks = pl.ds(pl.multiple_of(kt * T, T), T)
        k, v = k_ref[ks, :], v_ref[ks, :]
        kT = k.T
        kh, vh = [half(k, h) for h in range(HG)], [half(v, h) for h in range(HG)]

        def body(n, carry):
            at = pl.ds(pl.multiple_of(lst[kt, n] * T, T), T)
            q, do = q_ref[at, :], do_ref[at, :]
            vis = (row >= lo_ref[:, at] - base[kt]) & (row < hi_ref[:, at] - base[kt])
            raw = [dot_nt(kh[h], pair(q, h)) for h in range(HG)]
            dps = [dot_nt(vh[h], pair(do, h)) for h in range(HG)]
            out = []
            for h in range(HG):
                p = jnp.exp(jnp.where(vis, raw[h], NEG) - lse_ref[h : h + 1, at])
                ds = (p * (dps[h] - dl[h : h + 1, at])).astype(BF)
                out.append((carry[h][0] + dot(ds, pair(q, h)), carry[h][1] + dot(p.astype(BF), pair(do, h))))
                dqt[h * HD : (h + 1) * HD, at] += dot(kT[h * HD : (h + 1) * HD, :], ds)
            return tuple(out)

        one = (jnp.zeros((T, 2 * HD), F32), jnp.zeros((T, 2 * HD), F32))
        res = lax.fori_loop(0, cnt[kt], body, (one,) * HG)
        for p in range(HG // 2):
            cols = slice(p * 2 * HD, (p + 1) * 2 * HD)
            a, b = res[2 * p], res[2 * p + 1]
            out_ref[ks, W + cols.start : W + cols.stop] = jnp.where(lane < HD, a[0], b[0]).astype(BF)
            out_ref[ks, 2 * W + cols.start : 2 * W + cols.stop] = jnp.where(lane < HD, a[1], b[1]).astype(BF)

    @pl.loop(0, n_tiles)
    def _(t):
        at = pl.ds(pl.multiple_of(t * T, T), T)
        out_ref[at, :W] = (dqt[:, at].T * HD**-0.5).astype(BF)


def attend(kernel, scalars, ins, outs, scratch, flops):
    def spec(shape, cols):
        if cols is None:
            return pl.BlockSpec(shape, lambda i, *_: (0,) * len(shape))
        return pl.BlockSpec((shape[0], cols[0]), lambda i, *_: (0, cols[1]))

    size = sum(a.size * a.dtype.itemsize for a, _ in ins) + sum(o.size * o.dtype.itemsize for o in outs)
    return pl.pallas_call(
        kernel,
        out_shape=outs,
        grid_spec=pltpu.PrefetchScalarGridSpec(
            num_scalar_prefetch=len(scalars),
            grid=(1,),
            in_specs=[spec(a.shape, cols) for a, cols in ins],
            out_specs=[spec(o.shape, None) for o in outs],
            scratch_shapes=scratch,
        ),
        compiler_params=pltpu.CompilerParams(vmem_limit_bytes=40 << 20),
        cost_estimate=pl.CostEstimate(flops=flops, bytes_accessed=size, transcendentals=0),
    )(*scalars, *[a for a, _ in ins])


def tile_list(active):
    m = active.shape[1]
    hit = active.astype(jnp.int32)
    upto = jnp.tril(jnp.ones((m, m), jnp.int32))
    rank = jnp.sum(hit[:, None, :] * upto[None], axis=2) - 1
    ids = jnp.arange(m, dtype=jnp.int32)
    here = (rank[:, :, None] == ids[None, None, :]) & active[:, :, None]
    return jnp.sum(jnp.where(here, ids[None, :, None], 0), axis=1), jnp.sum(hit, axis=1)


def after(vals, deps):
    return lax.optimization_barrier((vals, deps))[0]


def shards(Z, X, Y, inputs, ln1_gain, ln1_bias, w_qkv, bias_q, bias_v, w_out, bias_out, ln2_gain, ln2_bias,
           w_up, bias_up, w_down, bias_down, lengths, cotangent):
    F = inputs.shape[1]
    K = 2 * Y
    S = F * K
    T = min(256, F)
    W = D // K
    HG = H // K
    B = Z * X
    zi, xi, y, c = (lax.axis_index(n) for n in ("z", "x", "y", "c"))
    group = y * 2 + c
    sds = jax.ShapeDtypeStruct

    def shift(v, axis, n, s):
        return lax.ppermute(v, axis, [(i, (i + s) % n) for i in range(n)])

    def mate(v):
        return lax.ppermute(v, "c", [(0, 1), (1, 0)])

    rel = [(s, d) for s in range(Y) for d in range(2)]

    def hop(v, s, d):
        pairs = [(yy * 2 + cc, ((yy + s) % Y) * 2 + (cc ^ d)) for yy in range(Y) for cc in range(2)]
        return lax.ppermute(v, ("y", "c"), pairs)

    def flip(d):
        return c if d == 0 else 1 - c

    blocks = jnp.stack([((y - s) % Y) * 2 + flip(d) for s, d in rel])
    ends = jnp.cumsum(lengths.reshape(-1))
    pos = (blocks[:, None] * F + jnp.arange(F, dtype=jnp.int32)[None]).reshape(1, S)
    piece = jnp.sum((pos >= ends[:, None]).astype(jnp.int32), axis=0, keepdims=True)
    pieces = ends.shape[0]
    starts = jnp.concatenate([jnp.zeros((1,), ends.dtype), ends[:-1]])

    def look(table, idx):
        return jnp.sum(jnp.where(idx == jnp.arange(pieces)[:, None], table[:, None], 0), axis=0, keepdims=True)

    pad = piece >= pieces
    lo = jnp.where(pad, pos, look(starts, (piece // 3) * 3)).astype(jnp.int32)
    hi = jnp.where(pad | (piece % 3 == 2), pos + 1, look(ends, piece)).astype(jnp.int32)
    base = pos[0, ::T].astype(jnp.int32)
    qlo = jnp.min(lo.reshape(S // T, T), axis=1)
    qhi = jnp.max(hi.reshape(S // T, T), axis=1)
    active = (base[None, :] < qhi[:, None]) & (base[None, :] + T > qlo[:, None])
    lst_q, cnt_q = tile_list(active)
    lst_k, cnt_k = tile_list(active.T)

    x_own = inputs.reshape(F, D)
    up = cotangent.reshape(F, D)
    flat_in = x_own.astype(F32)
    h1 = layer_norm(flat_in, ln1_gain, ln1_bias).astype(BF)
    got = [h1, mate(h1)]
    far = [shift(h1, "y", Y, s) for s in range(1, Y)]

    def cols_of(w, g):
        return [lax.dynamic_slice_in_dim(w, part * D + g * W, W, w.ndim - 1) for part in range(3)]

    w_g = jnp.concatenate(cols_of(w_qkv, group), axis=1)
    b_g = jnp.concatenate([lax.dynamic_slice_in_dim(bias_q, group * W, W, 0), jnp.zeros((W,), F32),
                           lax.dynamic_slice_in_dim(bias_v, group * W, W, 0)])
    sc_g = jnp.where(jnp.arange(3 * W) < W, HD**-0.5, 1.0).astype(BF)
    dg = dot_nt(after(up, h1), w_down).astype(BF)
    for r in far:
        got += [r, mate(r)]
    h_all = jnp.concatenate(got, axis=0)
    h_all, dg = lax.optimization_barrier((h_all, dg))
    qkv = (dot(h_all, w_g) + b_g).astype(BF) * sc_g
    lse_shape = sds((HG, S), F32)
    dense = S * S * W * 2 // 4
    ctx_g, lse = attend(
        functools.partial(fwd_kernel, T, HG), (lst_q, cnt_q, base),
        [(qkv, (W, 0)), (qkv, (W, 1)), (qkv, (W, 2)), (lo, None), (hi, None)],
        [sds((S, W), BF), lse_shape], [], 2 * dense)

    mine = [ctx_g[:F]] + [hop(ctx_g[(2 * s + d) * F : (2 * s + d + 1) * F], -s, d) for s, d in rel[1:]]
    mine = jnp.stack(mine)
    ctx = jnp.concatenate(
        [lax.dynamic_index_in_dim(mine, ((yy - y) % Y) * 2 + (cc ^ c), 0, keepdims=False)
         for yy in range(Y) for cc in range(2)], axis=1)
    middle = flat_in + (dot(ctx, w_out) + bias_out)
    h2 = layer_norm(middle, ln2_gain, ln2_bias).astype(BF)
    hidden = dot(h2, w_up) + bias_up
    act, gelu_back = jax.vjp(lambda t: jax.nn.gelu(t, approximate=False), hidden)
    act = act.astype(BF)
    du = gelu_back(dg.astype(F32))[0].astype(BF)

    def scatter(parts, axis, n, me):
        sent = [shift(lax.dynamic_index_in_dim(parts, (me + s) % n, 0, keepdims=False), axis, n, s) for s in range(1, n)]
        own = lax.dynamic_index_in_dim(parts, me, 0, keepdims=False).astype(F32)
        return sum((r.astype(F32) for r in sent), own).astype(BF)

    def give_c(a, b):
        n = b.shape[1] // 2
        return dot_tn(a, lax.dynamic_slice_in_dim(b, (1 - c) * n, n, 1)).astype(BF)

    def keep_c(a, b, got):
        n = b.shape[1] // 2
        return (dot_tn(a, lax.dynamic_slice_in_dim(b, c * n, n, 1)) + got.astype(F32)).astype(BF)

    def blocks_of(g):
        return g.reshape(Z, X, g.shape[0] // B, g.shape[1])

    def over_y(g):
        n = g.shape[-1] // Y
        return scatter(jnp.stack([g[..., i * n : (i + 1) * n] for i in range(Y)]), "y", Y, y)

    def over_x(g):
        return scatter(jnp.moveaxis(g, 1, 0), "x", X, xi)[:, None]

    def over_z(g):
        return scatter(g, "z", Z, zi)[None]

    def everywhere(g):
        two = jnp.stack([g, mate(g)])
        all_ = jnp.concatenate([two] + [shift(two, "y", Y, s) for s in range(1, Y)])
        return [[lax.dynamic_index_in_dim(all_, ((y - yy) % Y) * 2 + (cc ^ c), 0, keepdims=False) for cc in range(2)]
                for yy in range(Y)]

    def spread(g):
        e = everywhere(g)
        return jnp.concatenate([e[yy][cc] for cc in range(2) for yy in range(Y)], axis=1).astype(F32)

    down_give = give_c(act, up)
    down_got = mate(down_give)
    dh2 = dot_nt(after(du, down_give), w_up)
    _, norm_back_two = jax.vjp(layer_norm, middle, ln2_gain, ln2_bias)
    dmid, g_ln2g, g_ln2b = norm_back_two(dh2)
    dy1 = up.astype(F32) + dmid
    da = dy1.astype(BF)
    dctx = dot_nt(da, w_out).astype(BF)

    def heads_of(s, d):
        return lax.dynamic_slice_in_dim(dctx, (((y + s) % Y) * 2 + flip(d)) * W, W, 1)

    do_g = jnp.concatenate([heads_of(0, 0)] + [hop(heads_of(s, d), s, d) for s, d in rel[1:]], axis=0)

    act, up_, h2, du, ctx_ = after((act, up, h2, du, ctx), dctx)
    h_down = keep_c(act, up_, down_got)
    up_give = give_c(h2, du)
    up_got = mate(up_give)
    out_give = give_c(ctx_, da)
    out_got = mate(out_give)
    h_out = keep_c(ctx_, da, out_got)
    h_up = keep_c(h2, du, up_got)
    result = (middle + (dot(act, w_down) + bias_down)).astype(BF)
    one = jnp.concatenate([blocks_of(h_down).reshape(Z, X, -1, D // 2), blocks_of(h_out)], axis=2)
    two = blocks_of(h_up)
    do_g = after(do_g, (result, h_up, h_out))

    (dqkv,) = attend(
        functools.partial(bwd_kernel, T, HG), (lst_k, cnt_k, base),
        [(qkv, (W, 0)), (qkv, (W, 1)), (qkv, (W, 2)), (ctx_g, None), (do_g, None), (lse, None), (lo, None), (hi, None)],
        [sds((S, 3 * W), BF)], [pltpu.VMEM((W, S), F32), pltpu.VMEM((HG, S), F32)], 5 * dense)
    g_qkv = dot_tn(h_all, dqkv).astype(BF)
    three = blocks_of(g_qkv)

    part = dot_nt(after(dqkv, g_qkv), w_g).astype(BF).reshape(Y, 2, F, D)
    part = part[:, 0].astype(F32) + mate(part[:, 1]).astype(F32)
    far = [shift(part[s].astype(BF), "y", Y, -s) for s in range(1, Y)]
    dh1 = sum((r.astype(F32) for r in far), part[0])
    _, norm_back_one = jax.vjp(layer_norm, flat_in, ln1_gain, ln1_bias)
    dx, g_ln1g, g_ln1b = norm_back_one(dh1)
    grad_inputs = (dy1 + dx).reshape(1, F, D)

    one = over_z(over_x(over_y(one)))[0, 0]
    two = over_y(over_z(over_x(two)))[0, 0]
    three = over_z(over_x(three))[0, 0]
    ra = w_down.shape[0] // B
    one = spread(one)
    g_w_down, g_w_out = one[:ra], one[ra:]
    g_w_up = spread(two)
    e = everywhere(three)
    g_w_qkv = jnp.concatenate([e[yy][cc][:, p * W : (p + 1) * W] for p in range(3) for yy in range(Y) for cc in range(2)],
                              axis=1).astype(F32)

    def total(v):
        return jnp.sum(v.astype(F32), axis=0)

    def place(v):
        return lax.dynamic_update_slice_in_dim(jnp.zeros((D,), F32), v, group * W, 0)

    cols = total(dqkv)
    vecs = [g_ln1g, g_ln1b, place(cols[:W]), place(cols[2 * W :]), total(da), g_ln2g, g_ln2b, total(du), total(up)]
    flat = jnp.concatenate([v.reshape(B, -1) for v in vecs], axis=1)
    flat = flat + mate(flat)
    flat = sum((shift(flat, "y", Y, s) for s in range(1, Y)), flat)

    def scatter32(parts, axis, n, me):
        sent = [shift(lax.dynamic_index_in_dim(parts, (me + s) % n, 0, keepdims=False), axis, n, s) for s in range(1, n)]
        return sum(sent, lax.dynamic_index_in_dim(parts, me, 0, keepdims=False))

    flat = scatter32(jnp.moveaxis(flat.reshape(Z, X, -1), 1, 0), "x", X, xi)
    flat = scatter32(flat, "z", Z, zi)
    out, at = [], 0
    for v in vecs:
        n = v.shape[0] // B
        out.append(flat[at : at + n])
        at += n
    g_ln1g, g_ln1b, g_bq, g_bv, g_bo, g_ln2g, g_ln2b, g_bu, g_bd = out
    return (result.reshape(1, F, D), grad_inputs, g_ln1g, g_ln1b, g_w_qkv, g_bq, g_bv, g_w_out, g_bo, g_ln2g, g_ln2b,
            g_w_up, g_bu, g_w_down, g_bd)


def solution(mesh):
    batch, blk = mesh.shape["batch"], mesh.shape["blk"]
    Y = blk // 2
    X = Y if batch % Y == 0 else 1
    Z = batch // X
    fine = Mesh(mesh.devices.reshape(Z, X, Y, 2), ("z", "x", "y", "c"))
    rows, slots = ("z", "x"), ("y", "c")
    act = P(rows, slots, None)
    flat, mat = P(rows), P(rows, None)
    return jax.shard_map(
        functools.partial(shards, Z, X, Y),
        mesh=fine,
        in_specs=(act,) + (P(),) * 13 + (P(rows, None, None), act),
        out_specs=(act, act, flat, flat, mat, flat, flat, mat, flat, flat, flat, mat, flat, mat, flat),
        check_vma=False,
    )
```

```python
import functools

import jax
import jax.numpy as jnp
from jax import lax
from jax.experimental import pallas as pl
from jax.experimental.pallas import tpu as pltpu
from jax.sharding import Mesh
from jax.sharding import PartitionSpec as P

D = 1024
H = 16
HD = 64
EPS = 1e-05
NEG = -1e30
BF = jnp.bfloat16
F32 = jnp.float32


def layer_norm(values, gain_vec, shift_vec):
    center = values - jnp.mean(values, axis=-1, keepdims=True)
    spread = jnp.mean(center * center, axis=-1, keepdims=True)
    return center * lax.rsqrt(spread + EPS) * gain_vec + shift_vec


def dot(a, b):
    return jnp.dot(a, b, preferred_element_type=F32)


def dot_tn(a, b):
    return lax.dot_general(a, b, (((0,), (0,)), ((), ())), preferred_element_type=F32)


def dot_nt(a, b):
    return lax.dot_general(a, b, (((1,), (1,)), ((), ())), preferred_element_type=F32)


def half(a, h):
    a = a[:, (h // 2) * 2 * HD : (h // 2 + 1) * 2 * HD]
    lane = lax.broadcasted_iota(jnp.int32, a.shape, 1)
    zero = jnp.zeros_like(a)
    return jnp.where(lane < HD, a, zero) if h % 2 == 0 else jnp.where(lane < HD, zero, a)


def pair(a, h):
    return a[:, (h // 2) * 2 * HD : (h // 2 + 1) * 2 * HD]


def fwd_kernel(T, HG, lst, cnt, base, q_ref, k_ref, v_ref, lo_ref, hi_ref, ctx_ref, lse_ref):
    nq = q_ref.shape[0] // T
    row = lax.broadcasted_iota(jnp.int32, (T, T), 0)

    @pl.loop(0, nq)
    def _(qt):
        at = pl.ds(pl.multiple_of(qt * T, T), T)
        q = q_ref[at, :]
        qh = [half(q, h) for h in range(HG)]
        lo, hi = lo_ref[:, at], hi_ref[:, at]

        def body(n, carry):
            t = lst[qt, n]
            ks = pl.ds(pl.multiple_of(t * T, T), T)
            k, v = k_ref[ks, :], v_ref[ks, :].T
            vis = (row >= lo - base[t]) & (row < hi - base[t])
            raw = [dot_nt(pair(k, h), qh[h]) for h in range(HG)]
            out = []
            for h in range(HG):
                m, l, acc = carry[h]
                s = jnp.where(vis, raw[h], NEG)
                mn = jnp.maximum(m, jnp.max(s, axis=0, keepdims=True))
                a = jnp.exp(m - mn)
                p = jnp.exp(s - mn)
                l = a * l + jnp.sum(p, axis=0, keepdims=True)
                acc = acc * a + dot(v[h * HD : (h + 1) * HD, :], p.astype(BF))
                out.append((mn, l, acc))
            return tuple(out)

        one = (jnp.full((1, T), NEG, F32), jnp.zeros((1, T), F32), jnp.zeros((HD, T), F32))
        res = lax.fori_loop(0, cnt[qt], body, (one,) * HG)
        ctx_ref[at, :] = jnp.concatenate([r[2] / r[1] for r in res], axis=0).T.astype(BF)
        lse_ref[:, at] = jnp.concatenate([r[0] + jnp.log(r[1]) for r in res], axis=0)


def bwd_kernel(T, HG, lst, cnt, base, q_ref, k_ref, v_ref, ctx_ref, do_ref, lse_ref, lo_ref, hi_ref, out_ref, dqt, dl):
    n_tiles = q_ref.shape[0] // T
    W = HG * HD
    row = lax.broadcasted_iota(jnp.int32, (T, T), 0)
    lane = lax.broadcasted_iota(jnp.int32, (T, 2 * HD), 1)
    dqt[...] = jnp.zeros_like(dqt)

    @pl.loop(0, n_tiles)
    def _(t):
        at = pl.ds(pl.multiple_of(t * T, T), T)
        prod = (do_ref[at, :].astype(F32) * ctx_ref[at, :].astype(F32)).T
        dl[:, at] = jnp.concatenate([jnp.sum(prod[h * HD : (h + 1) * HD], axis=0, keepdims=True) for h in range(HG)], axis=0)

    @pl.loop(0, n_tiles)
    def _(kt):
        ks = pl.ds(pl.multiple_of(kt * T, T), T)
        k, v = k_ref[ks, :], v_ref[ks, :]
        kT = k.T
        kh, vh = [half(k, h) for h in range(HG)], [half(v, h) for h in range(HG)]

        def body(n, carry):
            at = pl.ds(pl.multiple_of(lst[kt, n] * T, T), T)
            q, do = q_ref[at, :], do_ref[at, :]
            vis = (row >= lo_ref[:, at] - base[kt]) & (row < hi_ref[:, at] - base[kt])
            raw = [dot_nt(kh[h], pair(q, h)) for h in range(HG)]
            dps = [dot_nt(vh[h], pair(do, h)) for h in range(HG)]
            out = []
            for h in range(HG):
                p = jnp.exp(jnp.where(vis, raw[h], NEG) - lse_ref[h : h + 1, at])
                ds = (p * (dps[h] - dl[h : h + 1, at])).astype(BF)
                out.append((carry[h][0] + dot(ds, pair(q, h)), carry[h][1] + dot(p.astype(BF), pair(do, h))))
                dqt[h * HD : (h + 1) * HD, at] += dot(kT[h * HD : (h + 1) * HD, :], ds)
            return tuple(out)

        one = (jnp.zeros((T, 2 * HD), F32), jnp.zeros((T, 2 * HD), F32))
        res = lax.fori_loop(0, cnt[kt], body, (one,) * HG)
        for p in range(HG // 2):
            cols = slice(p * 2 * HD, (p + 1) * 2 * HD)
            a, b = res[2 * p], res[2 * p + 1]
            out_ref[ks, W + cols.start : W + cols.stop] = jnp.where(lane < HD, a[0], b[0]).astype(BF)
            out_ref[ks, 2 * W + cols.start : 2 * W + cols.stop] = jnp.where(lane < HD, a[1], b[1]).astype(BF)

    @pl.loop(0, n_tiles)
    def _(t):
        at = pl.ds(pl.multiple_of(t * T, T), T)
        out_ref[at, :W] = (dqt[:, at].T * HD**-0.5).astype(BF)


def attend(kernel, scalars, ins, outs, scratch, flops):
    def spec(shape, cols):
        if cols is None:
            return pl.BlockSpec(shape, lambda i, *_: (0,) * len(shape))
        return pl.BlockSpec((shape[0], cols[0]), lambda i, *_: (0, cols[1]))

    size = sum(a.size * a.dtype.itemsize for a, _ in ins) + sum(o.size * o.dtype.itemsize for o in outs)
    return pl.pallas_call(
        kernel,
        out_shape=outs,
        grid_spec=pltpu.PrefetchScalarGridSpec(
            num_scalar_prefetch=len(scalars),
            grid=(1,),
            in_specs=[spec(a.shape, cols) for a, cols in ins],
            out_specs=[spec(o.shape, None) for o in outs],
            scratch_shapes=scratch,
        ),
        compiler_params=pltpu.CompilerParams(vmem_limit_bytes=40 << 20),
        cost_estimate=pl.CostEstimate(flops=flops, bytes_accessed=size, transcendentals=0),
    )(*scalars, *[a for a, _ in ins])


def grid_call(kernel, grid, scalars, ins, outs, flops, scratch=(), aliases=None, vmem=44):
    def spec(block, index):
        return pl.BlockSpec(memory_space=pl.ANY) if block is None else pl.BlockSpec(block, index)

    size = sum(a.size * a.dtype.itemsize for a, b, _ in ins if b is not None)
    size += sum(o.size * o.dtype.itemsize for o, _, _ in outs)
    return pl.pallas_call(
        kernel,
        out_shape=[o for o, _, _ in outs],
        grid_spec=pltpu.PrefetchScalarGridSpec(
            num_scalar_prefetch=len(scalars),
            grid=grid,
            in_specs=[spec(b, m) for _, b, m in ins],
            out_specs=[spec(b, m) for _, b, m in outs],
            scratch_shapes=list(scratch),
        ),
        input_output_aliases=aliases or {},
        compiler_params=pltpu.CompilerParams(vmem_limit_bytes=vmem << 20),
        cost_estimate=pl.CostEstimate(flops=flops, bytes_accessed=size, transcendentals=0),
    )(*scalars, *[a for a, _, _ in ins])


def whole(a):
    return a.shape, lambda *_: (0,) * len(a.shape)


def centred(x):
    x = x.astype(F32)
    center = x - jnp.mean(x, axis=-1, keepdims=True)
    spread = jnp.mean(center * center, axis=-1, keepdims=True)
    return center * lax.rsqrt(spread + EPS)


def qkv_kernel(x_ref, g_ref, b_ref, w_ref, bias_ref, sc_ref, *refs):
    h_ref, o_ref = refs[-2:]
    h = (centred(x_ref[...]) * g_ref[...] + b_ref[...]).astype(BF)
    h_ref[...] = h
    o = (dot(h, w_ref[...]) + bias_ref[...]).astype(BF)
    o_ref[...] = (o.astype(F32) * sc_ref[...]).astype(BF)


def qkv_call(x, g, b, w, bias, sc, r, blocks, held):
    F, n = x.shape[0], w.shape[1]
    TR = min(256, F)
    per = F // TR
    row = lambda i: (i, 0)
    to = lambda i: (r * per + i, 0)
    ins = [(x, (TR, D), row)] + [(v, *whole(v)) for v in (g, b, w, bias, sc)]
    shapes = [jax.ShapeDtypeStruct((blocks * F, D), BF), jax.ShapeDtypeStruct((blocks * F, n), BF)]
    aliases = {}
    if held is not None:
        ins += [(held[0], None, None), (held[1], None, None)]
        aliases = {6: 0, 7: 1}
    return grid_call(qkv_kernel, (per,), (), ins, [(shapes[0], (TR, D), to), (shapes[1], (TR, n), to)],
                     2 * F * D * n, aliases=aliases)


def mlp_kernel(sub, h_ref, w_ref, b_ref, dg_ref, act_ref, du_ref, dh_ref, bu_ref):
    rows = h_ref.shape[0]

    @pl.when(pl.program_id(0) == 0)
    def _():
        dh_ref[...] = jnp.zeros_like(dh_ref)

    bu = jnp.zeros(bu_ref.shape, F32)
    for r in range(0, rows, sub):
        at = slice(r, r + sub)
        u = dot(h_ref[at, :], w_ref[...]) + b_ref[...]
        cdf = 0.5 + 0.5 * lax.erf(u * 0.7071067811865476)
        pdf = jnp.exp(-0.5 * u * u) * 0.3989422804014327
        act_ref[at, :] = (u * cdf).astype(BF)
        du = (dg_ref[at, :].astype(F32) * (cdf + u * pdf)).astype(BF)
        du_ref[at, :] = du
        bu = bu + jnp.sum(du.astype(F32), axis=0, keepdims=True)
        dh_ref[at, :] += dot_nt(du, w_ref[...])
    bu_ref[...] = bu


def mlp_call(h2, w_up, bias_up, dg):
    F, FF = dg.shape
    N = 1024
    sds = jax.ShapeDtypeStruct
    col = lambda i: (0, i)
    return grid_call(
        functools.partial(mlp_kernel, min(256, F)), (FF // N,), (),
        [(h2, *whole(h2)), (w_up, (D, N), col), (bias_up, (1, N), col), (dg, (F, N), col)],
        [(sds((F, FF), BF), (F, N), col), (sds((F, FF), BF), (F, N), col), (sds((F, D), F32), (F, D), lambda i: (0, 0)),
         (sds((1, FF), F32), (1, N), col)], 4 * F * D * FF)


def wgrad_kernel(put, half_ref, a_ref, b_ref, *refs):
    put(dot_tn(a_ref[...], b_ref[...]), refs)


def wgrad(a, b, side, Y, B, rows_major, add=None):
    M, N, k = a.shape[1], b.shape[1] // 2, a.shape[0]
    W = D // (2 * Y)
    R = M // B
    cut = N // Y // W
    shape = jax.ShapeDtypeStruct((B, Y, R * cut, W), BF)

    if rows_major:
        per = min(B, max(1, 1024 // R))
        grid, a_spec, b_spec = (B // per,), ((k, per * R), lambda i, h: (0, i)), ((k, N), lambda i, h: (0, h[0]))
        o_spec = ((per, Y, R, W), lambda i, h: (i, 0, 0, 0))

        def put(o, refs):
            for p in range(per):
                for q in range(Y):
                    v = o[p * R : (p + 1) * R, q * W : (q + 1) * W]
                    if add is not None:
                        v = v + refs[0][p, q].astype(F32)
                    refs[-1][p, q] = v.astype(BF)
    else:
        grid, a_spec = (Y,), ((k, M), lambda j, h: (0, 0))
        b_spec = ((k, cut * W), lambda j, h: (0, h[0] * Y + j))
        o_spec = ((B, 1, R * cut, W), lambda j, h: (0, j, 0, 0))

        def put(o, refs):
            for p in range(cut):
                v = o[:, p * W : (p + 1) * W].reshape(B, R, W)
                if add is not None:
                    v = v + refs[0][:, 0, p * R : (p + 1) * R].astype(F32)
                refs[-1][:, 0, p * R : (p + 1) * R] = v.astype(BF)

    ins = [(a, *a_spec), (b, *b_spec)]
    if add is not None:
        ins.append((add, *o_spec))
    (out,) = grid_call(functools.partial(wgrad_kernel, put), grid, (side.reshape(1),), ins, [(shape, *o_spec)],
                       2 * k * M * N)
    return out


def qgrad_kernel(a_ref, b_ref, o_ref):
    o_ref[...] = dot_tn(a_ref[...], b_ref[...]).reshape(o_ref.shape).astype(BF)


def qgrad(h_all, dqkv, B):
    S, n = dqkv.shape
    W = n // 3
    (out,) = grid_call(
        qgrad_kernel, (3,), (), [(h_all, *whole(h_all)), (dqkv, (S, W), lambda p: (0, p))],
        [(jax.ShapeDtypeStruct((B, 3 * D // B, W), BF), (B, D // B, W), lambda p: (0, p, 0))], 2 * S * D * n)
    return out


def dh_kernel(dq_ref, w_ref, x_ref, part_ref, sum_ref):
    @pl.when(pl.program_id(0) == 0)
    def _():
        sum_ref[...] = jnp.zeros_like(sum_ref)

    part = dot_nt(dq_ref[...], w_ref[...])
    part_ref[...] = part.astype(BF)
    sum_ref[0:1, :] += jnp.sum(part * centred(x_ref[...]), axis=0, keepdims=True)
    sum_ref[1:2, :] += jnp.sum(part, axis=0, keepdims=True)


def dh_call(dqkv, w_g, x_all):
    S, n = dqkv.shape
    TR = min(512, S)
    row = lambda i: (i, 0)
    return grid_call(
        dh_kernel, (S // TR,), (), [(dqkv, (TR, n), row), (w_g, *whole(w_g)), (x_all, (TR, D), row)],
        [(jax.ShapeDtypeStruct((S, D), BF), (TR, D), row), (jax.ShapeDtypeStruct((2, D), F32), (2, D), lambda i: (0, 0))],
        2 * S * D * n)


def tile_list(active):
    m = active.shape[1]
    hit = active.astype(jnp.int32)
    upto = jnp.tril(jnp.ones((m, m), jnp.int32))
    rank = jnp.sum(hit[:, None, :] * upto[None], axis=2) - 1
    ids = jnp.arange(m, dtype=jnp.int32)
    here = (rank[:, :, None] == ids[None, None, :]) & active[:, :, None]
    return jnp.sum(jnp.where(here, ids[None, :, None], 0), axis=1), jnp.sum(hit, axis=1)


def after(vals, deps):
    return lax.optimization_barrier((vals, deps))[0]


def shards(Z, X, Y, inputs, ln1_gain, ln1_bias, w_qkv, bias_q, bias_v, w_out, bias_out, ln2_gain, ln2_bias,
           w_up, bias_up, w_down, bias_down, lengths, cotangent):
    F = inputs.shape[1]
    K = 2 * Y
    S = F * K
    T = min(256, F)
    W = D // K
    HG = H // K
    B = Z * X
    zi, xi, y, c = (lax.axis_index(n) for n in ("z", "x", "y", "c"))
    group = y * 2 + c
    sds = jax.ShapeDtypeStruct

    def shift(v, axis, n, s):
        return lax.ppermute(v, axis, [(i, (i + s) % n) for i in range(n)])

    def mate(v):
        return lax.ppermute(v, "c", [(0, 1), (1, 0)])

    rel = [(s, d) for s in range(Y) for d in range(2)]

    def hop(v, s, d):
        pairs = [(yy * 2 + cc, ((yy + s) % Y) * 2 + (cc ^ d)) for yy in range(Y) for cc in range(2)]
        return lax.ppermute(v, ("y", "c"), pairs)

    def flip(d):
        return c if d == 0 else 1 - c

    blocks = jnp.stack([((y - s) % Y) * 2 + flip(d) for s, d in rel])
    ends = jnp.cumsum(lengths.reshape(-1))
    pos = (blocks[:, None] * F + jnp.arange(F, dtype=jnp.int32)[None]).reshape(1, S)
    piece = jnp.sum((pos >= ends[:, None]).astype(jnp.int32), axis=0, keepdims=True)
    pieces = ends.shape[0]
    starts = jnp.concatenate([jnp.zeros((1,), ends.dtype), ends[:-1]])

    def look(table, idx):
        return jnp.sum(jnp.where(idx == jnp.arange(pieces)[:, None], table[:, None], 0), axis=0, keepdims=True)

    pad = piece >= pieces
    lo = jnp.where(pad, pos, look(starts, (piece // 3) * 3)).astype(jnp.int32)
    hi = jnp.where(pad | (piece % 3 == 2), pos + 1, look(ends, piece)).astype(jnp.int32)
    base = pos[0, ::T].astype(jnp.int32)
    qlo = jnp.min(lo.reshape(S // T, T), axis=1)
    qhi = jnp.max(hi.reshape(S // T, T), axis=1)
    active = (base[None, :] < qhi[:, None]) & (base[None, :] + T > qlo[:, None])
    lst_q, cnt_q = tile_list(active)
    lst_k, cnt_k = tile_list(active.T)

    x_own = inputs.reshape(F, D)
    up = cotangent.reshape(F, D)
    flat_in = x_own.astype(F32)

    def cols_of(w, g):
        return [lax.dynamic_slice_in_dim(w, part * D + g * W, W, w.ndim - 1) for part in range(3)]

    far = [shift(x_own, "y", Y, s) for s in range(1, Y)]
    near = mate(x_own)
    w_g = jnp.concatenate(cols_of(w_qkv, group), axis=1)
    b_g = jnp.concatenate([lax.dynamic_slice_in_dim(bias_q, group * W, W, 0), jnp.zeros((W,), F32),
                           lax.dynamic_slice_in_dim(bias_v, group * W, W, 0)])[None]
    sc_g = jnp.where(jnp.arange(3 * W) < W, HD**-0.5, 1.0).astype(F32)[None]
    ln1 = (ln1_gain[None], ln1_bias[None])
    held = qkv_call(x_own, *ln1, w_g, b_g, sc_g, 0, K, None)
    held = qkv_call(near, *ln1, w_g, b_g, sc_g, 1, K, held)
    dg = dot_nt(after(up, held[1]), w_down).astype(BF)
    xs = [x_own, near]
    for i, r in enumerate(far):
        r = after(r, dg) if i == 0 else r
        xs += [r, mate(r)]
        held = qkv_call(xs[-2], *ln1, w_g, b_g, sc_g, 2 * i + 2, K, held)
        held = qkv_call(xs[-1], *ln1, w_g, b_g, sc_g, 2 * i + 3, K, held)
    h_all, qkv = held
    lse_shape = sds((HG, S), F32)
    ctx_g, lse = attend(
        functools.partial(fwd_kernel, T, HG), (lst_q, cnt_q, base),
        [(qkv, (W, 0)), (qkv, (W, 1)), (qkv, (W, 2)), (lo, None), (hi, None)],
        [sds((S, W), BF), lse_shape], [], 12 * 10**9)

    mine = [ctx_g[:F]] + [hop(ctx_g[(2 * s + d) * F : (2 * s + d + 1) * F], -s, d) for s, d in rel[1:]]
    x_all = jnp.concatenate(after(xs, ctx_g), axis=0)
    mine = jnp.stack(after(mine, x_all))
    ctx = jnp.concatenate(
        [lax.dynamic_index_in_dim(mine, ((yy - y) % Y) * 2 + (cc ^ c), 0, keepdims=False)
         for yy in range(Y) for cc in range(2)], axis=1)
    middle = flat_in + (dot(ctx, w_out) + bias_out)
    h2 = layer_norm(middle, ln2_gain, ln2_bias).astype(BF)
    act, du, dh2, g_bu = mlp_call(h2, w_up, bias_up[None], dg)

    def shaped(g):
        return g.reshape(Z, X, Y, g.shape[2], W)

    def begin(items, n, me, send):
        def cut(g, axis, i):
            return lax.dynamic_index_in_dim(g, i, axis, keepdims=False)

        sent = [send(jnp.concatenate([cut(g, ax, (me + s) % n).reshape(-1, W) for g, ax in items]), s) for s in range(1, n)]
        return [cut(g, ax, me) for g, ax in items], sent

    def finish(state):
        own, sent = state
        out, at = [], 0
        for g in own:
            rows = g.size // W
            out.append(sum((r[at : at + rows].reshape(g.shape).astype(F32) for r in sent), g.astype(F32)).astype(BF))
            at += rows
        return out

    def over_y(items):
        return begin(items, Y, y, lambda v, s: shift(v, "y", Y, s))

    def over_x(items):
        return begin(items, X, xi, lambda v, s: shift(v, "x", X, s))

    def over_z(items, bit):
        bits = [(g.reshape((g.shape[0] // 2, 2) + g.shape[1:]), 1) for g in items]
        return begin(bits, 2, (zi // bit) % 2, lambda v, s: lax.ppermute(v, "z", [(i, i ^ bit) for i in range(Z)]))

    assert Z & (Z - 1) == 0
    zbits = [1 << i for i in range(Z.bit_length() - 1)]

    def total(v):
        return jnp.sum(v.astype(F32), axis=0)

    def rows_of(vecs):
        return jnp.concatenate([v.reshape(B, -1) for v in vecs], axis=1).astype(BF).reshape(B, -1, W)

    dn_give = wgrad(act, up, 1 - c, Y, B, True)
    dn_got = mate(dn_give)
    _, norm_back_two = jax.vjp(layer_norm, middle, ln2_gain, ln2_bias)
    dmid, g_ln2g, g_ln2b = norm_back_two(after(dh2, dn_give))
    dy1 = up.astype(F32) + dmid
    da = dy1.astype(BF)
    dctx = dot_nt(da, w_out).astype(BF)

    def heads_of(s, d):
        return lax.dynamic_slice_in_dim(dctx, (((y + s) % Y) * 2 + flip(d)) * W, W, 1)

    do_g = jnp.concatenate([heads_of(0, 0)] + [hop(heads_of(s, d), s, d) for s, d in rel[1:]], axis=0)

    dn = shaped(wgrad(act, after(up, dctx), c, Y, B, True, dn_got))
    hr = dn.shape[3] // 2
    dnP, dnQ = dn[:, :, :, :hr], dn[:, :, :, hr:]
    t_y, t_x = over_y([(dnP, 2)]), over_x([(dnQ, 1)])
    up_give = wgrad(after(h2, dn), du, 1 - c, Y, B, False)
    up_got = mate(up_give)
    ot_give = wgrad(ctx, after(da, up_give), 1 - c, Y, B, False)
    ot_got = mate(ot_give)
    upw = shaped(wgrad(h2, after(du, (ot_give, do_g)), c, Y, B, False, up_got))
    ot = shaped(wgrad(ctx, after(da, upw), c, Y, B, False, ot_got))
    t_y, t_x, upw, ot, do_g = lax.optimization_barrier((t_y, t_x, upw, ot, do_g))
    (dnP,), (dnQ,) = finish(t_y), finish(t_x)
    upP, upQ = upw[:, :, :, :hr], upw[:, :, :, hr:]

    t_y, t_x, t_z = over_y([(upP, 2)]), over_x([(upQ, 1)]), over_z([dnQ], 1)
    early = rows_of([total(da), g_ln2g, g_ln2b, total(up), g_bu[0]])
    do_g = after(do_g, (dnP, dnQ, t_y[0], t_x[0], early))
    (dqkv,) = attend(
        functools.partial(bwd_kernel, T, HG), (lst_k, cnt_k, base),
        [(qkv, (W, 0)), (qkv, (W, 1)), (qkv, (W, 2)), (ctx_g, None), (do_g, None), (lse, None), (lo, None), (hi, None)],
        [sds((S, 3 * W), BF)], [pltpu.VMEM((W, S), F32), pltpu.VMEM((HG, S), F32)], 20 * 10**9)
    t_y, t_x, t_z, dqkv, ot, dnP = lax.optimization_barrier((t_y, t_x, t_z, dqkv, ot, dnP))
    (upP,), (upQ,), (dnQ,) = finish(t_y), finish(t_x), finish(t_z)

    t_y, t_x = over_y([(ot, 2)]), over_x([(upP, 1), (dnP, 1)])
    t_a, t_b = over_z([upQ], 1), over_z([dnQ], zbits[1])
    part, g_ln1 = dh_call(after(dqkv, (upP, upQ, dnQ, t_y[0], t_x[0], t_a[0])), w_g, x_all)
    part = part.reshape(Y, 2, F, D)
    part_got = mate(part[:, 1])
    qv = qgrad(h_all, after(dqkv, part), B)
    act_ = after(act, qv)
    result = (middle + (dot(act_, w_down) + bias_down)).astype(BF)
    t_y, t_x, t_a, t_b, qv, result, part, part_got, g_ln1 = lax.optimization_barrier(
        (t_y, t_x, t_a, t_b, qv, result, part, part_got, g_ln1))
    (ot,), (upP, dnP), (upQ,), (dnQ,) = finish(t_y), finish(t_x), finish(t_a), finish(t_b)
    part = part[:, 0].astype(F32) + part_got.astype(F32)
    far = [shift(part[s].astype(BF), "y", Y, -s) for s in range(1, Y)]

    cols = total(dqkv)
    mine_only = jnp.arange(D) // W == group
    late = rows_of([g_ln1[0], g_ln1[1]] + [jnp.where(mine_only, jnp.tile(v, K), 0.0) for v in (cols[:W], cols[2 * W :])])
    vec = jnp.concatenate([late, early], axis=1)
    n_vec = vec.shape[1]
    vec = jnp.pad(vec, ((0, 0), (0, -n_vec % 16), (0, 0)))
    qv = jnp.concatenate([qv, vec], axis=1).reshape(Z, X, -1, W)
    t_x = over_x([(ot, 1), (qv, 1)])
    t_a, t_b = over_z([upP, dnP], 1), over_z([upQ], zbits[1])
    t_x, t_a, t_b, far = lax.optimization_barrier((t_x, t_a, t_b, far))

    def rest(items, k):
        for bit in zbits[k:]:
            items = finish(over_z(items, bit))
        return items

    (ot, qv), (upP, dnP), (upQ,), (dnQ,) = finish(t_x), finish(t_a), rest(finish(t_b), 2), rest([dnQ], 2)
    dh1 = sum((r.astype(F32) for r in far), part[0])

    t_a, t_b = over_z([ot, qv], 1), over_z([upP, dnP], zbits[1])
    t_y = over_y([(dnQ[0], 0), (upQ[0], 0)])
    _, norm_back_one = jax.vjp(lambda v: layer_norm(v, ln1_gain, ln1_bias), flat_in)
    (dx,) = norm_back_one(dh1)
    grad_inputs = (dy1 + dx).reshape(1, F, D)
    t_a, t_b, t_y, grad_inputs = lax.optimization_barrier((t_a, t_b, t_y, grad_inputs))
    (ot, qv), (upP, dnP), (dnQ, upQ) = finish(t_a), rest(finish(t_b), 2), finish(t_y)

    first = jnp.concatenate([dnP[0], dnQ, upP[0], upQ])
    def share_y(g):
        return [g] + [shift(g, "y", Y, s) for s in range(1, Y)]

    t_b = over_z([ot, qv], zbits[1])
    first_y = share_y(first)
    t_b, first_y = lax.optimization_barrier((t_b, first_y))
    ot, qv = rest(finish(t_b), 2)
    tail = jnp.concatenate([ot[0], qv[0]])
    tail_y = share_y(tail)

    def share_c(got):
        got = jnp.stack(got)
        other = mate(got)

        def piece(yy, cc):
            i = (y - yy) % Y
            return jnp.where(cc == c, lax.dynamic_index_in_dim(got, i, 0, keepdims=False),
                             lax.dynamic_index_in_dim(other, i, 0, keepdims=False))

        return [[piece(yy, cc) for cc in range(2)] for yy in range(Y)]

    dn_e, tail_e = share_c(first_y), share_c(tail_y)
    n_up, n_ot = 2 * hr, D // B

    def by_columns(e, at, rows, chunks):
        return jnp.concatenate([e[yy][cc][at + k * rows : at + (k + 1) * rows] for cc in range(2) for yy in range(Y)
                                for k in range(chunks)], axis=1).astype(F32)

    g_w_down = by_columns(dn_e, 0, 2 * hr, 1)
    g_w_up = by_columns(dn_e, n_up, D // B, 2 * hr * B // D)
    g_w_out = by_columns(tail_e, 0, n_ot, 1)
    at = n_ot
    g_w_qkv = jnp.concatenate([tail_e[yy][cc][at + p * n_ot : at + (p + 1) * n_ot] for p in range(3) for yy in range(Y)
                               for cc in range(2)], axis=1).astype(F32)
    at += 3 * n_ot
    flat = sum(tail_e[yy][cc][at:].astype(F32) for yy in range(Y) for cc in range(2)).reshape(-1)
    out, at = [], 0
    for n in (D, D, D, D, D, D, D, D, w_up.shape[1]):
        out.append(flat[at : at + n // B])
        at += n // B
    g_ln1g, g_ln1b, g_bq, g_bv, g_bo, g_ln2g, g_ln2b, g_bd, g_bu = out
    return (result.reshape(1, F, D), grad_inputs, g_ln1g, g_ln1b, g_w_qkv, g_bq, g_bv, g_w_out, g_bo, g_ln2g, g_ln2b,
            g_w_up, g_bu, g_w_down, g_bd)


def solution(mesh):
    batch, blk = mesh.shape["batch"], mesh.shape["blk"]
    Y = blk // 2
    X = Y if batch % Y == 0 else 1
    Z = batch // X
    fine = Mesh(mesh.devices.reshape(Z, X, Y, 2), ("z", "x", "y", "c"))
    rows, slots = ("z", "x"), ("y", "c")
    act = P(rows, slots, None)
    flat, mat = P(rows), P(rows, None)
    return jax.shard_map(
        functools.partial(shards, Z, X, Y),
        mesh=fine,
        in_specs=(act,) + (P(),) * 13 + (P(rows, None, None), act),
        out_specs=(act, act, flat, flat, mat, flat, flat, mat, flat, flat, flat, mat, flat, mat, flat),
        check_vma=False,
    )
```

```python
import functools

import jax
import jax.numpy as jnp
from jax import lax
from jax.experimental import pallas as pl
from jax.experimental.pallas import tpu as pltpu
from jax.sharding import Mesh
from jax.sharding import PartitionSpec as P

D = 1024
H = 16
HD = 64
EPS = 1e-05
NEG = -1e30
VM = 28
AV = 28
BF = jnp.bfloat16
F32 = jnp.float32


def layer_norm(values, gain_vec, shift_vec):
    center = values - jnp.mean(values, axis=-1, keepdims=True)
    spread = jnp.mean(center * center, axis=-1, keepdims=True)
    return center * lax.rsqrt(spread + EPS) * gain_vec + shift_vec


def dot(a, b):
    return jnp.dot(a, b, preferred_element_type=F32)


def dot_tn(a, b):
    return lax.dot_general(a, b, (((0,), (0,)), ((), ())), preferred_element_type=F32)


def dot_nt(a, b):
    return lax.dot_general(a, b, (((1,), (1,)), ((), ())), preferred_element_type=F32)


def half(a, h):
    a = a[:, (h // 2) * 2 * HD : (h // 2 + 1) * 2 * HD]
    lane = lax.broadcasted_iota(jnp.int32, a.shape, 1)
    zero = jnp.zeros_like(a)
    return jnp.where(lane < HD, a, zero) if h % 2 == 0 else jnp.where(lane < HD, zero, a)


def pair(a, h):
    return a[:, (h // 2) * 2 * HD : (h // 2 + 1) * 2 * HD]


def fwd_kernel(T, HG, lst, cnt, base, q_ref, k_ref, v_ref, lo_ref, hi_ref, ctx_ref, lse_ref):
    nq = q_ref.shape[0] // T
    row = lax.broadcasted_iota(jnp.int32, (T, T), 0)

    @pl.loop(0, nq)
    def _(qt):
        at = pl.ds(pl.multiple_of(qt * T, T), T)
        q = q_ref[at, :]
        qh = [half(q, h) for h in range(HG)]
        lo, hi = lo_ref[:, at], hi_ref[:, at]

        def body(n, carry):
            t = lst[qt, n]
            ks = pl.ds(pl.multiple_of(t * T, T), T)
            k, v = k_ref[ks, :], v_ref[ks, :].T
            vis = (row >= lo - base[t]) & (row < hi - base[t])
            raw = [dot_nt(pair(k, h), qh[h]) for h in range(HG)]
            out = []
            for h in range(HG):
                m, l, acc = carry[h]
                s = jnp.where(vis, raw[h], NEG)
                mn = jnp.maximum(m, jnp.max(s, axis=0, keepdims=True))
                a = jnp.exp(m - mn)
                p = jnp.exp(s - mn)
                l = a * l + jnp.sum(p, axis=0, keepdims=True)
                acc = acc * a + dot(v[h * HD : (h + 1) * HD, :], p.astype(BF))
                out.append((mn, l, acc))
            return tuple(out)

        one = (jnp.full((1, T), NEG, F32), jnp.zeros((1, T), F32), jnp.zeros((HD, T), F32))
        res = lax.fori_loop(0, cnt[qt], body, (one,) * HG)
        ctx_ref[at, :] = jnp.concatenate([r[2] / r[1] for r in res], axis=0).T.astype(BF)
        lse_ref[:, at] = jnp.concatenate([r[0] + jnp.log(r[1]) for r in res], axis=0)


def bwd_kernel(T, HG, lst, cnt, base, q_ref, k_ref, v_ref, ctx_ref, do_ref, lse_ref, lo_ref, hi_ref, out_ref, dqt, dl):
    n_tiles = q_ref.shape[0] // T
    W = HG * HD
    row = lax.broadcasted_iota(jnp.int32, (T, T), 0)
    lane = lax.broadcasted_iota(jnp.int32, (T, 2 * HD), 1)
    dqt[...] = jnp.zeros_like(dqt)

    @pl.loop(0, n_tiles)
    def _(t):
        at = pl.ds(pl.multiple_of(t * T, T), T)
        prod = (do_ref[at, :].astype(F32) * ctx_ref[at, :].astype(F32)).T
        dl[:, at] = jnp.concatenate([jnp.sum(prod[h * HD : (h + 1) * HD], axis=0, keepdims=True) for h in range(HG)], axis=0)

    @pl.loop(0, n_tiles)
    def _(kt):
        ks = pl.ds(pl.multiple_of(kt * T, T), T)
        k, v = k_ref[ks, :], v_ref[ks, :]
        kT = k.T
        kh, vh = [half(k, h) for h in range(HG)], [half(v, h) for h in range(HG)]

        def body(n, carry):
            at = pl.ds(pl.multiple_of(lst[kt, n] * T, T), T)
            q, do = q_ref[at, :], do_ref[at, :]
            vis = (row >= lo_ref[:, at] - base[kt]) & (row < hi_ref[:, at] - base[kt])
            raw = [dot_nt(kh[h], pair(q, h)) for h in range(HG)]
            dps = [dot_nt(vh[h], pair(do, h)) for h in range(HG)]
            out = []
            for h in range(HG):
                p = jnp.exp(jnp.where(vis, raw[h], NEG) - lse_ref[h : h + 1, at])
                ds = (p * (dps[h] - dl[h : h + 1, at])).astype(BF)
                out.append((carry[h][0] + dot(ds, pair(q, h)), carry[h][1] + dot(p.astype(BF), pair(do, h))))
                dqt[h * HD : (h + 1) * HD, at] += dot(kT[h * HD : (h + 1) * HD, :], ds)
            return tuple(out)

        one = (jnp.zeros((T, 2 * HD), F32), jnp.zeros((T, 2 * HD), F32))
        res = lax.fori_loop(0, cnt[kt], body, (one,) * HG)
        for p in range(HG // 2):
            cols = slice(p * 2 * HD, (p + 1) * 2 * HD)
            a, b = res[2 * p], res[2 * p + 1]
            out_ref[ks, W + cols.start : W + cols.stop] = jnp.where(lane < HD, a[0], b[0]).astype(BF)
            out_ref[ks, 2 * W + cols.start : 2 * W + cols.stop] = jnp.where(lane < HD, a[1], b[1]).astype(BF)

    @pl.loop(0, n_tiles)
    def _(t):
        at = pl.ds(pl.multiple_of(t * T, T), T)
        out_ref[at, :W] = (dqt[:, at].T * HD**-0.5).astype(BF)


def attend(kernel, scalars, ins, outs, scratch, flops):
    def spec(shape, cols):
        if cols is None:
            return pl.BlockSpec(shape, lambda i, *_: (0,) * len(shape))
        return pl.BlockSpec((shape[0], cols[0]), lambda i, *_: (0, cols[1]))

    size = sum(a.size * a.dtype.itemsize for a, _ in ins) + sum(o.size * o.dtype.itemsize for o in outs)
    return pl.pallas_call(
        kernel,
        out_shape=outs,
        grid_spec=pltpu.PrefetchScalarGridSpec(
            num_scalar_prefetch=len(scalars),
            grid=(1,),
            in_specs=[spec(a.shape, cols) for a, cols in ins],
            out_specs=[spec(o.shape, None) for o in outs],
            scratch_shapes=scratch,
        ),
        compiler_params=pltpu.CompilerParams(vmem_limit_bytes=AV << 20),
        cost_estimate=pl.CostEstimate(flops=flops, bytes_accessed=size, transcendentals=0),
    )(*scalars, *[a for a, _ in ins])


def grid_call(kernel, grid, scalars, ins, outs, flops, scratch=(), aliases=None, vmem=VM, light=1):
    def spec(block, index):
        return pl.BlockSpec(memory_space=pl.ANY) if block is None else pl.BlockSpec(block, index)

    size = sum(a.size * a.dtype.itemsize for a, b, _ in ins if b is not None)
    size += sum(o.size * o.dtype.itemsize for o, _, _ in outs)
    return pl.pallas_call(
        kernel,
        out_shape=[o for o, _, _ in outs],
        grid_spec=pltpu.PrefetchScalarGridSpec(
            num_scalar_prefetch=len(scalars),
            grid=grid,
            in_specs=[spec(b, m) for _, b, m in ins],
            out_specs=[spec(b, m) for _, b, m in outs],
            scratch_shapes=list(scratch),
        ),
        input_output_aliases=aliases or {},
        compiler_params=pltpu.CompilerParams(vmem_limit_bytes=vmem << 20),
        cost_estimate=pl.CostEstimate(flops=flops // light, bytes_accessed=size // light, transcendentals=0),
    )(*scalars, *[a for a, _, _ in ins])


def whole(a):
    return a.shape, lambda *_: (0,) * len(a.shape)


def centred(x):
    x = x.astype(F32)
    center = x - jnp.mean(x, axis=-1, keepdims=True)
    spread = jnp.mean(center * center, axis=-1, keepdims=True)
    return center * lax.rsqrt(spread + EPS)


def qkv_kernel(x_ref, g_ref, b_ref, w_ref, bias_ref, sc_ref, *refs):
    h_ref, o_ref = refs[-2:]
    h = (centred(x_ref[...]) * g_ref[...] + b_ref[...]).astype(BF)
    h_ref[...] = h
    o = (dot(h, w_ref[...]) + bias_ref[...]).astype(BF)
    o_ref[...] = (o.astype(F32) * sc_ref[...]).astype(BF)


def qkv_call(x, g, b, w, bias, sc, r, blocks, held):
    F, n = x.shape[0], w.shape[1]
    TR = min(256, F)
    per = F // TR
    row = lambda i: (i, 0)
    to = lambda i: (r * per + i, 0)
    ins = [(x, (TR, D), row)] + [(v, *whole(v)) for v in (g, b, w, bias, sc)]
    shapes = [jax.ShapeDtypeStruct((blocks * F, D), BF), jax.ShapeDtypeStruct((blocks * F, n), BF)]
    aliases = {}
    if held is not None:
        ins += [(held[0], None, None), (held[1], None, None)]
        aliases = {6: 0, 7: 1}
    return grid_call(qkv_kernel, (per,), (), ins, [(shapes[0], (TR, D), to), (shapes[1], (TR, n), to)],
                     2 * F * D * n, aliases=aliases)


def mlp_kernel(sub, h_ref, w_ref, b_ref, dg_ref, act_ref, du_ref, dh_ref, bu_ref):
    rows = h_ref.shape[0]

    @pl.when(pl.program_id(0) == 0)
    def _():
        dh_ref[...] = jnp.zeros_like(dh_ref)

    bu = jnp.zeros(bu_ref.shape, F32)
    for r in range(0, rows, sub):
        at = slice(r, r + sub)
        u = dot(h_ref[at, :], w_ref[...]) + b_ref[...]
        cdf = 0.5 + 0.5 * lax.erf(u * 0.7071067811865476)
        pdf = jnp.exp(-0.5 * u * u) * 0.3989422804014327
        act_ref[at, :] = (u * cdf).astype(BF)
        du = (dg_ref[at, :].astype(F32) * (cdf + u * pdf)).astype(BF)
        du_ref[at, :] = du
        bu = bu + jnp.sum(du.astype(F32), axis=0, keepdims=True)
        dh_ref[at, :] += dot_nt(du, w_ref[...])
    bu_ref[...] = bu


def mlp_call(h2, w_up, bias_up, dg):
    F, FF = dg.shape
    N = 1024
    sds = jax.ShapeDtypeStruct
    col = lambda i: (0, i)
    return grid_call(
        functools.partial(mlp_kernel, min(256, F)), (FF // N,), (),
        [(h2, *whole(h2)), (w_up, (D, N), col), (bias_up, (1, N), col), (dg, (F, N), col)],
        [(sds((F, FF), BF), (F, N), col), (sds((F, FF), BF), (F, N), col), (sds((F, D), F32), (F, D), lambda i: (0, 0)),
         (sds((1, FF), F32), (1, N), col)], 4 * F * D * FF)


def wgrad_kernel(put, n, half_ref, *refs):
    put([dot_tn(refs[2 * i][...], refs[2 * i + 1][...]) for i in range(n)], refs[2 * n :])


def wgrad_rows(a, b, side, Y, B, add=None):
    k, M = a.shape
    N = b.shape[1] // 2
    W, R = N // Y, M // B
    per = min(B, max(1, 1024 // R))
    o_spec = ((per, Y, R, W), lambda i, h: (i, 0, 0, 0))

    def put(prods, refs):
        (o,) = prods
        for p in range(per):
            for q in range(Y):
                v = o[p * R : (p + 1) * R, q * W : (q + 1) * W]
                if add is not None:
                    v = v + refs[0][p, q].astype(F32)
                refs[-1][p, q] = v.astype(BF)

    ins = [(a, (k, per * R), lambda i, h: (0, i)), (b, (k, N), lambda i, h: (0, h[0]))]
    if add is not None:
        ins.append((add, *o_spec))
    (out,) = grid_call(functools.partial(wgrad_kernel, put, 1), (B // per,), (side.reshape(1),), ins,
                       [(jax.ShapeDtypeStruct((B, Y, R, W), BF), *o_spec)], 2 * k * M * N)
    return out


def wgrad_cols(pairs, side, Y, B, W, add=None):
    k, M = pairs[0][0].shape
    R = M // B
    cuts = [b.shape[1] // (2 * Y * W) for _, b in pairs]
    rows = R * sum(cuts)
    o_spec = ((B, 1, rows, W), lambda j, h: (0, j, 0, 0))

    def put(prods, refs):
        at = 0
        for o, cut in zip(prods, cuts):
            for p in range(cut):
                v = o[:, p * W : (p + 1) * W].reshape(B, R, W)
                if add is not None:
                    v = v + refs[0][:, 0, at : at + R].astype(F32)
                refs[-1][:, 0, at : at + R] = v.astype(BF)
                at += R

    ins = []
    for (a, b), cut in zip(pairs, cuts):
        ins += [(a, *whole(a)), (b, (k, cut * W), lambda j, h: (0, h[0] * Y + j))]
    if add is not None:
        ins.append((add, *o_spec))
    (out,) = grid_call(functools.partial(wgrad_kernel, put, len(pairs)), (Y,), (side.reshape(1),), ins,
                       [(jax.ShapeDtypeStruct((B, Y, rows, W), BF), *o_spec)],
                       sum(2 * k * a.shape[1] * b.shape[1] // 2 for a, b in pairs))
    return out


def qgrad_kernel(a_ref, b_ref, o_ref):
    o_ref[...] = dot_tn(a_ref[...], b_ref[...]).reshape(o_ref.shape).astype(BF)


def qgrad(h_all, dqkv, B):
    S, n = dqkv.shape
    W = n // 3
    (out,) = grid_call(
        qgrad_kernel, (3,), (), [(h_all, *whole(h_all)), (dqkv, (S, W), lambda p: (0, p))],
        [(jax.ShapeDtypeStruct((B, 3 * D // B, W), BF), (B, D // B, W), lambda p: (0, p, 0))], 2 * S * D * n, light=8)
    return out


def dh_kernel(dq_ref, w_ref, x_ref, part_ref, sum_ref):
    @pl.when(pl.program_id(0) == 0)
    def _():
        sum_ref[...] = jnp.zeros_like(sum_ref)

    part = dot_nt(dq_ref[...], w_ref[...])
    part_ref[...] = part.astype(BF)
    sum_ref[0:1, :] += jnp.sum(part * centred(x_ref[...]), axis=0, keepdims=True)
    sum_ref[1:2, :] += jnp.sum(part, axis=0, keepdims=True)


def dh_call(dqkv, w_g, x_all):
    S, n = dqkv.shape
    TR = min(512, S)
    row = lambda i: (i, 0)
    return grid_call(
        dh_kernel, (S // TR,), (), [(dqkv, (TR, n), row), (w_g, *whole(w_g)), (x_all, (TR, D), row)],
        [(jax.ShapeDtypeStruct((S, D), BF), (TR, D), row), (jax.ShapeDtypeStruct((2, D), F32), (2, D), lambda i: (0, 0))],
        2 * S * D * n, light=8)


def tile_list(active):
    m = active.shape[1]
    hit = active.astype(jnp.int32)
    upto = jnp.tril(jnp.ones((m, m), jnp.int32))
    rank = jnp.sum(hit[:, None, :] * upto[None], axis=2) - 1
    ids = jnp.arange(m, dtype=jnp.int32)
    here = (rank[:, :, None] == ids[None, None, :]) & active[:, :, None]
    return jnp.sum(jnp.where(here, ids[None, :, None], 0), axis=1), jnp.sum(hit, axis=1)


def after(vals, deps):
    return lax.optimization_barrier((vals, deps))[0]


def shards(Z, X, Y, inputs, ln1_gain, ln1_bias, w_qkv, bias_q, bias_v, w_out, bias_out, ln2_gain, ln2_bias,
           w_up, bias_up, w_down, bias_down, lengths, cotangent):
    F = inputs.shape[1]
    K = 2 * Y
    S = F * K
    T = min(256, F)
    W = D // K
    HG = H // K
    B = Z * X
    zi, xi, y, c = (lax.axis_index(n) for n in ("z", "x", "y", "c"))
    group = y * 2 + c
    sds = jax.ShapeDtypeStruct

    def shift(v, axis, n, s):
        return lax.ppermute(v, axis, [(i, (i + s) % n) for i in range(n)])

    def mate(v):
        return lax.ppermute(v, "c", [(0, 1), (1, 0)])

    rel = [(s, d) for s in range(Y) for d in range(2)]

    def hop(v, s, d):
        pairs = [(yy * 2 + cc, ((yy + s) % Y) * 2 + (cc ^ d)) for yy in range(Y) for cc in range(2)]
        return lax.ppermute(v, ("y", "c"), pairs)

    def flip(d):
        return c if d == 0 else 1 - c

    blocks = jnp.stack([((y - s) % Y) * 2 + flip(d) for s, d in rel])
    ends = jnp.cumsum(lengths.reshape(-1))
    pos = (blocks[:, None] * F + jnp.arange(F, dtype=jnp.int32)[None]).reshape(1, S)
    piece = jnp.sum((pos >= ends[:, None]).astype(jnp.int32), axis=0, keepdims=True)
    pieces = ends.shape[0]
    starts = jnp.concatenate([jnp.zeros((1,), ends.dtype), ends[:-1]])

    def look(table, idx):
        return jnp.sum(jnp.where(idx == jnp.arange(pieces)[:, None], table[:, None], 0), axis=0, keepdims=True)

    pad = piece >= pieces
    lo = jnp.where(pad, pos, look(starts, (piece // 3) * 3)).astype(jnp.int32)
    hi = jnp.where(pad | (piece % 3 == 2), pos + 1, look(ends, piece)).astype(jnp.int32)
    base = pos[0, ::T].astype(jnp.int32)
    qlo = jnp.min(lo.reshape(S // T, T), axis=1)
    qhi = jnp.max(hi.reshape(S // T, T), axis=1)
    active = (base[None, :] < qhi[:, None]) & (base[None, :] + T > qlo[:, None])
    lst_q, cnt_q = tile_list(active)
    lst_k, cnt_k = tile_list(active.T)

    x_own = inputs.reshape(F, D)
    up = cotangent.reshape(F, D)
    flat_in = x_own.astype(F32)

    def cols_of(w, g):
        return [lax.dynamic_slice_in_dim(w, part * D + g * W, W, w.ndim - 1) for part in range(3)]

    far = [shift(x_own, "y", Y, s) for s in range(1, Y)]
    near = mate(x_own)
    w_g = jnp.concatenate(cols_of(w_qkv, group), axis=1)
    b_g = jnp.concatenate([lax.dynamic_slice_in_dim(bias_q, group * W, W, 0), jnp.zeros((W,), F32),
                           lax.dynamic_slice_in_dim(bias_v, group * W, W, 0)])[None]
    sc_g = jnp.where(jnp.arange(3 * W) < W, HD**-0.5, 1.0).astype(F32)[None]
    ln1 = (ln1_gain[None], ln1_bias[None])
    held = qkv_call(x_own, *ln1, w_g, b_g, sc_g, 0, K, None)
    held = qkv_call(near, *ln1, w_g, b_g, sc_g, 1, K, held)
    dg = dot_nt(after(up, held[1]), w_down).astype(BF)
    xs = [x_own, near]
    for i, r in enumerate(far):
        r = after(r, dg) if i == 0 else r
        xs += [r, mate(r)]
        held = qkv_call(xs[-2], *ln1, w_g, b_g, sc_g, 2 * i + 2, K, held)
        held = qkv_call(xs[-1], *ln1, w_g, b_g, sc_g, 2 * i + 3, K, held)
    h_all, qkv = held
    lse_shape = sds((HG, S), F32)
    ctx_g, lse = attend(
        functools.partial(fwd_kernel, T, HG), (lst_q, cnt_q, base),
        [(qkv, (W, 0)), (qkv, (W, 1)), (qkv, (W, 2)), (lo, None), (hi, None)],
        [sds((S, W), BF), lse_shape], [], 12 * 10**9)

    mine = [ctx_g[:F]] + [hop(ctx_g[(2 * s + d) * F : (2 * s + d + 1) * F], -s, d) for s, d in rel[1:]]
    x_all = jnp.concatenate(after(xs, ctx_g), axis=0)
    mine = jnp.stack(after(mine, x_all))
    ctx = jnp.concatenate(
        [lax.dynamic_index_in_dim(mine, ((yy - y) % Y) * 2 + (cc ^ c), 0, keepdims=False)
         for yy in range(Y) for cc in range(2)], axis=1)
    middle = flat_in + (dot(ctx, w_out) + bias_out)
    h2 = layer_norm(middle, ln2_gain, ln2_bias).astype(BF)
    act, du, dh2, g_bu = mlp_call(h2, w_up, bias_up[None], dg)

    def shaped(g):
        return g.reshape(Z, X, Y, g.shape[2], W)

    def begin(items, n, me, send):
        def cut(g, axis, i):
            return lax.dynamic_index_in_dim(g, i, axis, keepdims=False)

        sent = [send(jnp.concatenate([cut(g, ax, (me + s) % n).reshape(-1, W) for g, ax in items]), s) for s in range(1, n)]
        return [cut(g, ax, me) for g, ax in items], sent

    def finish(state):
        own, sent = state
        out, at = [], 0
        for g in own:
            rows = g.size // W
            out.append(sum((r[at : at + rows].reshape(g.shape).astype(F32) for r in sent), g.astype(F32)).astype(BF))
            at += rows
        return out

    def over_y(items):
        return begin(items, Y, y, lambda v, s: shift(v, "y", Y, s))

    def over_x(items):
        return begin(items, X, xi, lambda v, s: shift(v, "x", X, s))

    def over_z(items, bit):
        bits = [(g.reshape((g.shape[0] // 2, 2) + g.shape[1:]), 1) for g in items]
        return begin(bits, 2, (zi // bit) % 2, lambda v, s: lax.ppermute(v, "z", [(i, i ^ bit) for i in range(Z)]))

    assert Z & (Z - 1) == 0
    zbits = [1 << i for i in range(Z.bit_length() - 1)]

    def total(v):
        return jnp.sum(v.astype(F32), axis=0)

    def rows_of(vecs):
        return jnp.concatenate([v.reshape(B, -1) for v in vecs], axis=1).astype(BF).reshape(B, -1, W)

    dn_give = wgrad_rows(act, up, 1 - c, Y, B)
    dn_got = mate(dn_give)
    _, norm_back_two = jax.vjp(layer_norm, middle, ln2_gain, ln2_bias)
    dmid, g_ln2g, g_ln2b = norm_back_two(after(dh2, dn_give))
    dy1 = up.astype(F32) + dmid
    da = dy1.astype(BF)
    dctx = dot_nt(da, w_out).astype(BF)

    def heads_of(s, d):
        return lax.dynamic_slice_in_dim(dctx, (((y + s) % Y) * 2 + flip(d)) * W, W, 1)

    def both(s):
        return jnp.concatenate([heads_of(s, 0), heads_of(s, 1)])

    do_y = [both(0)] + [shift(both(s), "y", Y, s) for s in range(1, Y)]

    dn = shaped(wgrad_rows(act, after(up, do_y[0]), c, Y, B, dn_got))
    hr = dn.shape[3] // 2
    dnP, dnQ = dn[:, :, :, :hr], dn[:, :, :, hr:]
    t_y, t_x = over_y([(dnP, 2)]), over_x([(dnQ, 1)])
    h2_, du_, ctx_, da_ = after((h2, du, ctx, da), dn)
    upw_give = wgrad_cols([(h2_, du_), (ctx_, da_)], 1 - c, Y, B, W)
    upw_give, do_y = lax.optimization_barrier((upw_give, do_y))
    upw_got = mate(upw_give)
    result = (middle + (dot(after(act, upw_give), w_down) + bias_down)).astype(BF)
    do_c = mate(jnp.concatenate([v[F:] for v in do_y]))
    do_g = jnp.concatenate([b for s in range(Y) for b in (do_y[s][:F], do_c[s * F : (s + 1) * F])])
    upw = shaped(wgrad_cols([(h2_, du_), (ctx_, after(da_, (do_g, result)))], c, Y, B, W, upw_got))
    t_y, t_x, upw, do_g = lax.optimization_barrier((t_y, t_x, upw, do_g))
    (dnP,), (dnQ,) = finish(t_y), finish(t_x)
    ur = upw.shape[3] // 2
    upQ, upP = upw[:, :, :, :ur], upw[:, :, :, ur:]

    t_y, t_x, t_z = over_y([(upP, 2)]), over_x([(upQ, 1)]), over_z([dnQ], 1)
    early = rows_of([total(da), g_ln2g, g_ln2b, total(up), g_bu[0]])
    do_g = after(do_g, (dnP, dnQ, t_y[0], t_x[0], early))
    (dqkv,) = attend(
        functools.partial(bwd_kernel, T, HG), (lst_k, cnt_k, base),
        [(qkv, (W, 0)), (qkv, (W, 1)), (qkv, (W, 2)), (ctx_g, None), (do_g, None), (lse, None), (lo, None), (hi, None)],
        [sds((S, 3 * W), BF)], [pltpu.VMEM((W, S), F32), pltpu.VMEM((HG, S), F32)], 20 * 10**9)
    part, g_ln1 = dh_call(dqkv, w_g, x_all)
    t_y, t_x, t_z, dqkv, dnP, part, g_ln1 = lax.optimization_barrier((t_y, t_x, t_z, dqkv, dnP, part, g_ln1))
    (upP,), (upQ,), (dnQ,) = finish(t_y), finish(t_x), finish(t_z)

    part = part.reshape(Y, 2, F, D)
    part = part[:, 0].astype(F32) + mate(part[:, 1]).astype(F32)
    far = [shift(part[s].astype(BF), "y", Y, -s) for s in range(1, Y)]
    t_x, t_a, t_b = over_x([(upP, 1), (dnP, 1)]), over_z([upQ], 1), over_z([dnQ], zbits[1])
    qv = qgrad(h_all, after(dqkv, (upP, upQ, dnQ)), B)
    cols = total(dqkv)
    mine_only = jnp.arange(D) // W == group
    late = rows_of([g_ln1[0], g_ln1[1]] + [jnp.where(mine_only, jnp.tile(v, K), 0.0) for v in (cols[:W], cols[2 * W :])])
    vec = jnp.concatenate([late, early], axis=1)
    vec = jnp.pad(vec, ((0, 0), (0, -vec.shape[1] % 16), (0, 0)))
    qv = jnp.concatenate([qv, vec], axis=1).reshape(Z, X, -1, W)
    t_x, t_a, t_b, qv, far = lax.optimization_barrier((t_x, t_a, t_b, qv, far))
    (upP, dnP), (upQ,), (dnQ,) = finish(t_x), finish(t_a), finish(t_b)

    t_x = over_x([(qv, 1)])
    t_a, t_b = over_z([upP, dnP], 1), over_z([upQ], zbits[1])
    dh1 = sum((r.astype(F32) for r in far), part[0])
    _, norm_back_one = jax.vjp(lambda v: layer_norm(v, ln1_gain, ln1_bias), flat_in)
    (dx,) = norm_back_one(dh1)
    grad_inputs = (dy1 + dx).reshape(1, F, D)
    t_x, t_a, t_b, grad_inputs = lax.optimization_barrier((t_x, t_a, t_b, grad_inputs))

    def rest(items, k):
        for bit in zbits[k:]:
            items = finish(over_z(items, bit))
        return items

    (qv,), (upP, dnP), (upQ,), (dnQ,) = finish(t_x), finish(t_a), rest(finish(t_b), 2), rest([dnQ], 2)

    t_a, t_b = over_z([qv], 1), over_z([upP, dnP], zbits[1])
    t_y = over_y([(dnQ[0], 0), (upQ[0], 0)])
    t_a, t_b, t_y = lax.optimization_barrier((t_a, t_b, t_y))
    (qv,), (upP, dnP), (dnQ, upQ) = finish(t_a), rest(finish(t_b), 2), finish(t_y)

    first = jnp.concatenate([dnP[0], dnQ, upQ, upP[0]])

    def share_y(g):
        return [g] + [shift(g, "y", Y, s) for s in range(1, Y)]

    t_b = over_z([qv], zbits[1])
    first_y = share_y(first)
    t_b, first_y = lax.optimization_barrier((t_b, first_y))
    (qv,) = rest(finish(t_b), 2)
    tail_y = share_y(qv[0])

    def share_c(got):
        got = jnp.stack(got)
        other = mate(got)

        def piece(yy, cc):
            i = (y - yy) % Y
            return jnp.where(cc == c, lax.dynamic_index_in_dim(got, i, 0, keepdims=False),
                             lax.dynamic_index_in_dim(other, i, 0, keepdims=False))

        return [[piece(yy, cc) for cc in range(2)] for yy in range(Y)]

    def by_columns(e, at, rows, chunks):
        return jnp.concatenate([e[yy][cc][at + k * rows : at + (k + 1) * rows] for cc in range(2) for yy in range(Y)
                                for k in range(chunks)], axis=1).astype(F32)

    first_e = share_c(first_y)
    n_dn, n_ot = 2 * hr, D // B
    g_w_down = by_columns(first_e, 0, n_dn, 1)
    g_w_up = by_columns(first_e, n_dn, n_ot, 2 * ur // n_ot - 1)
    g_w_out = by_columns(first_e, n_dn + 2 * ur - n_ot, n_ot, 1)
    tail_y, g_w_down, g_w_up, g_w_out = lax.optimization_barrier((tail_y, g_w_down, g_w_up, g_w_out))
    tail_e = share_c(tail_y)
    g_w_qkv = jnp.concatenate([tail_e[yy][cc][p * n_ot : (p + 1) * n_ot] for p in range(3) for yy in range(Y)
                               for cc in range(2)], axis=1).astype(F32)
    at = 3 * n_ot
    flat = sum(tail_e[yy][cc][at:].astype(F32) for yy in range(Y) for cc in range(2)).reshape(-1)
    out, at = [], 0
    for n in (D, D, D, D, D, D, D, D, w_up.shape[1]):
        out.append(flat[at : at + n // B])
        at += n // B
    g_ln1g, g_ln1b, g_bq, g_bv, g_bo, g_ln2g, g_ln2b, g_bd, g_bu = out
    return (result.reshape(1, F, D), grad_inputs, g_ln1g, g_ln1b, g_w_qkv, g_bq, g_bv, g_w_out, g_bo, g_ln2g, g_ln2b,
            g_w_up, g_bu, g_w_down, g_bd)


def solution(mesh):
    batch, blk = mesh.shape["batch"], mesh.shape["blk"]
    Y = blk // 2
    X = Y if batch % Y == 0 else 1
    Z = batch // X
    fine = Mesh(mesh.devices.reshape(Z, X, Y, 2), ("z", "x", "y", "c"))
    rows, slots = ("z", "x"), ("y", "c")
    act = P(rows, slots, None)
    flat, mat = P(rows), P(rows, None)
    return jax.shard_map(
        functools.partial(shards, Z, X, Y),
        mesh=fine,
        in_specs=(act,) + (P(),) * 13 + (P(rows, None, None), act),
        out_specs=(act, act, flat, flat, mat, flat, flat, mat, flat, flat, flat, mat, flat, mat, flat),
        check_vma=False,
    )
```

```python
import functools

import jax
import jax.numpy as jnp
from jax import lax
from jax.experimental import pallas as pl
from jax.experimental.pallas import tpu as pltpu
from jax.sharding import Mesh
from jax.sharding import PartitionSpec as P

D = 1024
H = 16
HD = 64
EPS = 1e-05
NEG = -1e30
VM = 20
AV = 28
BF = jnp.bfloat16
F32 = jnp.float32


def layer_norm(values, gain_vec, shift_vec):
    center = values - jnp.mean(values, axis=-1, keepdims=True)
    spread = jnp.mean(center * center, axis=-1, keepdims=True)
    return center * lax.rsqrt(spread + EPS) * gain_vec + shift_vec


def dot(a, b):
    return jnp.dot(a, b, preferred_element_type=F32)


def dot_tn(a, b):
    return lax.dot_general(a, b, (((0,), (0,)), ((), ())), preferred_element_type=F32)


def dot_nt(a, b):
    return lax.dot_general(a, b, (((1,), (1,)), ((), ())), preferred_element_type=F32)


def half(a, h):
    a = a[:, (h // 2) * 2 * HD : (h // 2 + 1) * 2 * HD]
    lane = lax.broadcasted_iota(jnp.int32, a.shape, 1)
    zero = jnp.zeros_like(a)
    return jnp.where(lane < HD, a, zero) if h % 2 == 0 else jnp.where(lane < HD, zero, a)


def pair(a, h):
    return a[:, (h // 2) * 2 * HD : (h // 2 + 1) * 2 * HD]


def fwd_kernel(T, HG, lst, cnt, base, q_ref, k_ref, v_ref, lo_ref, hi_ref, ctx_ref, lse_ref):
    nq = q_ref.shape[0] // T
    row = lax.broadcasted_iota(jnp.int32, (T, T), 0)

    @pl.loop(0, nq)
    def _(qt):
        at = pl.ds(pl.multiple_of(qt * T, T), T)
        q = q_ref[at, :]
        qh = [half(q, h) for h in range(HG)]
        lo, hi = lo_ref[:, at], hi_ref[:, at]

        def body(n, carry):
            t = lst[qt, n]
            ks = pl.ds(pl.multiple_of(t * T, T), T)
            k, v = k_ref[ks, :], v_ref[ks, :].T
            vis = (row >= lo - base[t]) & (row < hi - base[t])
            raw = [dot_nt(pair(k, h), qh[h]) for h in range(HG)]
            out = []
            for h in range(HG):
                m, l, acc = carry[h]
                s = jnp.where(vis, raw[h], NEG)
                mn = jnp.maximum(m, jnp.max(s, axis=0, keepdims=True))
                a = jnp.exp(m - mn)
                p = jnp.exp(s - mn)
                l = a * l + jnp.sum(p, axis=0, keepdims=True)
                acc = acc * a + dot(v[h * HD : (h + 1) * HD, :], p.astype(BF))
                out.append((mn, l, acc))
            return tuple(out)

        one = (jnp.full((1, T), NEG, F32), jnp.zeros((1, T), F32), jnp.zeros((HD, T), F32))
        res = lax.fori_loop(0, cnt[qt], body, (one,) * HG)
        ctx_ref[at, :] = jnp.concatenate([r[2] / r[1] for r in res], axis=0).T.astype(BF)
        lse_ref[:, at] = jnp.concatenate([r[0] + jnp.log(r[1]) for r in res], axis=0)


def bwd_kernel(T, HG, lst, cnt, base, q_ref, k_ref, v_ref, ctx_ref, do_ref, lse_ref, lo_ref, hi_ref, out_ref, dqt, dl):
    n_tiles = q_ref.shape[0] // T
    W = HG * HD
    row = lax.broadcasted_iota(jnp.int32, (T, T), 0)
    lane = lax.broadcasted_iota(jnp.int32, (T, 2 * HD), 1)
    dqt[...] = jnp.zeros_like(dqt)

    @pl.loop(0, n_tiles)
    def _(t):
        at = pl.ds(pl.multiple_of(t * T, T), T)
        prod = (do_ref[at, :].astype(F32) * ctx_ref[at, :].astype(F32)).T
        dl[:, at] = jnp.concatenate([jnp.sum(prod[h * HD : (h + 1) * HD], axis=0, keepdims=True) for h in range(HG)], axis=0)

    @pl.loop(0, n_tiles)
    def _(kt):
        ks = pl.ds(pl.multiple_of(kt * T, T), T)
        k, v = k_ref[ks, :], v_ref[ks, :]
        kT = k.T
        kh, vh = [half(k, h) for h in range(HG)], [half(v, h) for h in range(HG)]

        def body(n, carry):
            at = pl.ds(pl.multiple_of(lst[kt, n] * T, T), T)
            q, do = q_ref[at, :], do_ref[at, :]
            vis = (row >= lo_ref[:, at] - base[kt]) & (row < hi_ref[:, at] - base[kt])
            raw = [dot_nt(kh[h], pair(q, h)) for h in range(HG)]
            dps = [dot_nt(vh[h], pair(do, h)) for h in range(HG)]
            out = []
            for h in range(HG):
                p = jnp.exp(jnp.where(vis, raw[h], NEG) - lse_ref[h : h + 1, at])
                ds = (p * (dps[h] - dl[h : h + 1, at])).astype(BF)
                out.append((carry[h][0] + dot(ds, pair(q, h)), carry[h][1] + dot(p.astype(BF), pair(do, h))))
                dqt[h * HD : (h + 1) * HD, at] += dot(kT[h * HD : (h + 1) * HD, :], ds)
            return tuple(out)

        one = (jnp.zeros((T, 2 * HD), F32), jnp.zeros((T, 2 * HD), F32))
        res = lax.fori_loop(0, cnt[kt], body, (one,) * HG)
        for p in range(HG // 2):
            cols = slice(p * 2 * HD, (p + 1) * 2 * HD)
            a, b = res[2 * p], res[2 * p + 1]
            out_ref[ks, W + cols.start : W + cols.stop] = jnp.where(lane < HD, a[0], b[0]).astype(BF)
            out_ref[ks, 2 * W + cols.start : 2 * W + cols.stop] = jnp.where(lane < HD, a[1], b[1]).astype(BF)

    @pl.loop(0, n_tiles)
    def _(t):
        at = pl.ds(pl.multiple_of(t * T, T), T)
        out_ref[at, :W] = (dqt[:, at].T * HD**-0.5).astype(BF)


def attend(kernel, scalars, ins, outs, scratch, flops):
    def spec(shape, cols):
        if cols is None:
            return pl.BlockSpec(shape, lambda i, *_: (0,) * len(shape))
        return pl.BlockSpec((shape[0], cols[0]), lambda i, *_: (0, cols[1]))

    size = sum(a.size * a.dtype.itemsize for a, _ in ins) + sum(o.size * o.dtype.itemsize for o in outs)
    return pl.pallas_call(
        kernel,
        out_shape=outs,
        grid_spec=pltpu.PrefetchScalarGridSpec(
            num_scalar_prefetch=len(scalars),
            grid=(1,),
            in_specs=[spec(a.shape, cols) for a, cols in ins],
            out_specs=[spec(o.shape, None) for o in outs],
            scratch_shapes=scratch,
        ),
        compiler_params=pltpu.CompilerParams(vmem_limit_bytes=AV << 20),
        cost_estimate=pl.CostEstimate(flops=flops, bytes_accessed=size, transcendentals=0),
    )(*scalars, *[a for a, _ in ins])


def grid_call(kernel, grid, scalars, ins, outs, flops, scratch=(), aliases=None, vmem=VM, light=1):
    def spec(block, index):
        return pl.BlockSpec(memory_space=pl.ANY) if block is None else pl.BlockSpec(block, index)

    size = sum(a.size * a.dtype.itemsize for a, b, _ in ins if b is not None)
    size += sum(o.size * o.dtype.itemsize for o, _, _ in outs)
    return pl.pallas_call(
        kernel,
        out_shape=[o for o, _, _ in outs],
        grid_spec=pltpu.PrefetchScalarGridSpec(
            num_scalar_prefetch=len(scalars),
            grid=grid,
            in_specs=[spec(b, m) for _, b, m in ins],
            out_specs=[spec(b, m) for _, b, m in outs],
            scratch_shapes=list(scratch),
        ),
        input_output_aliases=aliases or {},
        compiler_params=pltpu.CompilerParams(vmem_limit_bytes=vmem << 20),
        cost_estimate=pl.CostEstimate(flops=flops // light, bytes_accessed=size // light, transcendentals=0),
    )(*scalars, *[a for a, _, _ in ins])


def whole(a):
    return a.shape, lambda *_: (0,) * len(a.shape)


def centred(x):
    x = x.astype(F32)
    center = x - jnp.mean(x, axis=-1, keepdims=True)
    spread = jnp.mean(center * center, axis=-1, keepdims=True)
    return center * lax.rsqrt(spread + EPS)


def qkv_kernel(x_ref, g_ref, b_ref, w_ref, bias_ref, sc_ref, *refs):
    h_ref, o_ref = refs[-2:]
    h = (centred(x_ref[...]) * g_ref[...] + b_ref[...]).astype(BF)
    h_ref[...] = h
    o = (dot(h, w_ref[...]) + bias_ref[...]).astype(BF)
    o_ref[...] = (o.astype(F32) * sc_ref[...]).astype(BF)


def qkv_call(x, g, b, w, bias, sc, r, blocks, held):
    F, n = x.shape[0], w.shape[1]
    TR = min(256, F)
    per = F // TR
    row = lambda i: (i, 0)
    to = lambda i: (r * per + i, 0)
    ins = [(x, (TR, D), row)] + [(v, *whole(v)) for v in (g, b, w, bias, sc)]
    shapes = [jax.ShapeDtypeStruct((blocks * F, D), BF), jax.ShapeDtypeStruct((blocks * F, n), BF)]
    aliases = {}
    if held is not None:
        ins += [(held[0], None, None), (held[1], None, None)]
        aliases = {6: 0, 7: 1}
    return grid_call(qkv_kernel, (per,), (), ins, [(shapes[0], (TR, D), to), (shapes[1], (TR, n), to)],
                     2 * F * D * n, aliases=aliases)


def out_kernel(n, group_ref, *refs):
    x_ref, bias_ref, g_ref, b_ref, mid_ref, h_ref = refs[2 * n :]
    mid = sum(dot(refs[i][...], refs[n + i][...]) for i in range(n)) + bias_ref[...]
    mid = x_ref[...].astype(F32) + mid
    mid_ref[...] = mid
    h_ref[...] = (centred(mid) * g_ref[...] + b_ref[...]).astype(BF)


def out_call(mine, groups, w_out, x, bias, g, b):
    F, n = x.shape[0], len(mine)
    W = mine[0].shape[1]
    TR = min(256, F)
    row = lambda i, gr: (i, 0)
    ins = [(m, (TR, W), row) for m in mine]
    ins += [(w_out, (W, D), lambda i, gr, r=r: (gr[r], 0)) for r in range(n)]
    ins += [(x, (TR, D), row)] + [(v, *whole(v)) for v in (bias, g, b)]
    return grid_call(functools.partial(out_kernel, n), (F // TR,), (groups,), ins,
                     [(jax.ShapeDtypeStruct((F, D), F32), (TR, D), row), (jax.ShapeDtypeStruct((F, D), BF), (TR, D), row)],
                     2 * F * D * D)


def ln2_kernel(dh_ref, mid_ref, up_ref, g_ref, w_ref, dy_ref, da_ref, dctx_ref, sum_ref):
    @pl.when(pl.program_id(0) == 0)
    def _():
        sum_ref[...] = jnp.zeros_like(sum_ref)

    mid, dh, up = mid_ref[...], dh_ref[...], up_ref[...].astype(F32)
    center = mid - jnp.mean(mid, axis=-1, keepdims=True)
    rstd = lax.rsqrt(jnp.mean(center * center, axis=-1, keepdims=True) + EPS)
    xh = center * rstd
    t = dh * g_ref[...]
    d = rstd * (t - jnp.mean(t, axis=-1, keepdims=True) - xh * jnp.mean(t * xh, axis=-1, keepdims=True))
    dy = up + d
    dy_ref[...] = dy
    da = dy.astype(BF)
    da_ref[...] = da
    dctx_ref[...] = dot_nt(da, w_ref[...]).astype(BF)
    for k, v in enumerate((dh * xh, dh, da.astype(F32), up)):
        sum_ref[k : k + 1, :] += jnp.sum(v, axis=0, keepdims=True)


def ln2_call(dh2, middle, up, g, w_out):
    F = up.shape[0]
    TR = min(256, F)
    row = lambda i: (i, 0)
    sds = jax.ShapeDtypeStruct
    return grid_call(
        ln2_kernel, (F // TR,), (),
        [(dh2, (TR, D), row), (middle, (TR, D), row), (up, (TR, D), row), (g, *whole(g)), (w_out, *whole(w_out))],
        [(sds((F, D), F32), (TR, D), row), (sds((F, D), BF), (TR, D), row), (sds((F, D), BF), (TR, D), row),
         (sds((4, D), F32), (4, D), lambda i: (0, 0))], 2 * F * D * D)


def mlp_kernel(sub, h_ref, w_ref, b_ref, dg_ref, act_ref, du_ref, dh_ref, bu_ref):
    rows = h_ref.shape[0]

    @pl.when(pl.program_id(0) == 0)
    def _():
        dh_ref[...] = jnp.zeros_like(dh_ref)

    bu = jnp.zeros(bu_ref.shape, F32)
    for r in range(0, rows, sub):
        at = slice(r, r + sub)
        u = dot(h_ref[at, :], w_ref[...]) + b_ref[...]
        cdf = 0.5 + 0.5 * lax.erf(u * 0.7071067811865476)
        pdf = jnp.exp(-0.5 * u * u) * 0.3989422804014327
        act_ref[at, :] = (u * cdf).astype(BF)
        du = (dg_ref[at, :].astype(F32) * (cdf + u * pdf)).astype(BF)
        du_ref[at, :] = du
        bu = bu + jnp.sum(du.astype(F32), axis=0, keepdims=True)
        dh_ref[at, :] += dot_nt(du, w_ref[...])
    bu_ref[...] = bu


def dg_kernel(c_ref, w_ref, o_ref):
    o_ref[...] = dot_nt(c_ref[...], w_ref[...]).astype(BF)


def dg_call(c, w_down):
    F, FF = c.shape[0], w_down.shape[0]
    N = 512
    (out,) = grid_call(dg_kernel, (FF // N,), (), [(c, *whole(c)), (w_down, (N, D), lambda i: (i, 0))],
                       [(jax.ShapeDtypeStruct((F, FF), BF), (F, N), lambda i: (0, i))], 2 * F * D * FF)
    return out


def down_kernel(a_ref, w_ref, mid_ref, bias_ref, o_ref, acc):
    k = pl.program_id(0)

    @pl.when(k == 0)
    def _():
        acc[...] = mid_ref[...] + bias_ref[...]

    acc[...] += dot(a_ref[...], w_ref[...])

    @pl.when(k == pl.num_programs(0) - 1)
    def _():
        o_ref[...] = acc[...].astype(BF)


def down_call(act, w_down, middle, bias):
    F, FF = act.shape
    N = 1024
    (out,) = grid_call(
        down_kernel, (FF // N,), (),
        [(act, (F, N), lambda k: (0, k)), (w_down, (N, D), lambda k: (k, 0)), (middle, *whole(middle)), (bias, *whole(bias))],
        [(jax.ShapeDtypeStruct((F, D), BF), (F, D), lambda k: (0, 0))], 2 * F * D * FF,
        scratch=[pltpu.VMEM((F, D), F32)], light=8)
    return out


def mlp_call(h2, w_up, bias_up, dg):
    F, FF = dg.shape
    N = 1024
    sds = jax.ShapeDtypeStruct
    col = lambda i: (0, i)
    return grid_call(
        functools.partial(mlp_kernel, min(256, F)), (FF // N,), (),
        [(h2, *whole(h2)), (w_up, (D, N), col), (bias_up, (1, N), col), (dg, (F, N), col)],
        [(sds((F, FF), BF), (F, N), col), (sds((F, FF), BF), (F, N), col), (sds((F, D), F32), (F, D), lambda i: (0, 0)),
         (sds((1, FF), F32), (1, N), col)], 4 * F * D * FF, vmem=28)


def wgrad_kernel(put, n, half_ref, *refs):
    put([dot_tn(refs[2 * i][...], refs[2 * i + 1][...]) for i in range(n)], refs[2 * n :])


def wgrad_rows(a, b, side, Y, B, add=None, splits=()):
    k, M = a.shape
    N = b.shape[1] // 2
    W, R = N // Y, M // B
    per = min(B, max(1, 1024 // R))
    idx = lambda i, h: (i, 0, 0, 0)
    ends = list(splits) + [R]

    def put(prods, refs):
        (o,) = prods
        for p in range(per):
            for q in range(Y):
                v = o[p * R : (p + 1) * R, q * W : (q + 1) * W]
                if add is not None:
                    v = v + refs[0][p, q].astype(F32)
                v = v.astype(BF)
                for ref, lo, hi in zip(refs[-len(ends) :], [0] + ends, ends):
                    ref[p, q] = v[lo:hi]

    ins = [(a, (k, per * R), lambda i, h: (0, i)), (b, (k, N), lambda i, h: (0, h[0]))]
    if add is not None:
        ins.append((add, (per, Y, R, W), idx))
    sizes = [hi - lo for lo, hi in zip([0] + ends, ends)]
    return grid_call(functools.partial(wgrad_kernel, put, 1), (B // per,), (side.reshape(1),), ins,
                     [(jax.ShapeDtypeStruct((B, Y, r, W), BF), (per, Y, r, W), idx) for r in sizes], 2 * k * M * N)


def wgrad_cols(a, b, side, Y, B, W, add=None, splits=(), lead=None):
    k, M = a.shape
    R, cut = M // B, b.shape[1] // (2 * Y * W)
    before = 0 if lead is None else lead.shape[2]
    rows = R * cut
    idx = lambda j, h: (0, j, 0, 0)
    ends = [before + e for e in splits] + [before + rows]

    def put(prods, refs):
        (o,) = prods
        if lead is not None:
            refs[-1][:, 0, :before] = refs[-2][:, 0]
        for p in range(cut):
            v = o[:, p * W : (p + 1) * W].reshape(B, R, W)
            if add is not None:
                v = v + refs[0][:, 0, p * R : (p + 1) * R].astype(F32)
            v = v.astype(BF)
            for ref, lo, hi in zip(refs[-len(ends) :], [0] + ends, ends):
                a0, a1 = max(lo, before + p * R), min(hi, before + (p + 1) * R)
                if a0 < a1:
                    ref[:, 0, a0 - lo : a1 - lo] = v[:, a0 - before - p * R : a1 - before - p * R]

    ins = [(a, *whole(a)), (b, (k, cut * W), lambda j, h: (0, h[0] * Y + j))]
    if add is not None:
        ins.append((add, (B, 1, rows, W), idx))
    if lead is not None:
        ins.append((lead, (B, 1, before, W), idx))
    sizes = [hi - lo for lo, hi in zip([0] + ends, ends)]
    return grid_call(functools.partial(wgrad_kernel, put, 1), (Y,), (side.reshape(1),), ins,
                     [(jax.ShapeDtypeStruct((B, Y, r, W), BF), (B, 1, r, W), idx) for r in sizes],
                     2 * k * M * b.shape[1] // 2)


def qgrad_kernel(a_ref, b_ref, o_ref):
    o_ref[...] = dot_tn(a_ref[...], b_ref[...]).reshape(o_ref.shape).astype(BF)


def qgrad(h_all, dqkv, B):
    S, n = dqkv.shape
    W = n // 3
    (out,) = grid_call(
        qgrad_kernel, (3,), (), [(h_all, *whole(h_all)), (dqkv, (S, W), lambda p: (0, p))],
        [(jax.ShapeDtypeStruct((B, 3 * D // B, W), BF), (B, D // B, W), lambda p: (0, p, 0))], 2 * S * D * n, light=8)
    return out


def dh_kernel(n_far, dq_ref, got_ref, w_ref, wm_ref, x_ref, far_ref, own_ref, sum_ref):
    i = pl.program_id(0)

    @pl.when(i == 0)
    def _():
        sum_ref[...] = jnp.zeros_like(sum_ref)

    part = dot_nt(dq_ref[...], w_ref[...]) + dot_nt(got_ref[...], wm_ref[...])
    low = part.astype(BF)

    @pl.when(i < n_far)
    def _():
        far_ref[...] = low

    @pl.when(i >= n_far)
    def _():
        own_ref[...] = low

    sum_ref[0:1, :] += jnp.sum(part * centred(x_ref[...]), axis=0, keepdims=True)
    sum_ref[1:2, :] += jnp.sum(part, axis=0, keepdims=True)


def dh_call(dqkv, got, w_g, w_m, x_all, Y):
    S, n = dqkv.shape
    F = S // (2 * Y)
    TR = min(256, F)
    per = F // TR
    n_far = (Y - 1) * per
    block = lambda i: (i // per + 1) % Y
    full = lambda i: (2 * block(i) * per + i % per, 0)
    sds = jax.ShapeDtypeStruct
    return grid_call(
        functools.partial(dh_kernel, n_far), (Y * per,), (),
        [(dqkv, (TR, n), full), (got, (TR, n), lambda i: (block(i) * per + i % per, 0)), (w_g, *whole(w_g)),
         (w_m, *whole(w_m)), (x_all, (TR, D), full)],
        [(sds(((Y - 1) * F, D), BF), (TR, D), lambda i: (jnp.minimum(i, n_far - 1), 0)),
         (sds((F, D), BF), (TR, D), lambda i: (jnp.maximum(i - n_far, 0), 0)),
         (sds((2, D), F32), (2, D), lambda i: (0, 0))],
        2 * S * D * n, light=8)


def tile_list(active):
    m = active.shape[1]
    hit = active.astype(jnp.int32)
    upto = jnp.tril(jnp.ones((m, m), jnp.int32))
    rank = jnp.sum(hit[:, None, :] * upto[None], axis=2) - 1
    ids = jnp.arange(m, dtype=jnp.int32)
    here = (rank[:, :, None] == ids[None, None, :]) & active[:, :, None]
    return jnp.sum(jnp.where(here, ids[None, :, None], 0), axis=1), jnp.sum(hit, axis=1)


def after(vals, deps):
    return lax.optimization_barrier((vals, deps))[0]


def shards(Z, X, Y, inputs, ln1_gain, ln1_bias, w_qkv, bias_q, bias_v, w_out, bias_out, ln2_gain, ln2_bias,
           w_up, bias_up, w_down, bias_down, lengths, cotangent):
    F = inputs.shape[1]
    K = 2 * Y
    S = F * K
    T = min(256, F)
    W = D // K
    HG = H // K
    B = Z * X
    zi, xi, y, c = (lax.axis_index(n) for n in ("z", "x", "y", "c"))
    group = y * 2 + c
    sds = jax.ShapeDtypeStruct

    def shift(v, axis, n, s):
        return lax.ppermute(v, axis, [(i, (i + s) % n) for i in range(n)])

    def mate(v):
        return lax.ppermute(v, "c", [(0, 1), (1, 0)])

    rel = [(s, d) for s in range(Y) for d in range(2)]

    def hop(v, s, d):
        pairs = [(yy * 2 + cc, ((yy + s) % Y) * 2 + (cc ^ d)) for yy in range(Y) for cc in range(2)]
        return lax.ppermute(v, ("y", "c"), pairs)

    def flip(d):
        return c if d == 0 else 1 - c

    blocks = jnp.stack([((y - s) % Y) * 2 + flip(d) for s, d in rel])
    ends = jnp.cumsum(lengths.reshape(-1))
    pos = (blocks[:, None] * F + jnp.arange(F, dtype=jnp.int32)[None]).reshape(1, S)
    piece = jnp.sum((pos >= ends[:, None]).astype(jnp.int32), axis=0, keepdims=True)
    pieces = ends.shape[0]
    starts = jnp.concatenate([jnp.zeros((1,), ends.dtype), ends[:-1]])

    def look(table, idx):
        return jnp.sum(jnp.where(idx == jnp.arange(pieces)[:, None], table[:, None], 0), axis=0, keepdims=True)

    pad = piece >= pieces
    lo = jnp.where(pad, pos, look(starts, (piece // 3) * 3)).astype(jnp.int32)
    hi = jnp.where(pad | (piece % 3 == 2), pos + 1, look(ends, piece)).astype(jnp.int32)
    base = pos[0, ::T].astype(jnp.int32)
    qlo = jnp.min(lo.reshape(S // T, T), axis=1)
    qhi = jnp.max(hi.reshape(S // T, T), axis=1)
    active = (base[None, :] < qhi[:, None]) & (base[None, :] + T > qlo[:, None])
    lst_q, cnt_q = tile_list(active)
    lst_k, cnt_k = tile_list(active.T)

    x_own = inputs.reshape(F, D)
    up = cotangent.reshape(F, D)
    flat_in = x_own.astype(F32)

    def cols_of(w, g):
        return [lax.dynamic_slice_in_dim(w, part * D + g * W, W, w.ndim - 1) for part in range(3)]

    far = [shift(x_own, "y", Y, s) for s in range(1, Y)]
    near = mate(x_own)
    w_g = jnp.concatenate(cols_of(w_qkv, group), axis=1)
    w_m = jnp.concatenate(cols_of(w_qkv, y * 2 + 1 - c), axis=1)
    b_g = jnp.concatenate([lax.dynamic_slice_in_dim(bias_q, group * W, W, 0), jnp.zeros((W,), F32),
                           lax.dynamic_slice_in_dim(bias_v, group * W, W, 0)])[None]
    sc_g = jnp.where(jnp.arange(3 * W) < W, HD**-0.5, 1.0).astype(F32)[None]
    ln1 = (ln1_gain[None], ln1_bias[None])
    held = qkv_call(x_own, *ln1, w_g, b_g, sc_g, 0, K, None)
    held = qkv_call(near, *ln1, w_g, b_g, sc_g, 1, K, held)
    dg = dg_call(after(up, held[1]), w_down)
    xs = [x_own, near]
    for i, r in enumerate(far):
        r = after(r, dg) if i == 0 else r
        xs += [r, mate(r)]
        held = qkv_call(xs[-2], *ln1, w_g, b_g, sc_g, 2 * i + 2, K, held)
        held = qkv_call(xs[-1], *ln1, w_g, b_g, sc_g, 2 * i + 3, K, held)
    h_all, qkv = held
    lse_shape = sds((HG, S), F32)
    ctx_g, lse = attend(
        functools.partial(fwd_kernel, T, HG), (lst_q, cnt_q, base),
        [(qkv, (W, 0)), (qkv, (W, 1)), (qkv, (W, 2)), (lo, None), (hi, None)],
        [sds((S, W), BF), lse_shape], [], 12 * 10**9)

    mine = [ctx_g[:F]] + [hop(ctx_g[(2 * s + d) * F : (2 * s + d + 1) * F], -s, d) for s, d in rel[1:]]
    x_all = jnp.concatenate(after(xs, ctx_g), axis=0)
    mine[1:] = after(mine[1:], x_all)
    groups = jnp.stack([((y + s) % Y) * 2 + flip(d) for s, d in rel]).astype(jnp.int32)
    middle, h2 = out_call([ctx_g] + mine[1:], groups, w_out, x_own, bias_out[None], ln2_gain[None], ln2_bias[None])
    act, du, dh2, g_bu = mlp_call(h2, w_up, bias_up[None], dg)
    mine = jnp.stack(after(mine, dh2))
    ctx = jnp.concatenate(
        [lax.dynamic_index_in_dim(mine, ((yy - y) % Y) * 2 + (cc ^ c), 0, keepdims=False)
         for yy in range(Y) for cc in range(2)], axis=1)

    def shaped(g):
        return g.reshape(Z, X, Y, g.shape[2], W)

    def begin(items, n, me, send, dep=None):
        def cut(g, axis, i):
            return lax.dynamic_index_in_dim(g, i, axis, keepdims=False)

        def piece(terms, axis, i):
            return settle([cut(g, axis, i) for g in terms]).reshape(-1, W)

        bufs = [jnp.concatenate([piece(g, ax, (me + s) % n) for g, ax in items]) for s in range(1, n)]
        if dep is not None:
            bufs = after(bufs, dep)
        return [[cut(g, ax, me) for g in terms] for terms, ax in items], [send(b, s + 1) for s, b in enumerate(bufs)], bufs

    def settle(terms):
        return sum((g.astype(F32) for g in terms[1:]), terms[0].astype(F32)).astype(BF)

    def finish(state):
        own, sent, _ = state
        out, at = [], 0
        for terms in own:
            rows = terms[0].size // W
            out.append(terms + [r[at : at + rows].reshape(terms[0].shape) for r in sent])
            at += rows
        return out

    def hold(states, others):
        sent, others = lax.optimization_barrier(([st[1] for st in states], others))
        return [(st[0], r, st[2]) for st, r in zip(states, sent)], others

    def head(terms):
        return [g[0] for g in terms]

    def over_y(items):
        return begin(items, Y, y, lambda v, s: shift(v, "y", Y, s))

    def over_x(items):
        return begin(items, X, xi, lambda v, s: shift(v, "x", X, s))

    def over_z(items, bit, dep=None):
        bits = [([g.reshape((g.shape[0] // 2, 2) + g.shape[1:]) for g in terms], 1) for terms in items]
        return begin(bits, 2, (zi // bit) % 2, lambda v, s: lax.ppermute(v, "z", [(i, i ^ bit) for i in range(Z)]), dep)

    assert Z & (Z - 1) == 0
    zbits = [1 << i for i in range(Z.bit_length() - 1)]

    def total(v):
        return jnp.sum(v.astype(F32), axis=0)

    def rows_of(vecs):
        return jnp.concatenate([v.reshape(B, -1) for v in vecs], axis=1).astype(BF).reshape(B, -1, W)

    hr = w_down.shape[0] // B // 2
    n_ot = D // B
    ur = hr + n_ot // 2

    (dn_give,) = wgrad_rows(act, up, 1 - c, Y, B)
    dn_got = mate(dn_give)
    (up_give,) = wgrad_cols(h2, after(du, dn_give), 1 - c, Y, B, W)
    up_got = mate(up_give)
    dy1, da, dctx, sums = ln2_call(after(dh2, up_give), middle, up, ln2_gain[None], w_out)

    def heads_of(s, d):
        return lax.dynamic_slice_in_dim(dctx, (((y + s) % Y) * 2 + flip(d)) * W, W, 1)

    def both(s):
        return jnp.concatenate([heads_of(s, 0), heads_of(s, 1)])

    do_y = [both(0)] + [shift(both(s), "y", Y, s) for s in range(1, Y)]

    dnP, dnQ = wgrad_rows(act, after(up, do_y[0]), c, Y, B, dn_got, (hr,))
    t_y, t_x = over_y([([shaped(dnP)], 2)]), over_x([([shaped(dnQ)], 1)])
    ctx_, da_ = after((ctx, da), (t_y[2], t_x[2]))
    (ot_give,) = wgrad_cols(ctx_, da_, 1 - c, Y, B, W)
    ot_got = mate(ot_give)
    upQ, upP = wgrad_cols(h2, after(du, ot_give), c, Y, B, W, up_got, (ur,))
    do_y = after(do_y, ot_give)
    do_c = mate(jnp.concatenate([v[F:] for v in do_y]))
    do_g = jnp.concatenate([b for s in range(Y) for b in (do_y[s][:F], do_c[s * F : (s + 1) * F])])
    (upP,) = wgrad_cols(ctx_, da_, c, Y, B, W, ot_got, (), upP)
    n_y, n_x = over_y([([shaped(upP)], 2)]), over_x([([shaped(upQ)], 1)])
    (t_y, t_x), (n_bufs, do_g) = hold([t_y, t_x], ((n_y[2], n_x[2]), do_g))
    (dnP,), (dnQ,) = finish(t_y), finish(t_x)

    t_y, t_x, t_z = n_y, n_x, over_z([dnQ], 1)
    dnP = settle(dnP)
    early = rows_of([sums[2], sums[0], sums[1], sums[3], g_bu[0]])
    do_g = after(do_g, (n_bufs, t_z[2], early, dnP))
    (dqkv,) = attend(
        functools.partial(bwd_kernel, T, HG), (lst_k, cnt_k, base),
        [(qkv, (W, 0)), (qkv, (W, 1)), (qkv, (W, 2)), (ctx_g, None), (do_g, None), (lse, None), (lo, None), (hi, None)],
        [sds((S, 3 * W), BF)], [pltpu.VMEM((W, S), F32), pltpu.VMEM((HG, S), F32)], 20 * 10**9)
    (t_y, t_x, t_z), (dqkv, dnP) = hold([t_y, t_x, t_z], (dqkv, dnP))
    (upP,), (upQ,), (dnQ,) = finish(t_y), finish(t_x), finish(t_z)

    def of_x(i):
        return jnp.concatenate([settle([lax.dynamic_index_in_dim(g, i, 1, keepdims=False) for g in terms])
                                for terms in ([dnP], upP)], axis=1)

    p_bufs, p_own = [of_x((xi + s) % X) for s in range(1, X)], of_x(xi)
    t_x = ([[p_own]], [shift(b, "x", X, s + 1) for s, b in enumerate(p_bufs)], p_bufs)
    t_a, t_b = over_z([upQ], 1), over_z([dnQ], zbits[1])
    dq_got = mate(dqkv.reshape(Y, 2, F, 3 * W)[:, 1].reshape(Y * F, 3 * W))
    qv = qgrad(h_all, after(dqkv, (p_bufs, t_a[2])), B)
    dh_far, dh_own, g_ln1 = dh_call(dqkv, after(dq_got, qv), w_g, w_m, x_all, Y)
    far = [shift(dh_far[s * F : (s + 1) * F], "y", Y, -s - 1) for s in range(Y - 1)]
    cols = total(dqkv)
    mine_only = jnp.arange(D) // W == group
    late = rows_of([g_ln1[0], g_ln1[1]] + [jnp.where(mine_only, jnp.tile(v, K), 0.0) for v in (cols[:W], cols[2 * W :])])
    vec = jnp.concatenate([late, early], axis=1)
    vec = jnp.pad(vec, ((0, 0), (0, -vec.shape[1] % 16), (0, 0)))
    qv = jnp.concatenate([qv, vec], axis=1).reshape(Z, X, -1, W)
    n_x = over_x([([qv], 1)])
    (t_x, t_a, t_b), n_bufs = hold([t_x, t_a, t_b], n_x[2])
    parts, upQ, dnQ = [p_own] + t_x[1], finish(t_a)[0], finish(t_b)[0]

    t_x = n_x
    t_a, t_b = over_z([parts], 1), over_z([upQ], zbits[1])
    result = down_call(after(act, (n_bufs, t_a[2], t_b[2])), w_down, middle, bias_down[None])
    (t_x, t_a, t_b), (far, result) = hold([t_x, t_a, t_b], (far, result))

    def rest(items, k):
        for bit in zbits[k:]:
            items = finish(over_z(items, bit))
        return items

    (qv,), (parts,), (upQ,), (dnQ,) = finish(t_x), finish(t_a), rest(finish(t_b), 2), rest([dnQ], 2)

    t_a, t_b = over_z([qv], 1), over_z([parts], zbits[1])
    t_y = over_y([(head(dnQ), 0), (head(upQ), 0)])
    far, dh_own = after((far, dh_own), (t_a[2], t_b[2], t_y[2]))
    dh1 = sum((r.astype(F32) for r in far), dh_own.astype(F32))
    _, norm_back_one = jax.vjp(lambda v: layer_norm(v, ln1_gain, ln1_bias), flat_in)
    (dx,) = norm_back_one(dh1)
    grad_inputs = (dy1 + dx).reshape(1, F, D)
    (t_a, t_b, t_y), grad_inputs = hold([t_a, t_b, t_y], grad_inputs)
    (qv,), (parts,), (dnQ, upQ) = finish(t_a), rest(finish(t_b), 2), finish(t_y)

    parts = settle(head(parts))
    first = jnp.concatenate([parts[:hr], settle(dnQ), settle(upQ), parts[hr:]])

    def share_y(g):
        return [g] + [shift(g, "y", Y, s) for s in range(1, Y)]

    t_b = over_z([qv], zbits[1])
    first_y = share_y(first)
    (t_b,), first_y = hold([t_b], first_y)
    (qv,) = rest(finish(t_b), 2)
    tail_y = share_y(settle(head(qv)))

    def share_c(got):
        got = jnp.stack(got)
        other = mate(got)

        def piece(yy, cc):
            i = (y - yy) % Y
            return jnp.where(cc == c, lax.dynamic_index_in_dim(got, i, 0, keepdims=False),
                             lax.dynamic_index_in_dim(other, i, 0, keepdims=False))

        return [[piece(yy, cc) for cc in range(2)] for yy in range(Y)]

    def by_columns(e, at, rows, chunks):
        return jnp.concatenate([e[yy][cc][at + k * rows : at + (k + 1) * rows] for cc in range(2) for yy in range(Y)
                                for k in range(chunks)], axis=1).astype(F32)

    first_e = share_c(first_y)
    n_dn = 2 * hr
    g_w_down = by_columns(first_e, 0, n_dn, 1)
    g_w_up = by_columns(first_e, n_dn, n_ot, 2 * ur // n_ot - 1)
    g_w_out = by_columns(first_e, n_dn + 2 * ur - n_ot, n_ot, 1)
    tail_y, g_w_down, g_w_up, g_w_out = lax.optimization_barrier((tail_y, g_w_down, g_w_up, g_w_out))
    tail_e = share_c(tail_y)
    g_w_qkv = jnp.concatenate([tail_e[yy][cc][p * n_ot : (p + 1) * n_ot] for p in range(3) for yy in range(Y)
                               for cc in range(2)], axis=1).astype(F32)
    at = 3 * n_ot
    flat = sum(tail_e[yy][cc][at:].astype(F32) for yy in range(Y) for cc in range(2)).reshape(-1)
    out, at = [], 0
    for n in (D, D, D, D, D, D, D, D, w_up.shape[1]):
        out.append(flat[at : at + n // B])
        at += n // B
    g_ln1g, g_ln1b, g_bq, g_bv, g_bo, g_ln2g, g_ln2b, g_bd, g_bu = out
    return (result.reshape(1, F, D), grad_inputs, g_ln1g, g_ln1b, g_w_qkv, g_bq, g_bv, g_w_out, g_bo, g_ln2g, g_ln2b,
            g_w_up, g_bu, g_w_down, g_bd)


def solution(mesh):
    batch, blk = mesh.shape["batch"], mesh.shape["blk"]
    Y = blk // 2
    X = Y if batch % Y == 0 else 1
    Z = batch // X
    fine = Mesh(mesh.devices.reshape(Z, X, Y, 2), ("z", "x", "y", "c"))
    rows, slots = ("z", "x"), ("y", "c")
    act = P(rows, slots, None)
    flat, mat = P(rows), P(rows, None)
    return jax.shard_map(
        functools.partial(shards, Z, X, Y),
        mesh=fine,
        in_specs=(act,) + (P(),) * 13 + (P(rows, None, None), act),
        out_specs=(act, act, flat, flat, mat, flat, flat, mat, flat, flat, flat, mat, flat, mat, flat),
        check_vma=False,
    )
```

```python
import functools

import jax
import jax.numpy as jnp
from jax import lax
from jax.experimental import pallas as pl
from jax.experimental.pallas import tpu as pltpu
from jax.sharding import Mesh
from jax.sharding import PartitionSpec as P

D = 1024
H = 16
HD = 64
EPS = 1e-05
NEG = -1e30
VM = 20
AV = 28
BF = jnp.bfloat16
F32 = jnp.float32


def layer_norm(values, gain_vec, shift_vec):
    center = values - jnp.mean(values, axis=-1, keepdims=True)
    spread = jnp.mean(center * center, axis=-1, keepdims=True)
    return center * lax.rsqrt(spread + EPS) * gain_vec + shift_vec


def dot(a, b):
    return jnp.dot(a, b, preferred_element_type=F32)


def dot_tn(a, b):
    return lax.dot_general(a, b, (((0,), (0,)), ((), ())), preferred_element_type=F32)


def dot_nt(a, b):
    return lax.dot_general(a, b, (((1,), (1,)), ((), ())), preferred_element_type=F32)


def half(a, h):
    a = a[:, (h // 2) * 2 * HD : (h // 2 + 1) * 2 * HD]
    lane = lax.broadcasted_iota(jnp.int32, a.shape, 1)
    zero = jnp.zeros_like(a)
    return jnp.where(lane < HD, a, zero) if h % 2 == 0 else jnp.where(lane < HD, zero, a)


def pair(a, h):
    return a[:, (h // 2) * 2 * HD : (h // 2 + 1) * 2 * HD]


def fwd_kernel(T, HG, lst, cnt, base, q_ref, k_ref, v_ref, lo_ref, hi_ref, ctx_ref, lse_ref):
    nq = q_ref.shape[0] // T
    row = lax.broadcasted_iota(jnp.int32, (T, T), 0)

    @pl.loop(0, nq)
    def _(qt):
        at = pl.ds(pl.multiple_of(qt * T, T), T)
        q = q_ref[at, :]
        qh = [half(q, h) for h in range(HG)]
        lo, hi = lo_ref[:, at], hi_ref[:, at]

        def body(n, carry):
            t = lst[qt, n]
            ks = pl.ds(pl.multiple_of(t * T, T), T)
            k, v = k_ref[ks, :], v_ref[ks, :].T
            vis = (row >= lo - base[t]) & (row < hi - base[t])
            raw = [dot_nt(pair(k, h), qh[h]) for h in range(HG)]
            out = []
            for h in range(HG):
                m, l, acc = carry[h]
                s = jnp.where(vis, raw[h], NEG)
                mn = jnp.maximum(m, jnp.max(s, axis=0, keepdims=True))
                a = jnp.exp(m - mn)
                p = jnp.exp(s - mn)
                l = a * l + jnp.sum(p, axis=0, keepdims=True)
                acc = acc * a + dot(v[h * HD : (h + 1) * HD, :], p.astype(BF))
                out.append((mn, l, acc))
            return tuple(out)

        one = (jnp.full((1, T), NEG, F32), jnp.zeros((1, T), F32), jnp.zeros((HD, T), F32))
        res = lax.fori_loop(0, cnt[qt], body, (one,) * HG)
        ctx_ref[at, :] = jnp.concatenate([r[2] / r[1] for r in res], axis=0).T.astype(BF)
        lse_ref[:, at] = jnp.concatenate([r[0] + jnp.log(r[1]) for r in res], axis=0)


def bwd_kernel(T, HG, lst, cnt, base, q_ref, k_ref, v_ref, ctx_ref, do_ref, lse_ref, lo_ref, hi_ref, out_ref, dqt, dl):
    n_tiles = q_ref.shape[0] // T
    W = HG * HD
    row = lax.broadcasted_iota(jnp.int32, (T, T), 0)
    lane = lax.broadcasted_iota(jnp.int32, (T, 2 * HD), 1)
    dqt[...] = jnp.zeros_like(dqt)

    @pl.loop(0, n_tiles)
    def _(t):
        at = pl.ds(pl.multiple_of(t * T, T), T)
        prod = (do_ref[at, :].astype(F32) * ctx_ref[at, :].astype(F32)).T
        dl[:, at] = jnp.concatenate([jnp.sum(prod[h * HD : (h + 1) * HD], axis=0, keepdims=True) for h in range(HG)], axis=0)

    @pl.loop(0, n_tiles)
    def _(kt):
        ks = pl.ds(pl.multiple_of(kt * T, T), T)
        k, v = k_ref[ks, :], v_ref[ks, :]
        kT = k.T
        kh, vh = [half(k, h) for h in range(HG)], [half(v, h) for h in range(HG)]

        def body(n, carry):
            at = pl.ds(pl.multiple_of(lst[kt, n] * T, T), T)
            q, do = q_ref[at, :], do_ref[at, :]
            vis = (row >= lo_ref[:, at] - base[kt]) & (row < hi_ref[:, at] - base[kt])
            raw = [dot_nt(kh[h], pair(q, h)) for h in range(HG)]
            dps = [dot_nt(vh[h], pair(do, h)) for h in range(HG)]
            out = []
            for h in range(HG):
                p = jnp.exp(jnp.where(vis, raw[h], NEG) - lse_ref[h : h + 1, at])
                ds = (p * (dps[h] - dl[h : h + 1, at])).astype(BF)
                out.append((carry[h][0] + dot(ds, pair(q, h)), carry[h][1] + dot(p.astype(BF), pair(do, h))))
                dqt[h * HD : (h + 1) * HD, at] += dot(kT[h * HD : (h + 1) * HD, :], ds)
            return tuple(out)

        one = (jnp.zeros((T, 2 * HD), F32), jnp.zeros((T, 2 * HD), F32))
        res = lax.fori_loop(0, cnt[kt], body, (one,) * HG)
        for p in range(HG // 2):
            cols = slice(p * 2 * HD, (p + 1) * 2 * HD)
            a, b = res[2 * p], res[2 * p + 1]
            out_ref[ks, W + cols.start : W + cols.stop] = jnp.where(lane < HD, a[0], b[0]).astype(BF)
            out_ref[ks, 2 * W + cols.start : 2 * W + cols.stop] = jnp.where(lane < HD, a[1], b[1]).astype(BF)

    @pl.loop(0, n_tiles)
    def _(t):
        at = pl.ds(pl.multiple_of(t * T, T), T)
        out_ref[at, :W] = (dqt[:, at].T * HD**-0.5).astype(BF)


def attend(kernel, scalars, ins, outs, scratch, flops):
    def spec(shape, cols):
        if cols is None:
            return pl.BlockSpec(shape, lambda i, *_: (0,) * len(shape))
        return pl.BlockSpec((shape[0], cols[0]), lambda i, *_: (0, cols[1]))

    size = sum(a.size * a.dtype.itemsize for a, _ in ins) + sum(o.size * o.dtype.itemsize for o in outs)
    return pl.pallas_call(
        kernel,
        out_shape=outs,
        grid_spec=pltpu.PrefetchScalarGridSpec(
            num_scalar_prefetch=len(scalars),
            grid=(1,),
            in_specs=[spec(a.shape, cols) for a, cols in ins],
            out_specs=[spec(o.shape, None) for o in outs],
            scratch_shapes=scratch,
        ),
        compiler_params=pltpu.CompilerParams(vmem_limit_bytes=AV << 20),
        cost_estimate=pl.CostEstimate(flops=flops, bytes_accessed=size, transcendentals=0),
    )(*scalars, *[a for a, _ in ins])


def grid_call(kernel, grid, scalars, ins, outs, flops, scratch=(), aliases=None, vmem=VM, light=1):
    def spec(block, index):
        return pl.BlockSpec(memory_space=pl.ANY) if block is None else pl.BlockSpec(block, index)

    size = sum(a.size * a.dtype.itemsize for a, b, _ in ins if b is not None)
    size += sum(o.size * o.dtype.itemsize for o, _, _ in outs)
    return pl.pallas_call(
        kernel,
        out_shape=[o for o, _, _ in outs],
        grid_spec=pltpu.PrefetchScalarGridSpec(
            num_scalar_prefetch=len(scalars),
            grid=grid,
            in_specs=[spec(b, m) for _, b, m in ins],
            out_specs=[spec(b, m) for _, b, m in outs],
            scratch_shapes=list(scratch),
        ),
        input_output_aliases=aliases or {},
        compiler_params=pltpu.CompilerParams(vmem_limit_bytes=vmem << 20),
        cost_estimate=pl.CostEstimate(flops=flops // light, bytes_accessed=size // light, transcendentals=0),
    )(*scalars, *[a for a, _, _ in ins])


def whole(a):
    return a.shape, lambda *_: (0,) * len(a.shape)


def centred(x):
    x = x.astype(F32)
    center = x - jnp.mean(x, axis=-1, keepdims=True)
    spread = jnp.mean(center * center, axis=-1, keepdims=True)
    return center * lax.rsqrt(spread + EPS)


def qkv_kernel(x_ref, g_ref, b_ref, w_ref, bias_ref, sc_ref, *refs):
    h_ref, o_ref = refs[-2:]
    h = (centred(x_ref[...]) * g_ref[...] + b_ref[...]).astype(BF)
    h_ref[...] = h
    o = (dot(h, w_ref[...]) + bias_ref[...]).astype(BF)
    o_ref[...] = (o.astype(F32) * sc_ref[...]).astype(BF)


def qkv_call(x, g, b, w, bias, sc, r, blocks, held):
    F, n = x.shape[0], w.shape[1]
    TR = min(128, F)
    per = F // TR
    row = lambda i: (i, 0)
    to = lambda i: (r * per + i, 0)
    ins = [(x, (TR, D), row)] + [(v, *whole(v)) for v in (g, b, w, bias, sc)]
    shapes = [jax.ShapeDtypeStruct((blocks * F, D), BF), jax.ShapeDtypeStruct((blocks * F, n), BF)]
    aliases = {}
    if held is not None:
        ins += [(held[0], None, None), (held[1], None, None)]
        aliases = {6: 0, 7: 1}
    return grid_call(qkv_kernel, (per,), (), ins, [(shapes[0], (TR, D), to), (shapes[1], (TR, n), to)],
                     2 * F * D * n, aliases=aliases)


def out_kernel(n, group_ref, *refs):
    x_ref, bias_ref, g_ref, b_ref, mid_ref, h_ref = refs[2 * n :]
    mid = sum(dot(refs[i][...], refs[n + i][...]) for i in range(n)) + bias_ref[...]
    mid = x_ref[...].astype(F32) + mid
    mid_ref[...] = mid
    h_ref[...] = (centred(mid) * g_ref[...] + b_ref[...]).astype(BF)


def out_call(mine, groups, w_out, x, bias, g, b):
    F, n = x.shape[0], len(mine)
    W = mine[0].shape[1]
    TR = min(256, F)
    row = lambda i, gr: (i, 0)
    ins = [(m, (TR, W), row) for m in mine]
    ins += [(w_out, (W, D), lambda i, gr, r=r: (gr[r], 0)) for r in range(n)]
    ins += [(x, (TR, D), row)] + [(v, *whole(v)) for v in (bias, g, b)]
    return grid_call(functools.partial(out_kernel, n), (F // TR,), (groups,), ins,
                     [(jax.ShapeDtypeStruct((F, D), F32), (TR, D), row), (jax.ShapeDtypeStruct((F, D), BF), (TR, D), row)],
                     2 * F * D * D)


def ln2_kernel(dh_ref, mid_ref, up_ref, g_ref, w_ref, dy_ref, da_ref, dctx_ref, sum_ref):
    @pl.when(pl.program_id(0) == 0)
    def _():
        sum_ref[...] = jnp.zeros_like(sum_ref)

    mid, dh, up = mid_ref[...], dh_ref[...], up_ref[...].astype(F32)
    center = mid - jnp.mean(mid, axis=-1, keepdims=True)
    rstd = lax.rsqrt(jnp.mean(center * center, axis=-1, keepdims=True) + EPS)
    xh = center * rstd
    t = dh * g_ref[...]
    d = rstd * (t - jnp.mean(t, axis=-1, keepdims=True) - xh * jnp.mean(t * xh, axis=-1, keepdims=True))
    dy = up + d
    dy_ref[...] = dy
    da = dy.astype(BF)
    da_ref[...] = da
    dctx_ref[...] = dot_nt(da, w_ref[...]).astype(BF)
    for k, v in enumerate((dh * xh, dh, da.astype(F32), up)):
        sum_ref[k : k + 1, :] += jnp.sum(v, axis=0, keepdims=True)


def ln2_call(dh2, middle, up, g, w_out):
    F = up.shape[0]
    TR = min(256, F)
    row = lambda i: (i, 0)
    sds = jax.ShapeDtypeStruct
    return grid_call(
        ln2_kernel, (F // TR,), (),
        [(dh2, (TR, D), row), (middle, (TR, D), row), (up, (TR, D), row), (g, *whole(g)), (w_out, *whole(w_out))],
        [(sds((F, D), F32), (TR, D), row), (sds((F, D), BF), (TR, D), row), (sds((F, D), BF), (TR, D), row),
         (sds((4, D), F32), (4, D), lambda i: (0, 0))], 2 * F * D * D)


def mlp_kernel(sub, h_ref, w_ref, b_ref, dg_ref, act_ref, du_ref, dh_ref, bu_ref):
    rows = h_ref.shape[0]

    @pl.when(pl.program_id(0) == 0)
    def _():
        dh_ref[...] = jnp.zeros_like(dh_ref)

    bu = jnp.zeros(bu_ref.shape, F32)
    for r in range(0, rows, sub):
        at = slice(r, r + sub)
        u = dot(h_ref[at, :], w_ref[...]) + b_ref[...]
        cdf = 0.5 + 0.5 * lax.erf(u * 0.7071067811865476)
        pdf = jnp.exp(-0.5 * u * u) * 0.3989422804014327
        act_ref[at, :] = (u * cdf).astype(BF)
        du = (dg_ref[at, :].astype(F32) * (cdf + u * pdf)).astype(BF)
        du_ref[at, :] = du
        bu = bu + jnp.sum(du.astype(F32), axis=0, keepdims=True)
        dh_ref[at, :] += dot_nt(du, w_ref[...])
    bu_ref[...] = bu


def dg_kernel(c_ref, w_ref, o_ref):
    o_ref[...] = dot_nt(c_ref[...], w_ref[...]).astype(BF)


def dg_call(c, w_down):
    F, FF = c.shape[0], w_down.shape[0]
    N = 512
    (out,) = grid_call(dg_kernel, (FF // N,), (), [(c, *whole(c)), (w_down, (N, D), lambda i: (i, 0))],
                       [(jax.ShapeDtypeStruct((F, FF), BF), (F, N), lambda i: (0, i))], 2 * F * D * FF)
    return out


def down_kernel(a_ref, w_ref, mid_ref, bias_ref, o_ref, acc):
    k = pl.program_id(0)

    @pl.when(k == 0)
    def _():
        acc[...] = mid_ref[...] + bias_ref[...]

    acc[...] += dot(a_ref[...], w_ref[...])

    @pl.when(k == pl.num_programs(0) - 1)
    def _():
        o_ref[...] = acc[...].astype(BF)


def down_call(act, w_down, middle, bias):
    F, FF = act.shape
    N = 1024
    (out,) = grid_call(
        down_kernel, (FF // N,), (),
        [(act, (F, N), lambda k: (0, k)), (w_down, (N, D), lambda k: (k, 0)), (middle, *whole(middle)), (bias, *whole(bias))],
        [(jax.ShapeDtypeStruct((F, D), BF), (F, D), lambda k: (0, 0))], 2 * F * D * FF,
        scratch=[pltpu.VMEM((F, D), F32)], light=8)
    return out


def mlp_call(h2, w_up, bias_up, dg):
    F, FF = dg.shape
    N = 1024
    sds = jax.ShapeDtypeStruct
    col = lambda i: (0, i)
    return grid_call(
        functools.partial(mlp_kernel, min(256, F)), (FF // N,), (),
        [(h2, *whole(h2)), (w_up, (D, N), col), (bias_up, (1, N), col), (dg, (F, N), col)],
        [(sds((F, FF), BF), (F, N), col), (sds((F, FF), BF), (F, N), col), (sds((F, D), F32), (F, D), lambda i: (0, 0)),
         (sds((1, FF), F32), (1, N), col)], 4 * F * D * FF, vmem=28)


def wgrad_kernel(put, n, half_ref, *refs):
    put([dot_tn(refs[2 * i][...], refs[2 * i + 1][...]) for i in range(n)], refs[2 * n :])


def wgrad_rows(a, b, side, Y, B, add=None, splits=()):
    k, M = a.shape
    N = b.shape[1] // 2
    W, R = N // Y, M // B
    per = min(B, max(1, 1024 // R))
    idx = lambda i, h: (i, 0, 0, 0)
    ends = list(splits) + [R]

    def put(prods, refs):
        (o,) = prods
        for p in range(per):
            for q in range(Y):
                v = o[p * R : (p + 1) * R, q * W : (q + 1) * W]
                if add is not None:
                    v = v + refs[0][p, q].astype(F32)
                v = v.astype(BF)
                for ref, lo, hi in zip(refs[-len(ends) :], [0] + ends, ends):
                    ref[p, q] = v[lo:hi]

    ins = [(a, (k, per * R), lambda i, h: (0, i)), (b, (k, N), lambda i, h: (0, h[0]))]
    if add is not None:
        ins.append((add, (per, Y, R, W), idx))
    sizes = [hi - lo for lo, hi in zip([0] + ends, ends)]
    return grid_call(functools.partial(wgrad_kernel, put, 1), (B // per,), (side.reshape(1),), ins,
                     [(jax.ShapeDtypeStruct((B, Y, r, W), BF), (per, Y, r, W), idx) for r in sizes], 2 * k * M * N)


def wgrad_cols(a, b, side, Y, B, W, add=None, splits=(), lead=None):
    k, M = a.shape
    R, cut = M // B, b.shape[1] // (2 * Y * W)
    before = 0 if lead is None else lead.shape[2]
    rows = R * cut
    idx = lambda j, h: (0, j, 0, 0)
    ends = [before + e for e in splits] + [before + rows]

    def put(prods, refs):
        (o,) = prods
        if lead is not None:
            refs[-1][:, 0, :before] = refs[-2][:, 0]
        for p in range(cut):
            v = o[:, p * W : (p + 1) * W].reshape(B, R, W)
            if add is not None:
                v = v + refs[0][:, 0, p * R : (p + 1) * R].astype(F32)
            v = v.astype(BF)
            for ref, lo, hi in zip(refs[-len(ends) :], [0] + ends, ends):
                a0, a1 = max(lo, before + p * R), min(hi, before + (p + 1) * R)
                if a0 < a1:
                    ref[:, 0, a0 - lo : a1 - lo] = v[:, a0 - before - p * R : a1 - before - p * R]

    ins = [(a, *whole(a)), (b, (k, cut * W), lambda j, h: (0, h[0] * Y + j))]
    if add is not None:
        ins.append((add, (B, 1, rows, W), idx))
    if lead is not None:
        ins.append((lead, (B, 1, before, W), idx))
    sizes = [hi - lo for lo, hi in zip([0] + ends, ends)]
    return grid_call(functools.partial(wgrad_kernel, put, 1), (Y,), (side.reshape(1),), ins,
                     [(jax.ShapeDtypeStruct((B, Y, r, W), BF), (B, 1, r, W), idx) for r in sizes],
                     2 * k * M * b.shape[1] // 2)


def qgrad_kernel(a_ref, b_ref, o_ref):
    o_ref[...] = dot_tn(a_ref[...], b_ref[...]).reshape(o_ref.shape).astype(BF)


def qgrad(h_all, dqkv, B):
    S, n = dqkv.shape
    W = n // 3
    (out,) = grid_call(
        qgrad_kernel, (3,), (), [(h_all, *whole(h_all)), (dqkv, (S, W), lambda p: (0, p))],
        [(jax.ShapeDtypeStruct((B, 3 * D // B, W), BF), (B, D // B, W), lambda p: (0, p, 0))], 2 * S * D * n, light=8)
    return out


def dh_kernel(n_far, dq_ref, got_ref, w_ref, wm_ref, x_ref, far_ref, own_ref, sum_ref):
    i = pl.program_id(0)

    @pl.when(i == 0)
    def _():
        sum_ref[...] = jnp.zeros_like(sum_ref)

    part = dot_nt(dq_ref[...], w_ref[...]) + dot_nt(got_ref[...], wm_ref[...])
    low = part.astype(BF)

    @pl.when(i < n_far)
    def _():
        far_ref[...] = low

    @pl.when(i >= n_far)
    def _():
        own_ref[...] = low

    sum_ref[0:1, :] += jnp.sum(part * centred(x_ref[...]), axis=0, keepdims=True)
    sum_ref[1:2, :] += jnp.sum(part, axis=0, keepdims=True)


def dh_call(dqkv, got, w_g, w_m, x_all, Y):
    S, n = dqkv.shape
    F = S // (2 * Y)
    TR = min(256, F)
    per = F // TR
    n_far = (Y - 1) * per
    block = lambda i: (i // per + 1) % Y
    full = lambda i: (2 * block(i) * per + i % per, 0)
    sds = jax.ShapeDtypeStruct
    return grid_call(
        functools.partial(dh_kernel, n_far), (Y * per,), (),
        [(dqkv, (TR, n), full), (got, (TR, n), lambda i: (block(i) * per + i % per, 0)), (w_g, *whole(w_g)),
         (w_m, *whole(w_m)), (x_all, (TR, D), full)],
        [(sds(((Y - 1) * F, D), BF), (TR, D), lambda i: (jnp.minimum(i, n_far - 1), 0)),
         (sds((F, D), BF), (TR, D), lambda i: (jnp.maximum(i - n_far, 0), 0)),
         (sds((2, D), F32), (2, D), lambda i: (0, 0))],
        2 * S * D * n, light=8)


def tile_list(active):
    m = active.shape[1]
    hit = active.astype(jnp.int32)
    upto = jnp.tril(jnp.ones((m, m), jnp.int32))
    rank = jnp.sum(hit[:, None, :] * upto[None], axis=2) - 1
    ids = jnp.arange(m, dtype=jnp.int32)
    here = (rank[:, :, None] == ids[None, None, :]) & active[:, :, None]
    return jnp.sum(jnp.where(here, ids[None, :, None], 0), axis=1), jnp.sum(hit, axis=1)


def after(vals, deps):
    return lax.optimization_barrier((vals, deps))[0]


def shards(Z, X, Y, inputs, ln1_gain, ln1_bias, w_qkv, bias_q, bias_v, w_out, bias_out, ln2_gain, ln2_bias,
           w_up, bias_up, w_down, bias_down, lengths, cotangent):
    F = inputs.shape[1]
    K = 2 * Y
    S = F * K
    T = min(256, F)
    W = D // K
    HG = H // K
    B = Z * X
    zi, xi, y, c = (lax.axis_index(n) for n in ("z", "x", "y", "c"))
    group = y * 2 + c
    sds = jax.ShapeDtypeStruct

    def shift(v, axis, n, s):
        return lax.ppermute(v, axis, [(i, (i + s) % n) for i in range(n)])

    def mate(v):
        return lax.ppermute(v, "c", [(0, 1), (1, 0)])

    rel = [(s, d) for s in range(Y) for d in range(2)]

    def hop(v, s, d):
        pairs = [(yy * 2 + cc, ((yy + s) % Y) * 2 + (cc ^ d)) for yy in range(Y) for cc in range(2)]
        return lax.ppermute(v, ("y", "c"), pairs)

    def flip(d):
        return c if d == 0 else 1 - c

    blocks = jnp.stack([((y - s) % Y) * 2 + flip(d) for s, d in rel])
    ends = jnp.cumsum(lengths.reshape(-1))
    pos = (blocks[:, None] * F + jnp.arange(F, dtype=jnp.int32)[None]).reshape(1, S)
    piece = jnp.sum((pos >= ends[:, None]).astype(jnp.int32), axis=0, keepdims=True)
    pieces = ends.shape[0]
    starts = jnp.concatenate([jnp.zeros((1,), ends.dtype), ends[:-1]])

    def look(table, idx):
        return jnp.sum(jnp.where(idx == jnp.arange(pieces)[:, None], table[:, None], 0), axis=0, keepdims=True)

    pad = piece >= pieces
    lo = jnp.where(pad, pos, look(starts, (piece // 3) * 3)).astype(jnp.int32)
    hi = jnp.where(pad | (piece % 3 == 2), pos + 1, look(ends, piece)).astype(jnp.int32)
    base = pos[0, ::T].astype(jnp.int32)
    qlo = jnp.min(lo.reshape(S // T, T), axis=1)
    qhi = jnp.max(hi.reshape(S // T, T), axis=1)
    active = (base[None, :] < qhi[:, None]) & (base[None, :] + T > qlo[:, None])
    lst_q, cnt_q = tile_list(active)
    lst_k, cnt_k = tile_list(active.T)

    x_own = inputs.reshape(F, D)
    up = cotangent.reshape(F, D)
    flat_in = x_own.astype(F32)

    def cols_of(w, g):
        return [lax.dynamic_slice_in_dim(w, part * D + g * W, W, w.ndim - 1) for part in range(3)]

    far = [shift(x_own, "y", Y, s) for s in range(1, Y)]
    near = mate(x_own)
    w_g = jnp.concatenate(cols_of(w_qkv, group), axis=1)
    w_m = jnp.concatenate(cols_of(w_qkv, y * 2 + 1 - c), axis=1)
    b_g = jnp.concatenate([lax.dynamic_slice_in_dim(bias_q, group * W, W, 0), jnp.zeros((W,), F32),
                           lax.dynamic_slice_in_dim(bias_v, group * W, W, 0)])[None]
    sc_g = jnp.where(jnp.arange(3 * W) < W, HD**-0.5, 1.0).astype(F32)[None]
    ln1 = (ln1_gain[None], ln1_bias[None])
    held = qkv_call(x_own, *ln1, w_g, b_g, sc_g, 0, K, None)
    held = qkv_call(near, *ln1, w_g, b_g, sc_g, 1, K, held)
    dg = dg_call(after(up, (held[1], w_m)), w_down)
    xs = [x_own, near]
    for i, r in enumerate(far):
        r = after(r, dg) if i == 0 else r
        xs += [r, mate(r)]
        held = qkv_call(xs[-2], *ln1, w_g, b_g, sc_g, 2 * i + 2, K, held)
        held = qkv_call(xs[-1], *ln1, w_g, b_g, sc_g, 2 * i + 3, K, held)
    h_all, qkv = held
    lse_shape = sds((HG, S), F32)
    ctx_g, lse = attend(
        functools.partial(fwd_kernel, T, HG), (lst_q, cnt_q, base),
        [(qkv, (W, 0)), (qkv, (W, 1)), (qkv, (W, 2)), (lo, None), (hi, None)],
        [sds((S, W), BF), lse_shape], [], 12 * 10**9)

    mine = [ctx_g[:F]] + [hop(ctx_g[(2 * s + d) * F : (2 * s + d + 1) * F], -s, d) for s, d in rel[1:]]
    x_all = jnp.concatenate(after(xs, ctx_g), axis=0)
    mine[1:] = after(mine[1:], x_all)
    groups = jnp.stack([((y + s) % Y) * 2 + flip(d) for s, d in rel]).astype(jnp.int32)
    middle, h2 = out_call([ctx_g] + mine[1:], groups, w_out, x_own, bias_out[None], ln2_gain[None], ln2_bias[None])
    act, du, dh2, g_bu = mlp_call(h2, w_up, bias_up[None], dg)
    mine = jnp.stack(after(mine, dh2))
    ctx = jnp.concatenate(
        [lax.dynamic_index_in_dim(mine, ((yy - y) % Y) * 2 + (cc ^ c), 0, keepdims=False)
         for yy in range(Y) for cc in range(2)], axis=1)

    def shaped(g):
        return g.reshape(Z, X, Y, g.shape[2], W)

    def begin(items, n, me, send, dep=None):
        def cut(g, axis, i):
            return lax.dynamic_index_in_dim(g, i, axis, keepdims=False)

        def piece(terms, axis, i):
            return settle([cut(g, axis, i) for g in terms]).reshape(-1, W)

        bufs = [jnp.concatenate([piece(g, ax, (me + s) % n) for g, ax in items]) for s in range(1, n)]
        if dep is not None:
            bufs = after(bufs, dep)
        return [[cut(g, ax, me) for g in terms] for terms, ax in items], [send(b, s + 1) for s, b in enumerate(bufs)], bufs

    def settle(terms):
        return sum((g.astype(F32) for g in terms[1:]), terms[0].astype(F32)).astype(BF)

    def finish(state):
        own, sent, _ = state
        out, at = [], 0
        for terms in own:
            rows = terms[0].size // W
            out.append(terms + [r[at : at + rows].reshape(terms[0].shape) for r in sent])
            at += rows
        return out

    def hold(states, others):
        sent, others = lax.optimization_barrier(([st[1] for st in states], others))
        return [(st[0], r, st[2]) for st, r in zip(states, sent)], others

    def head(terms):
        return [g[0] for g in terms]

    def over_y(items):
        return begin(items, Y, y, lambda v, s: shift(v, "y", Y, s))

    def over_x(items):
        return begin(items, X, xi, lambda v, s: shift(v, "x", X, s))

    def over_z(items, bit, dep=None):
        bits = [([g.reshape((g.shape[0] // 2, 2) + g.shape[1:]) for g in terms], 1) for terms in items]
        return begin(bits, 2, (zi // bit) % 2, lambda v, s: lax.ppermute(v, "z", [(i, i ^ bit) for i in range(Z)]), dep)

    assert Z & (Z - 1) == 0
    zbits = [1 << i for i in range(Z.bit_length() - 1)]

    def total(v):
        return jnp.sum(v.astype(F32), axis=0)

    def rows_of(vecs):
        return jnp.concatenate([v.reshape(B, -1) for v in vecs], axis=1).astype(BF).reshape(B, -1, W)

    hr = w_down.shape[0] // B // 2
    pr = qr = 3 * hr // 4
    n_ot = D // B
    ur = hr + n_ot // 2

    (dn_give,) = wgrad_rows(act, up, 1 - c, Y, B)
    dn_got = mate(dn_give)
    (up_give,) = wgrad_cols(h2, after(du, dn_give), 1 - c, Y, B, W)
    up_got = mate(up_give)
    dy1, da, dctx, sums = ln2_call(after(dh2, up_give), middle, up, ln2_gain[None], w_out)

    def heads_of(s, d):
        return lax.dynamic_slice_in_dim(dctx, (((y + s) % Y) * 2 + flip(d)) * W, W, 1)

    def both(s):
        return jnp.concatenate([heads_of(s, 0), heads_of(s, 1)])

    do_y = [both(0)] + [shift(both(s), "y", Y, s) for s in range(1, Y)]

    (ot_give,) = wgrad_cols(ctx, after(da, do_y[0]), 1 - c, Y, B, W)
    ot_got = mate(ot_give)
    dnP, dnQ, dnR = wgrad_rows(act, after(up, ot_give), c, Y, B, dn_got, (pr, pr + qr))
    (dnP, dnQ, dnR), ot_got = lax.optimization_barrier(((dnP, dnQ, dnR), ot_got))
    t_y, t_x, t_r = over_y([([shaped(dnP)], 2)]), over_x([([shaped(dnQ)], 1)]), over_z([[shaped(dnR)]], 1)
    h2_, ctx_, da_ = after((h2, ctx, da), (t_y[2], t_x[2], t_r[2]))
    upQ, upP = wgrad_cols(h2_, du, c, Y, B, W, up_got, (ur,))
    do_y = after(do_y, (t_y[2], t_x[2], t_r[2]))
    do_c = mate(jnp.concatenate([v[F:] for v in do_y]))
    do_g = jnp.concatenate([b for s in range(Y) for b in (do_y[s][:F], do_c[s * F : (s + 1) * F])])
    (upP,) = wgrad_cols(ctx_, da_, c, Y, B, W, ot_got, (), upP)
    n_y, n_x = over_y([([shaped(upP)], 2)]), over_x([([shaped(upQ)], 1)])
    (t_y, t_x, t_r), (n_bufs, do_g) = hold([t_y, t_x, t_r], ((n_y[2], n_x[2]), do_g))
    (dnP,), (dnQ,), (dnR,) = finish(t_y), finish(t_x), finish(t_r)

    t_y, t_x, t_z, t_r = n_y, n_x, over_z([dnQ], 1), over_z([dnR], zbits[1])
    dnP = settle(dnP)
    early = rows_of([sums[2], sums[0], sums[1], sums[3], g_bu[0]])
    do_g = after(do_g, (n_bufs, t_z[2], t_r[2], early, dnP))
    (dqkv,) = attend(
        functools.partial(bwd_kernel, T, HG), (lst_k, cnt_k, base),
        [(qkv, (W, 0)), (qkv, (W, 1)), (qkv, (W, 2)), (ctx_g, None), (do_g, None), (lse, None), (lo, None), (hi, None)],
        [sds((S, 3 * W), BF)], [pltpu.VMEM((W, S), F32), pltpu.VMEM((HG, S), F32)], 20 * 10**9)
    (t_y, t_x, t_z, t_r), (dqkv, dnP) = hold([t_y, t_x, t_z, t_r], (dqkv, dnP))
    def rest(items, k):
        for bit in zbits[k:]:
            items = finish(over_z(items, bit))
        return items

    (upP,), (upQ,), (dnQ,), (dnR,) = finish(t_y), finish(t_x), finish(t_z), rest(finish(t_r), 2)

    def of_x(i):
        return jnp.concatenate([settle([lax.dynamic_index_in_dim(g, i, 1, keepdims=False) for g in terms])
                                for terms in ([dnP], upP)], axis=1)

    p_bufs, p_own = [of_x((xi + s) % X) for s in range(1, X)], of_x(xi)
    t_x = ([[p_own]], [shift(b, "x", X, s + 1) for s, b in enumerate(p_bufs)], p_bufs)
    t_a, t_b = over_z([upQ], 1), over_z([dnQ], zbits[1])
    dq_got = mate(dqkv.reshape(Y, 2, F, 3 * W)[:, 1].reshape(Y * F, 3 * W))
    qv = qgrad(h_all, after(dqkv, (p_bufs, t_a[2])), B)
    dh_far, dh_own, g_ln1 = dh_call(dqkv, after(dq_got, qv), w_g, w_m, x_all, Y)
    far = [shift(dh_far[s * F : (s + 1) * F], "y", Y, -s - 1) for s in range(Y - 1)]
    cols = total(dqkv)
    mine_only = jnp.arange(D) // W == group
    late = rows_of([g_ln1[0], g_ln1[1]] + [jnp.where(mine_only, jnp.tile(v, K), 0.0) for v in (cols[:W], cols[2 * W :])])
    vec = jnp.concatenate([late, early], axis=1)
    vec = jnp.pad(vec, ((0, 0), (0, -vec.shape[1] % 16), (0, 0)))
    qv = jnp.concatenate([qv, vec], axis=1).reshape(Z, X, -1, W)
    n_x = over_x([([qv], 1), (dnR, 1)])
    (t_x, t_a, t_b), n_bufs = hold([t_x, t_a, t_b], n_x[2])
    parts, upQ, dnQ = [p_own] + t_x[1], finish(t_a)[0], finish(t_b)[0]

    t_x = n_x
    t_a, t_b = over_z([parts], 1), over_z([upQ], zbits[1])
    result = down_call(after(act, (n_bufs, t_a[2], t_b[2])), w_down, middle, bias_down[None])
    (t_x, t_a, t_b), (far, result) = hold([t_x, t_a, t_b], (far, result))

    (qv, dnR), (parts,), (upQ,), (dnQ,) = finish(t_x), finish(t_a), rest(finish(t_b), 2), rest([dnQ], 2)

    t_a, t_b = over_z([qv], 1), over_z([parts], zbits[1])
    t_y = over_y([(head(dnQ), 0), (head(upQ), 0), (head(dnR), 0)])
    far, dh_own = after((far, dh_own), (t_a[2], t_b[2], t_y[2]))
    dh1 = sum((r.astype(F32) for r in far), dh_own.astype(F32))
    _, norm_back_one = jax.vjp(lambda v: layer_norm(v, ln1_gain, ln1_bias), flat_in)
    (dx,) = norm_back_one(dh1)
    grad_inputs = (dy1 + dx).reshape(1, F, D)
    (t_a, t_b, t_y), grad_inputs = hold([t_a, t_b, t_y], grad_inputs)
    (qv,), (parts,), (dnQ, upQ, dnR) = finish(t_a), rest(finish(t_b), 2), finish(t_y)

    t_b = over_z([qv], zbits[1])
    parts, dnQ, upQ, dnR = after((head(parts), dnQ, upQ, dnR), t_b[2])
    parts = settle(parts)
    first = jnp.concatenate([parts[:pr], settle(dnQ), settle(dnR), settle(upQ), parts[pr:]])

    def share_y(g):
        return [g] + [shift(g, "y", Y, s) for s in range(1, Y)]

    first_y = share_y(first)
    (t_b,), first_y = hold([t_b], first_y)
    (qv,) = rest(finish(t_b), 2)
    tail_y = share_y(settle(head(qv)))

    def share_c(got):
        got = jnp.stack(got)
        other = mate(got)

        def piece(yy, cc):
            i = (y - yy) % Y
            return jnp.where(cc == c, lax.dynamic_index_in_dim(got, i, 0, keepdims=False),
                             lax.dynamic_index_in_dim(other, i, 0, keepdims=False))

        return [[piece(yy, cc) for cc in range(2)] for yy in range(Y)]

    def by_columns(e, at, rows, chunks):
        return jnp.concatenate([e[yy][cc][at + k * rows : at + (k + 1) * rows] for cc in range(2) for yy in range(Y)
                                for k in range(chunks)], axis=1).astype(F32)

    first_e = share_c(first_y)
    n_dn = 2 * hr
    g_w_down = by_columns(first_e, 0, n_dn, 1)
    g_w_up = by_columns(first_e, n_dn, n_ot, 2 * ur // n_ot - 1)
    g_w_out = by_columns(first_e, n_dn + 2 * ur - n_ot, n_ot, 1)
    tail_y, g_w_down, g_w_up, g_w_out = lax.optimization_barrier((tail_y, g_w_down, g_w_up, g_w_out))
    tail_e = share_c(tail_y)
    g_w_qkv = jnp.concatenate([tail_e[yy][cc][p * n_ot : (p + 1) * n_ot] for p in range(3) for yy in range(Y)
                               for cc in range(2)], axis=1).astype(F32)
    at = 3 * n_ot
    flat = sum(tail_e[yy][cc][at:].astype(F32) for yy in range(Y) for cc in range(2)).reshape(-1)
    out, at = [], 0
    for n in (D, D, D, D, D, D, D, D, w_up.shape[1]):
        out.append(flat[at : at + n // B])
        at += n // B
    g_ln1g, g_ln1b, g_bq, g_bv, g_bo, g_ln2g, g_ln2b, g_bd, g_bu = out
    return (result.reshape(1, F, D), grad_inputs, g_ln1g, g_ln1b, g_w_qkv, g_bq, g_bv, g_w_out, g_bo, g_ln2g, g_ln2b,
            g_w_up, g_bu, g_w_down, g_bd)


def solution(mesh):
    batch, blk = mesh.shape["batch"], mesh.shape["blk"]
    Y = blk // 2
    X = Y if batch % Y == 0 else 1
    Z = batch // X
    fine = Mesh(mesh.devices.reshape(Z, X, Y, 2), ("z", "x", "y", "c"))
    rows, slots = ("z", "x"), ("y", "c")
    act = P(rows, slots, None)
    flat, mat = P(rows), P(rows, None)
    return jax.shard_map(
        functools.partial(shards, Z, X, Y),
        mesh=fine,
        in_specs=(act,) + (P(),) * 13 + (P(rows, None, None), act),
        out_specs=(act, act, flat, flat, mat, flat, flat, mat, flat, flat, flat, mat, flat, mat, flat),
        check_vma=False,
    )
```

```python
import functools

import jax
import jax.numpy as jnp
from jax import lax
from jax.experimental import pallas as pl
from jax.experimental.pallas import tpu as pltpu
from jax.sharding import Mesh
from jax.sharding import PartitionSpec as P

D = 1024
H = 16
HD = 64
EPS = 1e-05
NEG = -1e30
VM = 20
AV = 28
BF = jnp.bfloat16
F32 = jnp.float32


def layer_norm(values, gain_vec, shift_vec):
    center = values - jnp.mean(values, axis=-1, keepdims=True)
    spread = jnp.mean(center * center, axis=-1, keepdims=True)
    return center * lax.rsqrt(spread + EPS) * gain_vec + shift_vec


def dot(a, b):
    return jnp.dot(a, b, preferred_element_type=F32)


def dot_tn(a, b):
    return lax.dot_general(a, b, (((0,), (0,)), ((), ())), preferred_element_type=F32)


def dot_nt(a, b):
    return lax.dot_general(a, b, (((1,), (1,)), ((), ())), preferred_element_type=F32)


def half(a, h):
    a = a[:, (h // 2) * 2 * HD : (h // 2 + 1) * 2 * HD]
    lane = lax.broadcasted_iota(jnp.int32, a.shape, 1)
    zero = jnp.zeros_like(a)
    return jnp.where(lane < HD, a, zero) if h % 2 == 0 else jnp.where(lane < HD, zero, a)


def pair(a, h):
    return a[:, (h // 2) * 2 * HD : (h // 2 + 1) * 2 * HD]


def fwd_kernel(T, HG, lst, cnt, base, q_ref, k_ref, v_ref, lo_ref, hi_ref, ctx_ref, lse_ref):
    nq = q_ref.shape[0] // T
    row = lax.broadcasted_iota(jnp.int32, (T, T), 0)

    @pl.loop(0, nq)
    def _(qt):
        at = pl.ds(pl.multiple_of(qt * T, T), T)
        q = q_ref[at, :]
        qh = [half(q, h) for h in range(HG)]
        lo, hi = lo_ref[:, at], hi_ref[:, at]

        def body(n, carry):
            t = lst[qt, n]
            ks = pl.ds(pl.multiple_of(t * T, T), T)
            k, v = k_ref[ks, :], v_ref[ks, :].T
            vis = (row >= lo - base[t]) & (row < hi - base[t])
            raw = [dot_nt(pair(k, h), qh[h]) for h in range(HG)]
            out = []
            for h in range(HG):
                m, l, acc = carry[h]
                s = jnp.where(vis, raw[h], NEG)
                mn = jnp.maximum(m, jnp.max(s, axis=0, keepdims=True))
                a = jnp.exp(m - mn)
                p = jnp.exp(s - mn)
                l = a * l + jnp.sum(p, axis=0, keepdims=True)
                acc = acc * a + dot(v[h * HD : (h + 1) * HD, :], p.astype(BF))
                out.append((mn, l, acc))
            return tuple(out)

        one = (jnp.full((1, T), NEG, F32), jnp.zeros((1, T), F32), jnp.zeros((HD, T), F32))
        res = lax.fori_loop(0, cnt[qt], body, (one,) * HG)
        ctx_ref[at, :] = jnp.concatenate([r[2] / r[1] for r in res], axis=0).T.astype(BF)
        lse_ref[:, at] = jnp.concatenate([r[0] + jnp.log(r[1]) for r in res], axis=0)


def bwd_kernel(T, HG, lst, cnt, base, q_ref, k_ref, v_ref, ctx_ref, do_ref, lse_ref, lo_ref, hi_ref, out_ref, dqt, dl):
    n_tiles = q_ref.shape[0] // T
    W = HG * HD
    row = lax.broadcasted_iota(jnp.int32, (T, T), 0)
    lane = lax.broadcasted_iota(jnp.int32, (T, 2 * HD), 1)
    dqt[...] = jnp.zeros_like(dqt)

    @pl.loop(0, n_tiles)
    def _(t):
        at = pl.ds(pl.multiple_of(t * T, T), T)
        prod = (do_ref[at, :].astype(F32) * ctx_ref[at, :].astype(F32)).T
        dl[:, at] = jnp.concatenate([jnp.sum(prod[h * HD : (h + 1) * HD], axis=0, keepdims=True) for h in range(HG)], axis=0)

    @pl.loop(0, n_tiles)
    def _(kt):
        ks = pl.ds(pl.multiple_of(kt * T, T), T)
        k, v = k_ref[ks, :], v_ref[ks, :]
        kT = k.T
        kh, vh = [half(k, h) for h in range(HG)], [half(v, h) for h in range(HG)]

        def body(n, carry):
            at = pl.ds(pl.multiple_of(lst[kt, n] * T, T), T)
            q, do = q_ref[at, :], do_ref[at, :]
            vis = (row >= lo_ref[:, at] - base[kt]) & (row < hi_ref[:, at] - base[kt])
            raw = [dot_nt(kh[h], pair(q, h)) for h in range(HG)]
            dps = [dot_nt(vh[h], pair(do, h)) for h in range(HG)]
            out = []
            for h in range(HG):
                p = jnp.exp(jnp.where(vis, raw[h], NEG) - lse_ref[h : h + 1, at])
                ds = (p * (dps[h] - dl[h : h + 1, at])).astype(BF)
                out.append((carry[h][0] + dot(ds, pair(q, h)), carry[h][1] + dot(p.astype(BF), pair(do, h))))
                dqt[h * HD : (h + 1) * HD, at] += dot(kT[h * HD : (h + 1) * HD, :], ds)
            return tuple(out)

        one = (jnp.zeros((T, 2 * HD), F32), jnp.zeros((T, 2 * HD), F32))
        res = lax.fori_loop(0, cnt[kt], body, (one,) * HG)
        for p in range(HG // 2):
            cols = slice(p * 2 * HD, (p + 1) * 2 * HD)
            a, b = res[2 * p], res[2 * p + 1]
            out_ref[ks, W + cols.start : W + cols.stop] = jnp.where(lane < HD, a[0], b[0]).astype(BF)
            out_ref[ks, 2 * W + cols.start : 2 * W + cols.stop] = jnp.where(lane < HD, a[1], b[1]).astype(BF)

    @pl.loop(0, n_tiles)
    def _(t):
        at = pl.ds(pl.multiple_of(t * T, T), T)
        out_ref[at, :W] = (dqt[:, at].T * HD**-0.5).astype(BF)


def attend(kernel, scalars, ins, outs, scratch, flops):
    def spec(shape, cols):
        if cols is None:
            return pl.BlockSpec(shape, lambda i, *_: (0,) * len(shape))
        return pl.BlockSpec((shape[0], cols[0]), lambda i, *_: (0, cols[1]))

    size = sum(a.size * a.dtype.itemsize for a, _ in ins) + sum(o.size * o.dtype.itemsize for o in outs)
    return pl.pallas_call(
        kernel,
        out_shape=outs,
        grid_spec=pltpu.PrefetchScalarGridSpec(
            num_scalar_prefetch=len(scalars),
            grid=(1,),
            in_specs=[spec(a.shape, cols) for a, cols in ins],
            out_specs=[spec(o.shape, None) for o in outs],
            scratch_shapes=scratch,
        ),
        compiler_params=pltpu.CompilerParams(vmem_limit_bytes=AV << 20),
        cost_estimate=pl.CostEstimate(flops=flops, bytes_accessed=size, transcendentals=0),
    )(*scalars, *[a for a, _ in ins])


def grid_call(kernel, grid, scalars, ins, outs, flops, scratch=(), aliases=None, vmem=VM, light=1):
    def spec(block, index):
        return pl.BlockSpec(memory_space=pl.ANY) if block is None else pl.BlockSpec(block, index)

    size = sum(a.size * a.dtype.itemsize for a, b, _ in ins if b is not None)
    size += sum(o.size * o.dtype.itemsize for o, _, _ in outs)
    return pl.pallas_call(
        kernel,
        out_shape=[o for o, _, _ in outs],
        grid_spec=pltpu.PrefetchScalarGridSpec(
            num_scalar_prefetch=len(scalars),
            grid=grid,
            in_specs=[spec(b, m) for _, b, m in ins],
            out_specs=[spec(b, m) for _, b, m in outs],
            scratch_shapes=list(scratch),
        ),
        input_output_aliases=aliases or {},
        compiler_params=pltpu.CompilerParams(vmem_limit_bytes=vmem << 20),
        cost_estimate=pl.CostEstimate(flops=flops // light, bytes_accessed=size // light, transcendentals=0),
    )(*scalars, *[a for a, _, _ in ins])


def whole(a):
    return a.shape, lambda *_: (0,) * len(a.shape)


def centred(x):
    x = x.astype(F32)
    center = x - jnp.mean(x, axis=-1, keepdims=True)
    spread = jnp.mean(center * center, axis=-1, keepdims=True)
    return center * lax.rsqrt(spread + EPS)


def qkv_kernel(x_ref, g_ref, b_ref, w_ref, bias_ref, sc_ref, *refs):
    h_ref, o_ref = refs[-2:]
    h = (centred(x_ref[...]) * g_ref[...] + b_ref[...]).astype(BF)
    h_ref[...] = h
    o = (dot(h, w_ref[...]) + bias_ref[...]).astype(BF)
    o_ref[...] = (o.astype(F32) * sc_ref[...]).astype(BF)


def qkv_call(x, g, b, w, bias, sc, r, blocks, held):
    F, n = x.shape[0], w.shape[1]
    TR = min(128, F)
    per = F // TR
    row = lambda i: (i, 0)
    to = lambda i: (r * per + i, 0)
    ins = [(x, (TR, D), row)] + [(v, *whole(v)) for v in (g, b, w, bias, sc)]
    shapes = [jax.ShapeDtypeStruct((blocks * F, D), BF), jax.ShapeDtypeStruct((blocks * F, n), BF)]
    aliases = {}
    if held is not None:
        ins += [(held[0], None, None), (held[1], None, None)]
        aliases = {6: 0, 7: 1}
    return grid_call(qkv_kernel, (per,), (), ins, [(shapes[0], (TR, D), to), (shapes[1], (TR, n), to)],
                     2 * F * D * n, aliases=aliases)


def out_kernel(n, group_ref, *refs):
    x_ref, bias_ref, g_ref, b_ref, mid_ref, h_ref = refs[2 * n :]
    mid = sum(dot(refs[i][...], refs[n + i][...]) for i in range(n)) + bias_ref[...]
    mid = x_ref[...].astype(F32) + mid
    mid_ref[...] = mid
    h_ref[...] = (centred(mid) * g_ref[...] + b_ref[...]).astype(BF)


def out_call(mine, groups, w_out, x, bias, g, b):
    F, n = x.shape[0], len(mine)
    W = mine[0].shape[1]
    TR = min(256, F)
    row = lambda i, gr: (i, 0)
    ins = [(m, (TR, W), row) for m in mine]
    ins += [(w_out, (W, D), lambda i, gr, r=r: (gr[r], 0)) for r in range(n)]
    ins += [(x, (TR, D), row)] + [(v, *whole(v)) for v in (bias, g, b)]
    return grid_call(functools.partial(out_kernel, n), (F // TR,), (groups,), ins,
                     [(jax.ShapeDtypeStruct((F, D), F32), (TR, D), row), (jax.ShapeDtypeStruct((F, D), BF), (TR, D), row)],
                     2 * F * D * D)


def ln2_kernel(dh_ref, mid_ref, up_ref, g_ref, w_ref, dy_ref, da_ref, dctx_ref, sum_ref):
    @pl.when(pl.program_id(0) == 0)
    def _():
        sum_ref[...] = jnp.zeros_like(sum_ref)

    mid, dh, up = mid_ref[...], dh_ref[...], up_ref[...].astype(F32)
    center = mid - jnp.mean(mid, axis=-1, keepdims=True)
    rstd = lax.rsqrt(jnp.mean(center * center, axis=-1, keepdims=True) + EPS)
    xh = center * rstd
    t = dh * g_ref[...]
    d = rstd * (t - jnp.mean(t, axis=-1, keepdims=True) - xh * jnp.mean(t * xh, axis=-1, keepdims=True))
    dy = up + d
    dy_ref[...] = dy
    da = dy.astype(BF)
    da_ref[...] = da
    dctx_ref[...] = dot_nt(da, w_ref[...]).astype(BF)
    for k, v in enumerate((dh * xh, dh, da.astype(F32), up)):
        sum_ref[k : k + 1, :] += jnp.sum(v, axis=0, keepdims=True)


def ln2_call(dh2, middle, up, g, w_out):
    F = up.shape[0]
    TR = min(256, F)
    row = lambda i: (i, 0)
    sds = jax.ShapeDtypeStruct
    return grid_call(
        ln2_kernel, (F // TR,), (),
        [(dh2, (TR, D), row), (middle, (TR, D), row), (up, (TR, D), row), (g, *whole(g)), (w_out, *whole(w_out))],
        [(sds((F, D), F32), (TR, D), row), (sds((F, D), BF), (TR, D), row), (sds((F, D), BF), (TR, D), row),
         (sds((4, D), F32), (4, D), lambda i: (0, 0))], 2 * F * D * D)


def mlp_kernel(sub, h_ref, w_ref, b_ref, dg_ref, act_ref, du_ref, dh_ref, bu_ref):
    rows = h_ref.shape[0]

    @pl.when(pl.program_id(0) == 0)
    def _():
        dh_ref[...] = jnp.zeros_like(dh_ref)

    bu = jnp.zeros(bu_ref.shape, F32)
    for r in range(0, rows, sub):
        at = slice(r, r + sub)
        u = dot(h_ref[at, :], w_ref[...]) + b_ref[...]
        cdf = 0.5 + 0.5 * lax.erf(u * 0.7071067811865476)
        pdf = jnp.exp(-0.5 * u * u) * 0.3989422804014327
        act_ref[at, :] = (u * cdf).astype(BF)
        du = (dg_ref[at, :].astype(F32) * (cdf + u * pdf)).astype(BF)
        du_ref[at, :] = du
        bu = bu + jnp.sum(du.astype(F32), axis=0, keepdims=True)
        dh_ref[at, :] += dot_nt(du, w_ref[...])
    bu_ref[...] = bu


def dg_kernel(c_ref, w_ref, o_ref):
    o_ref[...] = dot_nt(c_ref[...], w_ref[...]).astype(BF)


def dg_call(c, w_down):
    F, FF = c.shape[0], w_down.shape[0]
    N = 512
    (out,) = grid_call(dg_kernel, (FF // N,), (), [(c, *whole(c)), (w_down, (N, D), lambda i: (i, 0))],
                       [(jax.ShapeDtypeStruct((F, FF), BF), (F, N), lambda i: (0, i))], 2 * F * D * FF)
    return out


def down_kernel(a_ref, w_ref, mid_ref, bias_ref, o_ref, acc):
    k = pl.program_id(0)

    @pl.when(k == 0)
    def _():
        acc[...] = mid_ref[...] + bias_ref[...]

    acc[...] += dot(a_ref[...], w_ref[...])

    @pl.when(k == pl.num_programs(0) - 1)
    def _():
        o_ref[...] = acc[...].astype(BF)


def down_call(act, w_down, middle, bias):
    F, FF = act.shape
    N = 1024
    (out,) = grid_call(
        down_kernel, (FF // N,), (),
        [(act, (F, N), lambda k: (0, k)), (w_down, (N, D), lambda k: (k, 0)), (middle, *whole(middle)), (bias, *whole(bias))],
        [(jax.ShapeDtypeStruct((F, D), BF), (F, D), lambda k: (0, 0))], 2 * F * D * FF,
        scratch=[pltpu.VMEM((F, D), F32)], light=8)
    return out


def mlp_call(h2, w_up, bias_up, dg):
    F, FF = dg.shape
    N = 1024
    sds = jax.ShapeDtypeStruct
    col = lambda i: (0, i)
    return grid_call(
        functools.partial(mlp_kernel, min(256, F)), (FF // N,), (),
        [(h2, *whole(h2)), (w_up, (D, N), col), (bias_up, (1, N), col), (dg, (F, N), col)],
        [(sds((F, FF), BF), (F, N), col), (sds((F, FF), BF), (F, N), col), (sds((F, D), F32), (F, D), lambda i: (0, 0)),
         (sds((1, FF), F32), (1, N), col)], 4 * F * D * FF, vmem=28)


def wgrad_kernel(put, n, half_ref, *refs):
    put([dot_tn(refs[2 * i][...], refs[2 * i + 1][...]) for i in range(n)], refs[2 * n :])


def wgrad_rows(a, b, side, Y, B, add=None, splits=()):
    k, M = a.shape
    N = b.shape[1] // 2
    W, R = N // Y, M // B
    per = min(B, max(1, 1024 // R))
    idx = lambda i, h: (i, 0, 0, 0)
    ends = list(splits) + [R]

    def put(prods, refs):
        (o,) = prods
        for p in range(per):
            for q in range(Y):
                v = o[p * R : (p + 1) * R, q * W : (q + 1) * W]
                if add is not None:
                    v = v + refs[0][p, q].astype(F32)
                v = v.astype(BF)
                for ref, lo, hi in zip(refs[-len(ends) :], [0] + ends, ends):
                    ref[p, q] = v[lo:hi]

    ins = [(a, (k, per * R), lambda i, h: (0, i)), (b, (k, N), lambda i, h: (0, h[0]))]
    if add is not None:
        ins.append((add, (per, Y, R, W), idx))
    sizes = [hi - lo for lo, hi in zip([0] + ends, ends)]
    return grid_call(functools.partial(wgrad_kernel, put, 1), (B // per,), (side.reshape(1),), ins,
                     [(jax.ShapeDtypeStruct((B, Y, r, W), BF), (per, Y, r, W), idx) for r in sizes], 2 * k * M * N)


def wgrad_cols(a, b, side, Y, B, W, add=None, splits=(), lead=None):
    k, M = a.shape
    R, cut = M // B, b.shape[1] // (2 * Y * W)
    before = 0 if lead is None else lead.shape[2]
    rows = R * cut
    idx = lambda j, h: (0, j, 0, 0)
    ends = [before + e for e in splits] + [before + rows]

    def put(prods, refs):
        (o,) = prods
        if lead is not None:
            refs[-1][:, 0, :before] = refs[-2][:, 0]
        for p in range(cut):
            v = o[:, p * W : (p + 1) * W].reshape(B, R, W)
            if add is not None:
                v = v + refs[0][:, 0, p * R : (p + 1) * R].astype(F32)
            v = v.astype(BF)
            for ref, lo, hi in zip(refs[-len(ends) :], [0] + ends, ends):
                a0, a1 = max(lo, before + p * R), min(hi, before + (p + 1) * R)
                if a0 < a1:
                    ref[:, 0, a0 - lo : a1 - lo] = v[:, a0 - before - p * R : a1 - before - p * R]

    ins = [(a, *whole(a)), (b, (k, cut * W), lambda j, h: (0, h[0] * Y + j))]
    if add is not None:
        ins.append((add, (B, 1, rows, W), idx))
    if lead is not None:
        ins.append((lead, (B, 1, before, W), idx))
    sizes = [hi - lo for lo, hi in zip([0] + ends, ends)]
    return grid_call(functools.partial(wgrad_kernel, put, 1), (Y,), (side.reshape(1),), ins,
                     [(jax.ShapeDtypeStruct((B, Y, r, W), BF), (B, 1, r, W), idx) for r in sizes],
                     2 * k * M * b.shape[1] // 2)


def qgrad_kernel(a_ref, b_ref, o_ref):
    o_ref[...] = dot_tn(a_ref[...], b_ref[...]).reshape(o_ref.shape).astype(BF)


def qgrad(h_all, dqkv, B):
    S, n = dqkv.shape
    W = n // 3
    (out,) = grid_call(
        qgrad_kernel, (3,), (), [(h_all, *whole(h_all)), (dqkv, (S, W), lambda p: (0, p))],
        [(jax.ShapeDtypeStruct((B, 3 * D // B, W), BF), (B, D // B, W), lambda p: (0, p, 0))], 2 * S * D * n, light=8)
    return out


def dh_kernel(n_far, dq_ref, got_ref, w_ref, wm_ref, x_ref, far_ref, own_ref, sum_ref):
    i = pl.program_id(0)

    @pl.when(i == 0)
    def _():
        sum_ref[...] = jnp.zeros_like(sum_ref)

    part = dot_nt(dq_ref[...], w_ref[...]) + dot_nt(got_ref[...], wm_ref[...])
    low = part.astype(BF)

    @pl.when(i < n_far)
    def _():
        far_ref[...] = low

    @pl.when(i >= n_far)
    def _():
        own_ref[...] = low

    sum_ref[0:1, :] += jnp.sum(part * centred(x_ref[...]), axis=0, keepdims=True)
    sum_ref[1:2, :] += jnp.sum(part, axis=0, keepdims=True)


def dh_call(dqkv, got, w_g, w_m, x_all, Y):
    S, n = dqkv.shape
    F = S // (2 * Y)
    TR = min(256, F)
    per = F // TR
    n_far = (Y - 1) * per
    block = lambda i: (i // per + 1) % Y
    full = lambda i: (2 * block(i) * per + i % per, 0)
    sds = jax.ShapeDtypeStruct
    return grid_call(
        functools.partial(dh_kernel, n_far), (Y * per,), (),
        [(dqkv, (TR, n), full), (got, (TR, n), lambda i: (block(i) * per + i % per, 0)), (w_g, *whole(w_g)),
         (w_m, *whole(w_m)), (x_all, (TR, D), full)],
        [(sds(((Y - 1) * F, D), BF), (TR, D), lambda i: (jnp.minimum(i, n_far - 1), 0)),
         (sds((F, D), BF), (TR, D), lambda i: (jnp.maximum(i - n_far, 0), 0)),
         (sds((2, D), F32), (2, D), lambda i: (0, 0))],
        2 * S * D * n, light=8)


def tile_list(active):
    m = active.shape[1]
    hit = active.astype(jnp.int32)
    upto = jnp.tril(jnp.ones((m, m), jnp.int32))
    rank = jnp.sum(hit[:, None, :] * upto[None], axis=2) - 1
    ids = jnp.arange(m, dtype=jnp.int32)
    here = (rank[:, :, None] == ids[None, None, :]) & active[:, :, None]
    return jnp.sum(jnp.where(here, ids[None, :, None], 0), axis=1), jnp.sum(hit, axis=1)


def after(vals, deps):
    return lax.optimization_barrier((vals, deps))[0]


def shards(Z, X, Y, inputs, ln1_gain, ln1_bias, w_qkv, bias_q, bias_v, w_out, bias_out, ln2_gain, ln2_bias,
           w_up, bias_up, w_down, bias_down, lengths, cotangent):
    F = inputs.shape[1]
    K = 2 * Y
    S = F * K
    T = min(256, F)
    W = D // K
    HG = H // K
    B = Z * X
    zi, xi, y, c = (lax.axis_index(n) for n in ("z", "x", "y", "c"))
    group = y * 2 + c
    sds = jax.ShapeDtypeStruct

    def shift(v, axis, n, s):
        return lax.ppermute(v, axis, [(i, (i + s) % n) for i in range(n)])

    def mate(v):
        return lax.ppermute(v, "c", [(0, 1), (1, 0)])

    rel = [(s, d) for s in range(Y) for d in range(2)]

    def hop(v, s, d):
        pairs = [(yy * 2 + cc, ((yy + s) % Y) * 2 + (cc ^ d)) for yy in range(Y) for cc in range(2)]
        return lax.ppermute(v, ("y", "c"), pairs)

    def flip(d):
        return c if d == 0 else 1 - c

    blocks = jnp.stack([((y - s) % Y) * 2 + flip(d) for s, d in rel])
    ends = jnp.cumsum(lengths.reshape(-1))
    pos = (blocks[:, None] * F + jnp.arange(F, dtype=jnp.int32)[None]).reshape(1, S)
    piece = jnp.sum((pos >= ends[:, None]).astype(jnp.int32), axis=0, keepdims=True)
    pieces = ends.shape[0]
    starts = jnp.concatenate([jnp.zeros((1,), ends.dtype), ends[:-1]])

    def look(table, idx):
        return jnp.sum(jnp.where(idx == jnp.arange(pieces)[:, None], table[:, None], 0), axis=0, keepdims=True)

    pad = piece >= pieces
    lo = jnp.where(pad, pos, look(starts, (piece // 3) * 3)).astype(jnp.int32)
    hi = jnp.where(pad | (piece % 3 == 2), pos + 1, look(ends, piece)).astype(jnp.int32)
    base = pos[0, ::T].astype(jnp.int32)
    qlo = jnp.min(lo.reshape(S // T, T), axis=1)
    qhi = jnp.max(hi.reshape(S // T, T), axis=1)
    active = (base[None, :] < qhi[:, None]) & (base[None, :] + T > qlo[:, None])
    lst_q, cnt_q = tile_list(active)
    lst_k, cnt_k = tile_list(active.T)

    x_own = inputs.reshape(F, D)
    up = cotangent.reshape(F, D)
    flat_in = x_own.astype(F32)

    def cols_of(w, g):
        return [lax.dynamic_slice_in_dim(w, part * D + g * W, W, w.ndim - 1) for part in range(3)]

    far = [shift(x_own, "y", Y, s) for s in range(1, Y)]
    near = mate(x_own)
    w_g = jnp.concatenate(cols_of(w_qkv, group), axis=1)
    w_m = jnp.concatenate(cols_of(w_qkv, y * 2 + 1 - c), axis=1)
    b_g = jnp.concatenate([lax.dynamic_slice_in_dim(bias_q, group * W, W, 0), jnp.zeros((W,), F32),
                           lax.dynamic_slice_in_dim(bias_v, group * W, W, 0)])[None]
    sc_g = jnp.where(jnp.arange(3 * W) < W, HD**-0.5, 1.0).astype(F32)[None]
    ln1 = (ln1_gain[None], ln1_bias[None])
    held = qkv_call(x_own, *ln1, w_g, b_g, sc_g, 0, K, None)
    held = qkv_call(near, *ln1, w_g, b_g, sc_g, 1, K, held)
    dg = dg_call(after(up, (held[1], w_m)), w_down)
    xs = [x_own, near]
    for i, r in enumerate(far):
        r = after(r, dg) if i == 0 else r
        xs += [r, mate(r)]
        held = qkv_call(xs[-2], *ln1, w_g, b_g, sc_g, 2 * i + 2, K, held)
        held = qkv_call(xs[-1], *ln1, w_g, b_g, sc_g, 2 * i + 3, K, held)
    h_all, qkv = held
    lse_shape = sds((HG, S), F32)
    ctx_g, lse = attend(
        functools.partial(fwd_kernel, T, HG), (lst_q, cnt_q, base),
        [(qkv, (W, 0)), (qkv, (W, 1)), (qkv, (W, 2)), (lo, None), (hi, None)],
        [sds((S, W), BF), lse_shape], [], 12 * 10**9)

    mine = [ctx_g[:F]] + [hop(ctx_g[(2 * s + d) * F : (2 * s + d + 1) * F], -s, d) for s, d in rel[1:]]
    x_all = jnp.concatenate(after(xs, ctx_g), axis=0)
    mine[1:] = after(mine[1:], x_all)
    groups = jnp.stack([((y + s) % Y) * 2 + flip(d) for s, d in rel]).astype(jnp.int32)
    middle, h2 = out_call([ctx_g] + mine[1:], groups, w_out, x_own, bias_out[None], ln2_gain[None], ln2_bias[None])
    act, du, dh2, g_bu = mlp_call(h2, w_up, bias_up[None], dg)
    mine = jnp.stack(after(mine, dh2))
    ctx = jnp.concatenate(
        [lax.dynamic_index_in_dim(mine, ((yy - y) % Y) * 2 + (cc ^ c), 0, keepdims=False)
         for yy in range(Y) for cc in range(2)], axis=1)

    def shaped(g):
        return g.reshape(Z, X, Y, g.shape[2], W)

    def begin(items, n, me, send, dep=None):
        def cut(g, axis, i):
            return lax.dynamic_index_in_dim(g, i, axis, keepdims=False)

        def piece(terms, axis, i):
            return settle([cut(g, axis, i) for g in terms]).reshape(-1, W)

        bufs = [jnp.concatenate([piece(g, ax, (me + s) % n) for g, ax in items]) for s in range(1, n)]
        if dep is not None:
            bufs = after(bufs, dep)
        return [[cut(g, ax, me) for g in terms] for terms, ax in items], [send(b, s + 1) for s, b in enumerate(bufs)], bufs

    def settle(terms):
        return sum((g.astype(F32) for g in terms[1:]), terms[0].astype(F32)).astype(BF)

    def finish(state):
        own, sent, _ = state
        out, at = [], 0
        for terms in own:
            rows = terms[0].size // W
            out.append(terms + [r[at : at + rows].reshape(terms[0].shape) for r in sent])
            at += rows
        return out

    def hold(states, others):
        sent, others = lax.optimization_barrier(([st[1] for st in states], others))
        return [(st[0], r, st[2]) for st, r in zip(states, sent)], others

    def head(terms):
        return [g[0] for g in terms]

    def over_y(items):
        return begin(items, Y, y, lambda v, s: shift(v, "y", Y, s))

    def over_x(items):
        return begin(items, X, xi, lambda v, s: shift(v, "x", X, s))

    def over_z(items, bit, dep=None):
        bits = [([g.reshape((g.shape[0] // 2, 2) + g.shape[1:]) for g in terms], 1) for terms in items]
        return begin(bits, 2, (zi // bit) % 2, lambda v, s: lax.ppermute(v, "z", [(i, i ^ bit) for i in range(Z)]), dep)

    assert Z & (Z - 1) == 0
    zbits = [1 << i for i in range(Z.bit_length() - 1)]

    def total(v):
        return jnp.sum(v.astype(F32), axis=0)

    def rows_of(vecs):
        return jnp.concatenate([v.reshape(B, -1) for v in vecs], axis=1).astype(BF).reshape(B, -1, W)

    hr = w_down.shape[0] // B // 2
    pr = qr = 5 * hr // 8 // 16 * 16
    n_ot = D // B
    ur = hr + n_ot // 2

    (dn_give,) = wgrad_rows(act, up, 1 - c, Y, B)
    dn_got = mate(dn_give)
    (up_give,) = wgrad_cols(h2, after(du, dn_give), 1 - c, Y, B, W)
    up_got = mate(up_give)
    dy1, da, dctx, sums = ln2_call(after(dh2, up_give), middle, up, ln2_gain[None], w_out)

    def heads_of(s, d):
        return lax.dynamic_slice_in_dim(dctx, (((y + s) % Y) * 2 + flip(d)) * W, W, 1)

    def both(s):
        return jnp.concatenate([heads_of(s, 0), heads_of(s, 1)])

    do_y = [both(0)] + [shift(both(s), "y", Y, s) for s in range(1, Y)]

    (ot_give,) = wgrad_cols(ctx, after(da, do_y[0]), 1 - c, Y, B, W)
    ot_got = mate(ot_give)
    dnP, dnQ, dnR = wgrad_rows(act, after(up, ot_give), c, Y, B, dn_got, (pr, pr + qr))
    (dnP, dnQ, dnR), ot_got = lax.optimization_barrier(((dnP, dnQ, dnR), ot_got))
    t_y, t_x, t_r = over_y([([shaped(dnP)], 2)]), over_x([([shaped(dnQ)], 1)]), over_z([[shaped(dnR)]], 1)
    h2_, ctx_, da_ = after((h2, ctx, da), (t_y[2], t_x[2], t_r[2]))
    upQ, upP = wgrad_cols(h2_, du, c, Y, B, W, up_got, (ur,))
    do_y = after(do_y, (t_y[2], t_x[2], t_r[2]))
    do_c = mate(jnp.concatenate([v[F:] for v in do_y]))
    do_g = jnp.concatenate([b for s in range(Y) for b in (do_y[s][:F], do_c[s * F : (s + 1) * F])])
    (upP,) = wgrad_cols(ctx_, da_, c, Y, B, W, ot_got, (), upP)
    n_y, n_x = over_y([([shaped(upP)], 2)]), over_x([([shaped(upQ)], 1)])
    (t_y, t_x, t_r), (n_bufs, do_g) = hold([t_y, t_x, t_r], ((n_y[2], n_x[2]), do_g))
    (dnP,), (dnQ,), (dnR,) = finish(t_y), finish(t_x), finish(t_r)

    t_y, t_x, t_z, t_r = n_y, n_x, over_z([dnQ], 1), over_z([dnR], zbits[1])
    dnP = settle(dnP)
    early = rows_of([sums[2], sums[0], sums[1], sums[3], g_bu[0]])
    do_g = after(do_g, (n_bufs, t_z[2], t_r[2], early, dnP))
    (dqkv,) = attend(
        functools.partial(bwd_kernel, T, HG), (lst_k, cnt_k, base),
        [(qkv, (W, 0)), (qkv, (W, 1)), (qkv, (W, 2)), (ctx_g, None), (do_g, None), (lse, None), (lo, None), (hi, None)],
        [sds((S, 3 * W), BF)], [pltpu.VMEM((W, S), F32), pltpu.VMEM((HG, S), F32)], 20 * 10**9)
    (t_y, t_x, t_z, t_r), (dqkv, dnP) = hold([t_y, t_x, t_z, t_r], (dqkv, dnP))
    def rest(items, k):
        for bit in zbits[k:]:
            items = finish(over_z(items, bit))
        return items

    (upP,), (upQ,), (dnQ,), (dnR,) = finish(t_y), finish(t_x), finish(t_z), rest(finish(t_r), 2)

    def of_x(i):
        return jnp.concatenate([settle([lax.dynamic_index_in_dim(g, i, 1, keepdims=False) for g in terms])
                                for terms in ([dnP], upP)], axis=1)

    p_bufs, p_own = [of_x((xi + s) % X) for s in range(1, X)], of_x(xi)
    t_x = ([[p_own]], [shift(b, "x", X, s + 1) for s, b in enumerate(p_bufs)], p_bufs)
    t_a, t_b = over_z([upQ], 1), over_z([dnQ], zbits[1])
    dq_got = mate(dqkv.reshape(Y, 2, F, 3 * W)[:, 1].reshape(Y * F, 3 * W))
    qv = qgrad(h_all, after(dqkv, (p_bufs, t_a[2])), B)
    dh_far, dh_own, g_ln1 = dh_call(dqkv, after(dq_got, qv), w_g, w_m, x_all, Y)
    far = [shift(dh_far[s * F : (s + 1) * F], "y", Y, -s - 1) for s in range(Y - 1)]
    cols = total(dqkv)
    mine_only = jnp.arange(D) // W == group
    late = rows_of([g_ln1[0], g_ln1[1]] + [jnp.where(mine_only, jnp.tile(v, K), 0.0) for v in (cols[:W], cols[2 * W :])])
    vec = jnp.concatenate([late, early], axis=1)
    vec = jnp.pad(vec, ((0, 0), (0, -vec.shape[1] % 16), (0, 0)))
    qv = jnp.concatenate([qv, vec], axis=1).reshape(Z, X, -1, W)
    n_x = over_x([([qv], 1), (dnR, 1)])
    (t_x, t_a, t_b), n_bufs = hold([t_x, t_a, t_b], n_x[2])
    parts, upQ, dnQ = [p_own] + t_x[1], finish(t_a)[0], finish(t_b)[0]

    t_x = n_x
    t_a, t_b = over_z([parts], 1), over_z([upQ], zbits[1])
    result = down_call(after(act, (n_bufs, t_a[2], t_b[2])), w_down, middle, bias_down[None])
    (t_x, t_a, t_b), (far, result) = hold([t_x, t_a, t_b], (far, result))

    (qv, dnR), (parts,), (upQ,), (dnQ,) = finish(t_x), finish(t_a), rest(finish(t_b), 2), rest([dnQ], 2)

    t_a, t_b = over_z([qv], 1), over_z([parts], zbits[1])
    t_y = over_y([(head(dnQ), 0), (head(upQ), 0), (head(dnR), 0)])
    far, dh_own = after((far, dh_own), (t_a[2], t_b[2], t_y[2]))
    dh1 = sum((r.astype(F32) for r in far), dh_own.astype(F32))
    _, norm_back_one = jax.vjp(lambda v: layer_norm(v, ln1_gain, ln1_bias), flat_in)
    (dx,) = norm_back_one(dh1)
    grad_inputs = (dy1 + dx).reshape(1, F, D)
    (t_a, t_b, t_y), grad_inputs = hold([t_a, t_b, t_y], grad_inputs)
    (qv,), (parts,), (dnQ, upQ, dnR) = finish(t_a), rest(finish(t_b), 2), finish(t_y)

    t_b = over_z([qv], zbits[1])
    parts, dnQ, upQ, dnR = after((head(parts), dnQ, upQ, dnR), t_b[2])
    parts = settle(parts)
    first = jnp.concatenate([parts[:pr], settle(dnQ), settle(dnR), settle(upQ), parts[pr:]])

    def share_y(g):
        return [g] + [shift(g, "y", Y, s) for s in range(1, Y)]

    first_y = share_y(first)
    (t_b,), first_y = hold([t_b], first_y)
    (qv,) = rest(finish(t_b), 2)
    tail_y = share_y(settle(head(qv)))

    def share_c(got):
        got = jnp.stack(got)
        other = mate(got)

        def piece(yy, cc):
            i = (y - yy) % Y
            return jnp.where(cc == c, lax.dynamic_index_in_dim(got, i, 0, keepdims=False),
                             lax.dynamic_index_in_dim(other, i, 0, keepdims=False))

        return [[piece(yy, cc) for cc in range(2)] for yy in range(Y)]

    def by_columns(e, at, rows, chunks):
        return jnp.concatenate([e[yy][cc][at + k * rows : at + (k + 1) * rows] for cc in range(2) for yy in range(Y)
                                for k in range(chunks)], axis=1).astype(F32)

    first_e = share_c(first_y)
    n_dn = 2 * hr
    g_w_down = by_columns(first_e, 0, n_dn, 1)
    g_w_up = by_columns(first_e, n_dn, n_ot, 2 * ur // n_ot - 1)
    g_w_out = by_columns(first_e, n_dn + 2 * ur - n_ot, n_ot, 1)
    tail_y, g_w_down, g_w_up, g_w_out = lax.optimization_barrier((tail_y, g_w_down, g_w_up, g_w_out))
    tail_e = share_c(tail_y)
    g_w_qkv = jnp.concatenate([tail_e[yy][cc][p * n_ot : (p + 1) * n_ot] for p in range(3) for yy in range(Y)
                               for cc in range(2)], axis=1).astype(F32)
    at = 3 * n_ot
    flat = sum(tail_e[yy][cc][at:].astype(F32) for yy in range(Y) for cc in range(2)).reshape(-1)
    out, at = [], 0
    for n in (D, D, D, D, D, D, D, D, w_up.shape[1]):
        out.append(flat[at : at + n // B])
        at += n // B
    g_ln1g, g_ln1b, g_bq, g_bv, g_bo, g_ln2g, g_ln2b, g_bd, g_bu = out
    return (result.reshape(1, F, D), grad_inputs, g_ln1g, g_ln1b, g_w_qkv, g_bq, g_bv, g_w_out, g_bo, g_ln2g, g_ln2b,
            g_w_up, g_bu, g_w_down, g_bd)


def solution(mesh):
    batch, blk = mesh.shape["batch"], mesh.shape["blk"]
    Y = blk // 2
    X = Y if batch % Y == 0 else 1
    Z = batch // X
    fine = Mesh(mesh.devices.reshape(Z, X, Y, 2), ("z", "x", "y", "c"))
    rows, slots = ("z", "x"), ("y", "c")
    act = P(rows, slots, None)
    flat, mat = P(rows), P(rows, None)
    return jax.shard_map(
        functools.partial(shards, Z, X, Y),
        mesh=fine,
        in_specs=(act,) + (P(),) * 13 + (P(rows, None, None), act),
        out_specs=(act, act, flat, flat, mat, flat, flat, mat, flat, flat, flat, mat, flat, mat, flat),
        check_vma=False,
    )
```

```python
import functools

import jax
import jax.numpy as jnp
from jax import lax
from jax.experimental import pallas as pl
from jax.experimental.pallas import tpu as pltpu
from jax.sharding import Mesh
from jax.sharding import PartitionSpec as P

D = 1024
H = 16
HD = 64
EPS = 1e-05
NEG = -1e30
VM = 20
AV = 28
BF = jnp.bfloat16
F32 = jnp.float32


def layer_norm(values, gain_vec, shift_vec):
    center = values - jnp.mean(values, axis=-1, keepdims=True)
    spread = jnp.mean(center * center, axis=-1, keepdims=True)
    return center * lax.rsqrt(spread + EPS) * gain_vec + shift_vec


def dot(a, b):
    return jnp.dot(a, b, preferred_element_type=F32)


def dot_tn(a, b):
    return lax.dot_general(a, b, (((0,), (0,)), ((), ())), preferred_element_type=F32)


def dot_nt(a, b):
    return lax.dot_general(a, b, (((1,), (1,)), ((), ())), preferred_element_type=F32)


def half(a, h):
    a = a[:, (h // 2) * 2 * HD : (h // 2 + 1) * 2 * HD]
    lane = lax.broadcasted_iota(jnp.int32, a.shape, 1)
    zero = jnp.zeros_like(a)
    return jnp.where(lane < HD, a, zero) if h % 2 == 0 else jnp.where(lane < HD, zero, a)


def pair(a, h):
    return a[:, (h // 2) * 2 * HD : (h // 2 + 1) * 2 * HD]


def fwd_kernel(T, HG, lst, cnt, base, q_ref, k_ref, v_ref, lo_ref, hi_ref, ctx_ref, lse_ref):
    nq = q_ref.shape[0] // T
    row = lax.broadcasted_iota(jnp.int32, (T, T), 0)

    @pl.loop(0, nq)
    def _(qt):
        at = pl.ds(pl.multiple_of(qt * T, T), T)
        q = q_ref[at, :]
        qh = [half(q, h) for h in range(HG)]
        lo, hi = lo_ref[:, at], hi_ref[:, at]

        def body(n, carry):
            t = lst[qt, n]
            ks = pl.ds(pl.multiple_of(t * T, T), T)
            k, v = k_ref[ks, :], v_ref[ks, :].T
            vis = (row >= lo - base[t]) & (row < hi - base[t])
            raw = [dot_nt(pair(k, h), qh[h]) for h in range(HG)]
            out = []
            for h in range(HG):
                m, l, acc = carry[h]
                s = jnp.where(vis, raw[h], NEG)
                mn = jnp.maximum(m, jnp.max(s, axis=0, keepdims=True))
                a = jnp.exp(m - mn)
                p = jnp.exp(s - mn)
                l = a * l + jnp.sum(p, axis=0, keepdims=True)
                acc = acc * a + dot(v[h * HD : (h + 1) * HD, :], p.astype(BF))
                out.append((mn, l, acc))
            return tuple(out)

        one = (jnp.full((1, T), NEG, F32), jnp.zeros((1, T), F32), jnp.zeros((HD, T), F32))
        res = lax.fori_loop(0, cnt[qt], body, (one,) * HG)
        ctx_ref[at, :] = jnp.concatenate([r[2] / r[1] for r in res], axis=0).T.astype(BF)
        lse_ref[:, at] = jnp.concatenate([r[0] + jnp.log(r[1]) for r in res], axis=0)


def bwd_kernel(T, HG, lst, cnt, base, q_ref, k_ref, v_ref, ctx_ref, do_ref, lse_ref, lo_ref, hi_ref, out_ref, dqt, dl):
    n_tiles = q_ref.shape[0] // T
    W = HG * HD
    row = lax.broadcasted_iota(jnp.int32, (T, T), 0)
    lane = lax.broadcasted_iota(jnp.int32, (T, 2 * HD), 1)
    dqt[...] = jnp.zeros_like(dqt)

    @pl.loop(0, n_tiles)
    def _(t):
        at = pl.ds(pl.multiple_of(t * T, T), T)
        prod = (do_ref[at, :].astype(F32) * ctx_ref[at, :].astype(F32)).T
        dl[:, at] = jnp.concatenate([jnp.sum(prod[h * HD : (h + 1) * HD], axis=0, keepdims=True) for h in range(HG)], axis=0)

    @pl.loop(0, n_tiles)
    def _(kt):
        ks = pl.ds(pl.multiple_of(kt * T, T), T)
        k, v = k_ref[ks, :], v_ref[ks, :]
        kT = k.T
        kh, vh = [half(k, h) for h in range(HG)], [half(v, h) for h in range(HG)]

        def body(n, carry):
            at = pl.ds(pl.multiple_of(lst[kt, n] * T, T), T)
            q, do = q_ref[at, :], do_ref[at, :]
            vis = (row >= lo_ref[:, at] - base[kt]) & (row < hi_ref[:, at] - base[kt])
            raw = [dot_nt(kh[h], pair(q, h)) for h in range(HG)]
            dps = [dot_nt(vh[h], pair(do, h)) for h in range(HG)]
            out = []
            for h in range(HG):
                p = jnp.exp(jnp.where(vis, raw[h], NEG) - lse_ref[h : h + 1, at])
                ds = (p * (dps[h] - dl[h : h + 1, at])).astype(BF)
                out.append((carry[h][0] + dot(ds, pair(q, h)), carry[h][1] + dot(p.astype(BF), pair(do, h))))
                dqt[h * HD : (h + 1) * HD, at] += dot(kT[h * HD : (h + 1) * HD, :], ds)
            return tuple(out)

        one = (jnp.zeros((T, 2 * HD), F32), jnp.zeros((T, 2 * HD), F32))
        res = lax.fori_loop(0, cnt[kt], body, (one,) * HG)
        for p in range(HG // 2):
            cols = slice(p * 2 * HD, (p + 1) * 2 * HD)
            a, b = res[2 * p], res[2 * p + 1]
            out_ref[ks, W + cols.start : W + cols.stop] = jnp.where(lane < HD, a[0], b[0]).astype(BF)
            out_ref[ks, 2 * W + cols.start : 2 * W + cols.stop] = jnp.where(lane < HD, a[1], b[1]).astype(BF)

    @pl.loop(0, n_tiles)
    def _(t):
        at = pl.ds(pl.multiple_of(t * T, T), T)
        out_ref[at, :W] = (dqt[:, at].T * HD**-0.5).astype(BF)


def attend(kernel, scalars, ins, outs, scratch, flops):
    def spec(shape, cols):
        if cols is None:
            return pl.BlockSpec(shape, lambda i, *_: (0,) * len(shape))
        return pl.BlockSpec((shape[0], cols[0]), lambda i, *_: (0, cols[1]))

    size = sum(a.size * a.dtype.itemsize for a, _ in ins) + sum(o.size * o.dtype.itemsize for o in outs)
    return pl.pallas_call(
        kernel,
        out_shape=outs,
        grid_spec=pltpu.PrefetchScalarGridSpec(
            num_scalar_prefetch=len(scalars),
            grid=(1,),
            in_specs=[spec(a.shape, cols) for a, cols in ins],
            out_specs=[spec(o.shape, None) for o in outs],
            scratch_shapes=scratch,
        ),
        compiler_params=pltpu.CompilerParams(vmem_limit_bytes=AV << 20),
        cost_estimate=pl.CostEstimate(flops=flops, bytes_accessed=size, transcendentals=0),
    )(*scalars, *[a for a, _ in ins])


def grid_call(kernel, grid, scalars, ins, outs, flops, scratch=(), aliases=None, vmem=VM, light=1):
    def spec(block, index):
        return pl.BlockSpec(memory_space=pl.ANY) if block is None else pl.BlockSpec(block, index)

    size = sum(a.size * a.dtype.itemsize for a, b, _ in ins if b is not None)
    size += sum(o.size * o.dtype.itemsize for o, _, _ in outs)
    return pl.pallas_call(
        kernel,
        out_shape=[o for o, _, _ in outs],
        grid_spec=pltpu.PrefetchScalarGridSpec(
            num_scalar_prefetch=len(scalars),
            grid=grid,
            in_specs=[spec(b, m) for _, b, m in ins],
            out_specs=[spec(b, m) for _, b, m in outs],
            scratch_shapes=list(scratch),
        ),
        input_output_aliases=aliases or {},
        compiler_params=pltpu.CompilerParams(vmem_limit_bytes=vmem << 20),
        cost_estimate=pl.CostEstimate(flops=flops // light, bytes_accessed=size // light, transcendentals=0),
    )(*scalars, *[a for a, _, _ in ins])


def whole(a):
    return a.shape, lambda *_: (0,) * len(a.shape)


def centred(x):
    x = x.astype(F32)
    center = x - jnp.mean(x, axis=-1, keepdims=True)
    spread = jnp.mean(center * center, axis=-1, keepdims=True)
    return center * lax.rsqrt(spread + EPS)


def qkv_kernel(x_ref, g_ref, b_ref, w_ref, bias_ref, sc_ref, *refs):
    h_ref, o_ref = refs[-2:]
    h = (centred(x_ref[...]) * g_ref[...] + b_ref[...]).astype(BF)
    h_ref[...] = h
    o = (dot(h, w_ref[...]) + bias_ref[...]).astype(BF)
    o_ref[...] = (o.astype(F32) * sc_ref[...]).astype(BF)


def qkv_call(x, g, b, w, bias, sc, r, blocks, held):
    F, n = x.shape[0], w.shape[1]
    TR = min(128, F)
    per = F // TR
    row = lambda i: (i, 0)
    to = lambda i: (r * per + i, 0)
    ins = [(x, (TR, D), row)] + [(v, *whole(v)) for v in (g, b, w, bias, sc)]
    shapes = [jax.ShapeDtypeStruct((blocks * F, D), BF), jax.ShapeDtypeStruct((blocks * F, n), BF)]
    aliases = {}
    if held is not None:
        ins += [(held[0], None, None), (held[1], None, None)]
        aliases = {6: 0, 7: 1}
    return grid_call(qkv_kernel, (per,), (), ins, [(shapes[0], (TR, D), to), (shapes[1], (TR, n), to)],
                     2 * F * D * n, aliases=aliases)


def out_kernel(n, group_ref, *refs):
    x_ref, bias_ref, g_ref, b_ref, mid_ref, h_ref = refs[2 * n :]
    mid = sum(dot(refs[i][...], refs[n + i][...]) for i in range(n)) + bias_ref[...]
    mid = x_ref[...].astype(F32) + mid
    mid_ref[...] = mid
    h_ref[...] = (centred(mid) * g_ref[...] + b_ref[...]).astype(BF)


def out_call(mine, groups, w_out, x, bias, g, b):
    F, n = x.shape[0], len(mine)
    W = mine[0].shape[1]
    TR = min(256, F)
    row = lambda i, gr: (i, 0)
    ins = [(m, (TR, W), row) for m in mine]
    ins += [(w_out, (W, D), lambda i, gr, r=r: (gr[r], 0)) for r in range(n)]
    ins += [(x, (TR, D), row)] + [(v, *whole(v)) for v in (bias, g, b)]
    return grid_call(functools.partial(out_kernel, n), (F // TR,), (groups,), ins,
                     [(jax.ShapeDtypeStruct((F, D), F32), (TR, D), row), (jax.ShapeDtypeStruct((F, D), BF), (TR, D), row)],
                     2 * F * D * D)


def ln2_kernel(dh_ref, mid_ref, up_ref, g_ref, w_ref, dy_ref, da_ref, dctx_ref, sum_ref):
    @pl.when(pl.program_id(0) == 0)
    def _():
        sum_ref[...] = jnp.zeros_like(sum_ref)

    mid, dh, up = mid_ref[...], dh_ref[...], up_ref[...].astype(F32)
    center = mid - jnp.mean(mid, axis=-1, keepdims=True)
    rstd = lax.rsqrt(jnp.mean(center * center, axis=-1, keepdims=True) + EPS)
    xh = center * rstd
    t = dh * g_ref[...]
    d = rstd * (t - jnp.mean(t, axis=-1, keepdims=True) - xh * jnp.mean(t * xh, axis=-1, keepdims=True))
    dy = up + d
    dy_ref[...] = dy
    da = dy.astype(BF)
    da_ref[...] = da
    dctx_ref[...] = dot_nt(da, w_ref[...]).astype(BF)
    for k, v in enumerate((dh * xh, dh, da.astype(F32), up)):
        sum_ref[k : k + 1, :] += jnp.sum(v, axis=0, keepdims=True)


def ln2_call(dh2, middle, up, g, w_out):
    F = up.shape[0]
    TR = min(256, F)
    row = lambda i: (i, 0)
    sds = jax.ShapeDtypeStruct
    return grid_call(
        ln2_kernel, (F // TR,), (),
        [(dh2, (TR, D), row), (middle, (TR, D), row), (up, (TR, D), row), (g, *whole(g)), (w_out, *whole(w_out))],
        [(sds((F, D), F32), (TR, D), row), (sds((F, D), BF), (TR, D), row), (sds((F, D), BF), (TR, D), row),
         (sds((4, D), F32), (4, D), lambda i: (0, 0))], 2 * F * D * D)


def mlp_kernel(sub, h_ref, w_ref, b_ref, dg_ref, act_ref, du_ref, dh_ref, bu_ref):
    rows = h_ref.shape[0]

    @pl.when(pl.program_id(0) == 0)
    def _():
        dh_ref[...] = jnp.zeros_like(dh_ref)

    bu = jnp.zeros(bu_ref.shape, F32)
    for r in range(0, rows, sub):
        at = slice(r, r + sub)
        u = dot(h_ref[at, :], w_ref[...]) + b_ref[...]
        cdf = 0.5 + 0.5 * lax.erf(u * 0.7071067811865476)
        pdf = jnp.exp(-0.5 * u * u) * 0.3989422804014327
        act_ref[at, :] = (u * cdf).astype(BF)
        du = (dg_ref[at, :].astype(F32) * (cdf + u * pdf)).astype(BF)
        du_ref[at, :] = du
        bu = bu + jnp.sum(du.astype(F32), axis=0, keepdims=True)
        dh_ref[at, :] += dot_nt(du, w_ref[...])
    bu_ref[...] = bu


def dg_kernel(c_ref, w_ref, o_ref):
    o_ref[...] = dot_nt(c_ref[...], w_ref[...]).astype(BF)


def dg_call(c, w_down):
    F, FF = c.shape[0], w_down.shape[0]
    N = 512
    (out,) = grid_call(dg_kernel, (FF // N,), (), [(c, *whole(c)), (w_down, (N, D), lambda i: (i, 0))],
                       [(jax.ShapeDtypeStruct((F, FF), BF), (F, N), lambda i: (0, i))], 2 * F * D * FF)
    return out


def down_kernel(a_ref, w_ref, mid_ref, bias_ref, o_ref, acc):
    k = pl.program_id(0)

    @pl.when(k == 0)
    def _():
        acc[...] = mid_ref[...] + bias_ref[...]

    acc[...] += dot(a_ref[...], w_ref[...])

    @pl.when(k == pl.num_programs(0) - 1)
    def _():
        o_ref[...] = acc[...].astype(BF)


def down_call(act, w_down, middle, bias):
    F, FF = act.shape
    N = 1024
    (out,) = grid_call(
        down_kernel, (FF // N,), (),
        [(act, (F, N), lambda k: (0, k)), (w_down, (N, D), lambda k: (k, 0)), (middle, *whole(middle)), (bias, *whole(bias))],
        [(jax.ShapeDtypeStruct((F, D), BF), (F, D), lambda k: (0, 0))], 2 * F * D * FF,
        scratch=[pltpu.VMEM((F, D), F32)], light=8)
    return out


def mlp_call(h2, w_up, bias_up, dg):
    F, FF = dg.shape
    N = 1024
    sds = jax.ShapeDtypeStruct
    col = lambda i: (0, i)
    return grid_call(
        functools.partial(mlp_kernel, min(256, F)), (FF // N,), (),
        [(h2, *whole(h2)), (w_up, (D, N), col), (bias_up, (1, N), col), (dg, (F, N), col)],
        [(sds((F, FF), BF), (F, N), col), (sds((F, FF), BF), (F, N), col), (sds((F, D), F32), (F, D), lambda i: (0, 0)),
         (sds((1, FF), F32), (1, N), col)], 4 * F * D * FF, vmem=28)


def wgrad_kernel(put, n, half_ref, *refs):
    put([dot_tn(refs[2 * i][...], refs[2 * i + 1][...]) for i in range(n)], refs[2 * n :])


def wgrad_rows(a, b, side, Y, B, add=None, splits=()):
    k, M = a.shape
    N = b.shape[1] // 2
    W, R = N // Y, M // B
    per = min(B, max(1, 1024 // R))
    idx = lambda i, h: (i, 0, 0, 0)
    ends = list(splits) + [R]

    def put(prods, refs):
        (o,) = prods
        for p in range(per):
            for q in range(Y):
                v = o[p * R : (p + 1) * R, q * W : (q + 1) * W]
                if add is not None:
                    v = v + refs[0][p, q].astype(F32)
                v = v.astype(BF)
                for ref, lo, hi in zip(refs[-len(ends) :], [0] + ends, ends):
                    ref[p, q] = v[lo:hi]

    ins = [(a, (k, per * R), lambda i, h: (0, i)), (b, (k, N), lambda i, h: (0, h[0]))]
    if add is not None:
        ins.append((add, (per, Y, R, W), idx))
    sizes = [hi - lo for lo, hi in zip([0] + ends, ends)]
    return grid_call(functools.partial(wgrad_kernel, put, 1), (B // per,), (side.reshape(1),), ins,
                     [(jax.ShapeDtypeStruct((B, Y, r, W), BF), (per, Y, r, W), idx) for r in sizes], 2 * k * M * N)


def wgrad_cols(a, b, side, Y, B, W, add=None, splits=(), lead=None):
    k, M = a.shape
    R, cut = M // B, b.shape[1] // (2 * Y * W)
    before = 0 if lead is None else lead.shape[2]
    rows = R * cut
    idx = lambda j, h: (0, j, 0, 0)
    ends = [before + e for e in splits] + [before + rows]

    def put(prods, refs):
        (o,) = prods
        if lead is not None:
            refs[-1][:, 0, :before] = refs[-2][:, 0]
        for p in range(cut):
            v = o[:, p * W : (p + 1) * W].reshape(B, R, W)
            if add is not None:
                v = v + refs[0][:, 0, p * R : (p + 1) * R].astype(F32)
            v = v.astype(BF)
            for ref, lo, hi in zip(refs[-len(ends) :], [0] + ends, ends):
                a0, a1 = max(lo, before + p * R), min(hi, before + (p + 1) * R)
                if a0 < a1:
                    ref[:, 0, a0 - lo : a1 - lo] = v[:, a0 - before - p * R : a1 - before - p * R]

    ins = [(a, *whole(a)), (b, (k, cut * W), lambda j, h: (0, h[0] * Y + j))]
    if add is not None:
        ins.append((add, (B, 1, rows, W), idx))
    if lead is not None:
        ins.append((lead, (B, 1, before, W), idx))
    sizes = [hi - lo for lo, hi in zip([0] + ends, ends)]
    return grid_call(functools.partial(wgrad_kernel, put, 1), (Y,), (side.reshape(1),), ins,
                     [(jax.ShapeDtypeStruct((B, Y, r, W), BF), (B, 1, r, W), idx) for r in sizes],
                     2 * k * M * b.shape[1] // 2)


def qgrad_kernel(a_ref, b_ref, o_ref):
    o_ref[...] = dot_tn(a_ref[...], b_ref[...]).reshape(o_ref.shape).astype(BF)


def qgrad(h_all, dqkv, B):
    S, n = dqkv.shape
    W = n // 3
    (out,) = grid_call(
        qgrad_kernel, (3,), (), [(h_all, *whole(h_all)), (dqkv, (S, W), lambda p: (0, p))],
        [(jax.ShapeDtypeStruct((B, 3 * D // B, W), BF), (B, D // B, W), lambda p: (0, p, 0))], 2 * S * D * n, light=8)
    return out


def dh_kernel(n_far, dq_ref, got_ref, w_ref, wm_ref, x_ref, far_ref, own_ref, sum_ref):
    i = pl.program_id(0)

    @pl.when(i == 0)
    def _():
        sum_ref[...] = jnp.zeros_like(sum_ref)

    part = dot_nt(dq_ref[...], w_ref[...]) + dot_nt(got_ref[...], wm_ref[...])
    low = part.astype(BF)

    @pl.when(i < n_far)
    def _():
        far_ref[...] = low

    @pl.when(i >= n_far)
    def _():
        own_ref[...] = low

    sum_ref[0:1, :] += jnp.sum(part * centred(x_ref[...]), axis=0, keepdims=True)
    sum_ref[1:2, :] += jnp.sum(part, axis=0, keepdims=True)


def dh_call(dqkv, got, w_g, w_m, x_all, Y):
    S, n = dqkv.shape
    F = S // (2 * Y)
    TR = min(256, F)
    per = F // TR
    n_far = (Y - 1) * per
    block = lambda i: (i // per + 1) % Y
    full = lambda i: (2 * block(i) * per + i % per, 0)
    sds = jax.ShapeDtypeStruct
    return grid_call(
        functools.partial(dh_kernel, n_far), (Y * per,), (),
        [(dqkv, (TR, n), full), (got, (TR, n), lambda i: (block(i) * per + i % per, 0)), (w_g, *whole(w_g)),
         (w_m, *whole(w_m)), (x_all, (TR, D), full)],
        [(sds(((Y - 1) * F, D), BF), (TR, D), lambda i: (jnp.minimum(i, n_far - 1), 0)),
         (sds((F, D), BF), (TR, D), lambda i: (jnp.maximum(i - n_far, 0), 0)),
         (sds((2, D), F32), (2, D), lambda i: (0, 0))],
        2 * S * D * n, light=8)


def tile_list(active):
    m = active.shape[1]
    hit = active.astype(jnp.int32)
    upto = jnp.tril(jnp.ones((m, m), jnp.int32))
    rank = jnp.sum(hit[:, None, :] * upto[None], axis=2) - 1
    ids = jnp.arange(m, dtype=jnp.int32)
    here = (rank[:, :, None] == ids[None, None, :]) & active[:, :, None]
    return jnp.sum(jnp.where(here, ids[None, :, None], 0), axis=1), jnp.sum(hit, axis=1)


def after(vals, deps):
    return lax.optimization_barrier((vals, deps))[0]


def shards(Z, X, Y, inputs, ln1_gain, ln1_bias, w_qkv, bias_q, bias_v, w_out, bias_out, ln2_gain, ln2_bias,
           w_up, bias_up, w_down, bias_down, lengths, cotangent):
    F = inputs.shape[1]
    K = 2 * Y
    S = F * K
    T = min(256, F)
    W = D // K
    HG = H // K
    B = Z * X
    zi, xi, y, c = (lax.axis_index(n) for n in ("z", "x", "y", "c"))
    group = y * 2 + c
    sds = jax.ShapeDtypeStruct

    def shift(v, axis, n, s):
        return lax.ppermute(v, axis, [(i, (i + s) % n) for i in range(n)])

    def mate(v):
        return lax.ppermute(v, "c", [(0, 1), (1, 0)])

    rel = [(s, d) for s in range(Y) for d in range(2)]

    def hop(v, s, d):
        pairs = [(yy * 2 + cc, ((yy + s) % Y) * 2 + (cc ^ d)) for yy in range(Y) for cc in range(2)]
        return lax.ppermute(v, ("y", "c"), pairs)

    def flip(d):
        return c if d == 0 else 1 - c

    blocks = jnp.stack([((y - s) % Y) * 2 + flip(d) for s, d in rel])
    ends = jnp.cumsum(lengths.reshape(-1))
    pos = (blocks[:, None] * F + jnp.arange(F, dtype=jnp.int32)[None]).reshape(1, S)
    piece = jnp.sum((pos >= ends[:, None]).astype(jnp.int32), axis=0, keepdims=True)
    pieces = ends.shape[0]
    starts = jnp.concatenate([jnp.zeros((1,), ends.dtype), ends[:-1]])

    def look(table, idx):
        return jnp.sum(jnp.where(idx == jnp.arange(pieces)[:, None], table[:, None], 0), axis=0, keepdims=True)

    pad = piece >= pieces
    lo = jnp.where(pad, pos, look(starts, (piece // 3) * 3)).astype(jnp.int32)
    hi = jnp.where(pad | (piece % 3 == 2), pos + 1, look(ends, piece)).astype(jnp.int32)
    base = pos[0, ::T].astype(jnp.int32)
    qlo = jnp.min(lo.reshape(S // T, T), axis=1)
    qhi = jnp.max(hi.reshape(S // T, T), axis=1)
    active = (base[None, :] < qhi[:, None]) & (base[None, :] + T > qlo[:, None])
    lst_q, cnt_q = tile_list(active)
    lst_k, cnt_k = tile_list(active.T)

    x_own = inputs.reshape(F, D)
    up = cotangent.reshape(F, D)
    flat_in = x_own.astype(F32)

    def cols_of(w, g):
        return [lax.dynamic_slice_in_dim(w, part * D + g * W, W, w.ndim - 1) for part in range(3)]

    far = [shift(x_own, "y", Y, s) for s in range(1, Y)]
    near = mate(x_own)
    w_g = jnp.concatenate(cols_of(w_qkv, group), axis=1)
    w_m = jnp.concatenate(cols_of(w_qkv, y * 2 + 1 - c), axis=1)
    b_g = jnp.concatenate([lax.dynamic_slice_in_dim(bias_q, group * W, W, 0), jnp.zeros((W,), F32),
                           lax.dynamic_slice_in_dim(bias_v, group * W, W, 0)])[None]
    sc_g = jnp.where(jnp.arange(3 * W) < W, HD**-0.5, 1.0).astype(F32)[None]
    ln1 = (ln1_gain[None], ln1_bias[None])
    held = qkv_call(x_own, *ln1, w_g, b_g, sc_g, 0, K, None)
    held = qkv_call(near, *ln1, w_g, b_g, sc_g, 1, K, held)
    dg = dg_call(after(up, (held[1], w_m)), w_down)
    xs = [x_own, near]
    for i, r in enumerate(far):
        r = after(r, dg) if i == 0 else r
        xs += [r, mate(r)]
        held = qkv_call(xs[-2], *ln1, w_g, b_g, sc_g, 2 * i + 2, K, held)
        held = qkv_call(xs[-1], *ln1, w_g, b_g, sc_g, 2 * i + 3, K, held)
    h_all, qkv = held
    lse_shape = sds((HG, S), F32)
    ctx_g, lse = attend(
        functools.partial(fwd_kernel, T, HG), (lst_q, cnt_q, base),
        [(qkv, (W, 0)), (qkv, (W, 1)), (qkv, (W, 2)), (lo, None), (hi, None)],
        [sds((S, W), BF), lse_shape], [], 12 * 10**9)

    mine = [ctx_g[:F]] + [hop(ctx_g[(2 * s + d) * F : (2 * s + d + 1) * F], -s, d) for s, d in rel[1:]]
    x_all = jnp.concatenate(after(xs, ctx_g), axis=0)
    mine[1:] = after(mine[1:], x_all)
    groups = jnp.stack([((y + s) % Y) * 2 + flip(d) for s, d in rel]).astype(jnp.int32)
    middle, h2 = out_call([ctx_g] + mine[1:], groups, w_out, x_own, bias_out[None], ln2_gain[None], ln2_bias[None])
    act, du, dh2, g_bu = mlp_call(h2, w_up, bias_up[None], dg)
    mine = jnp.stack(after(mine, dh2))
    ctx = jnp.concatenate(
        [lax.dynamic_index_in_dim(mine, ((yy - y) % Y) * 2 + (cc ^ c), 0, keepdims=False)
         for yy in range(Y) for cc in range(2)], axis=1)

    def shaped(g):
        return g.reshape(Z, X, Y, g.shape[2], W)

    def begin(items, n, me, send, dep=None):
        def cut(g, axis, i):
            return lax.dynamic_index_in_dim(g, i, axis, keepdims=False)

        def piece(terms, axis, i):
            return settle([cut(g, axis, i) for g in terms]).reshape(-1, W)

        bufs = [jnp.concatenate([piece(g, ax, (me + s) % n) for g, ax in items]) for s in range(1, n)]
        if dep is not None:
            bufs = after(bufs, dep)
        return [[cut(g, ax, me) for g in terms] for terms, ax in items], [send(b, s + 1) for s, b in enumerate(bufs)], bufs

    def settle(terms):
        return sum((g.astype(F32) for g in terms[1:]), terms[0].astype(F32)).astype(BF)

    def finish(state):
        own, sent, _ = state
        out, at = [], 0
        for terms in own:
            rows = terms[0].size // W
            out.append(terms + [r[at : at + rows].reshape(terms[0].shape) for r in sent])
            at += rows
        return out

    def hold(states, others):
        sent, others = lax.optimization_barrier(([st[1] for st in states], others))
        return [(st[0], r, st[2]) for st, r in zip(states, sent)], others

    def head(terms):
        return [g[0] for g in terms]

    def over_y(items):
        return begin(items, Y, y, lambda v, s: shift(v, "y", Y, s))

    def over_x(items):
        return begin(items, X, xi, lambda v, s: shift(v, "x", X, s))

    def over_z(items, bit, dep=None):
        bits = [([g.reshape((g.shape[0] // 2, 2) + g.shape[1:]) for g in terms], 1) for terms in items]
        return begin(bits, 2, (zi // bit) % 2, lambda v, s: lax.ppermute(v, "z", [(i, i ^ bit) for i in range(Z)]), dep)

    assert Z & (Z - 1) == 0
    zbits = [1 << i for i in range(Z.bit_length() - 1)]

    def total(v):
        return jnp.sum(v.astype(F32), axis=0)

    def rows_of(vecs):
        return jnp.concatenate([v.reshape(B, -1) for v in vecs], axis=1).astype(BF).reshape(B, -1, W)

    hr = w_down.shape[0] // B // 2
    pr = qr = 9 * hr // 16 // 16 * 16
    n_ot = D // B
    ur = hr + n_ot // 2

    (dn_give,) = wgrad_rows(act, up, 1 - c, Y, B)
    dn_got = mate(dn_give)
    (up_give,) = wgrad_cols(h2, after(du, dn_give), 1 - c, Y, B, W)
    up_got = mate(up_give)
    dy1, da, dctx, sums = ln2_call(after(dh2, up_give), middle, up, ln2_gain[None], w_out)

    def heads_of(s, d):
        return lax.dynamic_slice_in_dim(dctx, (((y + s) % Y) * 2 + flip(d)) * W, W, 1)

    def both(s):
        return jnp.concatenate([heads_of(s, 0), heads_of(s, 1)])

    do_y = [both(0)] + [shift(both(s), "y", Y, s) for s in range(1, Y)]

    (ot_give,) = wgrad_cols(ctx, after(da, do_y[0]), 1 - c, Y, B, W)
    ot_got = mate(ot_give)
    dnP, dnQ, dnR = wgrad_rows(act, after(up, ot_give), c, Y, B, dn_got, (pr, pr + qr))
    (dnP, dnQ, dnR), ot_got = lax.optimization_barrier(((dnP, dnQ, dnR), ot_got))
    t_y, t_x, t_r = over_y([([shaped(dnP)], 2)]), over_x([([shaped(dnQ)], 1)]), over_z([[shaped(dnR)]], 1)
    h2_, ctx_, da_ = after((h2, ctx, da), (t_y[2], t_x[2], t_r[2]))
    upQ, upP = wgrad_cols(h2_, du, c, Y, B, W, up_got, (ur,))
    do_y = after(do_y, (t_y[2], t_x[2], t_r[2]))
    do_c = mate(jnp.concatenate([v[F:] for v in do_y]))
    do_g = jnp.concatenate([b for s in range(Y) for b in (do_y[s][:F], do_c[s * F : (s + 1) * F])])
    (upP,) = wgrad_cols(ctx_, da_, c, Y, B, W, ot_got, (), upP)
    n_y, n_x = over_y([([shaped(upP)], 2)]), over_x([([shaped(upQ)], 1)])
    (t_y, t_x, t_r), (n_bufs, do_g) = hold([t_y, t_x, t_r], ((n_y[2], n_x[2]), do_g))
    (dnP,), (dnQ,), (dnR,) = finish(t_y), finish(t_x), finish(t_r)

    t_y, t_x, t_z, t_r = n_y, n_x, over_z([dnQ], 1), over_z([dnR], zbits[1])
    dnP = settle(dnP)
    early = rows_of([sums[2], sums[0], sums[1], sums[3], g_bu[0]])
    do_g = after(do_g, (n_bufs, t_z[2], t_r[2], early, dnP))
    (dqkv,) = attend(
        functools.partial(bwd_kernel, T, HG), (lst_k, cnt_k, base),
        [(qkv, (W, 0)), (qkv, (W, 1)), (qkv, (W, 2)), (ctx_g, None), (do_g, None), (lse, None), (lo, None), (hi, None)],
        [sds((S, 3 * W), BF)], [pltpu.VMEM((W, S), F32), pltpu.VMEM((HG, S), F32)], 20 * 10**9)
    (t_y, t_x, t_z, t_r), (dqkv, dnP) = hold([t_y, t_x, t_z, t_r], (dqkv, dnP))
    def rest(items, k):
        for bit in zbits[k:]:
            items = finish(over_z(items, bit))
        return items

    (upP,), (upQ,), (dnQ,), (dnR,) = finish(t_y), finish(t_x), finish(t_z), rest(finish(t_r), 2)

    def of_x(i):
        return jnp.concatenate([settle([lax.dynamic_index_in_dim(g, i, 1, keepdims=False) for g in terms])
                                for terms in ([dnP], upP)], axis=1)

    p_bufs, p_own = [of_x((xi + s) % X) for s in range(1, X)], of_x(xi)
    t_x = ([[p_own]], [shift(b, "x", X, s + 1) for s, b in enumerate(p_bufs)], p_bufs)
    t_a, t_b = over_z([upQ], 1), over_z([dnQ], zbits[1])
    dq_got = mate(dqkv.reshape(Y, 2, F, 3 * W)[:, 1].reshape(Y * F, 3 * W))
    qv = qgrad(h_all, after(dqkv, (p_bufs, t_a[2])), B)
    dh_far, dh_own, g_ln1 = dh_call(dqkv, after(dq_got, qv), w_g, w_m, x_all, Y)
    far = [shift(dh_far[s * F : (s + 1) * F], "y", Y, -s - 1) for s in range(Y - 1)]
    cols = total(dqkv)
    mine_only = jnp.arange(D) // W == group
    late = rows_of([g_ln1[0], g_ln1[1]] + [jnp.where(mine_only, jnp.tile(v, K), 0.0) for v in (cols[:W], cols[2 * W :])])
    vec = jnp.concatenate([late, early], axis=1)
    vec = jnp.pad(vec, ((0, 0), (0, -vec.shape[1] % 16), (0, 0)))
    qv = jnp.concatenate([qv, vec], axis=1).reshape(Z, X, -1, W)
    n_x = over_x([([qv], 1), (dnR, 1)])
    (t_x, t_a, t_b), n_bufs = hold([t_x, t_a, t_b], n_x[2])
    parts, upQ, dnQ = [p_own] + t_x[1], finish(t_a)[0], finish(t_b)[0]

    t_x = n_x
    t_a, t_b = over_z([parts], 1), over_z([upQ], zbits[1])
    result = down_call(after(act, (n_bufs, t_a[2], t_b[2])), w_down, middle, bias_down[None])
    (t_x, t_a, t_b), (far, result) = hold([t_x, t_a, t_b], (far, result))

    (qv, dnR), (parts,), (upQ,), (dnQ,) = finish(t_x), finish(t_a), rest(finish(t_b), 2), rest([dnQ], 2)

    t_a, t_b = over_z([qv], 1), over_z([parts], zbits[1])
    t_y = over_y([(head(dnQ), 0), (head(upQ), 0), (head(dnR), 0)])
    far, dh_own = after((far, dh_own), (t_a[2], t_b[2], t_y[2]))
    dh1 = sum((r.astype(F32) for r in far), dh_own.astype(F32))
    _, norm_back_one = jax.vjp(lambda v: layer_norm(v, ln1_gain, ln1_bias), flat_in)
    (dx,) = norm_back_one(dh1)
    grad_inputs = (dy1 + dx).reshape(1, F, D)
    (t_a, t_b, t_y), grad_inputs = hold([t_a, t_b, t_y], grad_inputs)
    (qv,), (parts,), (dnQ, upQ, dnR) = finish(t_a), rest(finish(t_b), 2), finish(t_y)

    t_b = over_z([qv], zbits[1])
    parts, dnQ, upQ, dnR = after((head(parts), dnQ, upQ, dnR), t_b[2])
    parts = settle(parts)
    first = jnp.concatenate([parts[:pr], settle(dnQ), settle(dnR), settle(upQ), parts[pr:]])

    def share_y(g):
        return [g] + [shift(g, "y", Y, s) for s in range(1, Y)]

    first_y = share_y(first)
    (t_b,), first_y = hold([t_b], first_y)
    (qv,) = rest(finish(t_b), 2)
    tail_y = share_y(settle(head(qv)))

    def share_c(got):
        got = jnp.stack(got)
        other = mate(got)

        def piece(yy, cc):
            i = (y - yy) % Y
            return jnp.where(cc == c, lax.dynamic_index_in_dim(got, i, 0, keepdims=False),
                             lax.dynamic_index_in_dim(other, i, 0, keepdims=False))

        return [[piece(yy, cc) for cc in range(2)] for yy in range(Y)]

    def by_columns(e, at, rows, chunks):
        return jnp.concatenate([e[yy][cc][at + k * rows : at + (k + 1) * rows] for cc in range(2) for yy in range(Y)
                                for k in range(chunks)], axis=1).astype(F32)

    first_e = share_c(first_y)
    n_dn = 2 * hr
    g_w_down = by_columns(first_e, 0, n_dn, 1)
    g_w_up = by_columns(first_e, n_dn, n_ot, 2 * ur // n_ot - 1)
    g_w_out = by_columns(first_e, n_dn + 2 * ur - n_ot, n_ot, 1)
    tail_y, g_w_down, g_w_up, g_w_out = lax.optimization_barrier((tail_y, g_w_down, g_w_up, g_w_out))
    tail_e = share_c(tail_y)
    g_w_qkv = jnp.concatenate([tail_e[yy][cc][p * n_ot : (p + 1) * n_ot] for p in range(3) for yy in range(Y)
                               for cc in range(2)], axis=1).astype(F32)
    at = 3 * n_ot
    flat = sum(tail_e[yy][cc][at:].astype(F32) for yy in range(Y) for cc in range(2)).reshape(-1)
    out, at = [], 0
    for n in (D, D, D, D, D, D, D, D, w_up.shape[1]):
        out.append(flat[at : at + n // B])
        at += n // B
    g_ln1g, g_ln1b, g_bq, g_bv, g_bo, g_ln2g, g_ln2b, g_bd, g_bu = out
    return (result.reshape(1, F, D), grad_inputs, g_ln1g, g_ln1b, g_w_qkv, g_bq, g_bv, g_w_out, g_bo, g_ln2g, g_ln2b,
            g_w_up, g_bu, g_w_down, g_bd)


def solution(mesh):
    batch, blk = mesh.shape["batch"], mesh.shape["blk"]
    Y = blk // 2
    X = Y if batch % Y == 0 else 1
    Z = batch // X
    fine = Mesh(mesh.devices.reshape(Z, X, Y, 2), ("z", "x", "y", "c"))
    rows, slots = ("z", "x"), ("y", "c")
    act = P(rows, slots, None)
    flat, mat = P(rows), P(rows, None)
    return jax.shard_map(
        functools.partial(shards, Z, X, Y),
        mesh=fine,
        in_specs=(act,) + (P(),) * 13 + (P(rows, None, None), act),
        out_specs=(act, act, flat, flat, mat, flat, flat, mat, flat, flat, flat, mat, flat, mat, flat),
        check_vma=False,
    )
```

```python
import functools

import jax
import jax.numpy as jnp
from jax import lax
from jax.experimental import pallas as pl
from jax.experimental.pallas import tpu as pltpu
from jax.sharding import Mesh
from jax.sharding import PartitionSpec as P

D = 1024
H = 16
HD = 64
EPS = 1e-05
NEG = -1e30
VM = 20
AV = 28
BF = jnp.bfloat16
F32 = jnp.float32


def layer_norm(values, gain_vec, shift_vec):
    center = values - jnp.mean(values, axis=-1, keepdims=True)
    spread = jnp.mean(center * center, axis=-1, keepdims=True)
    return center * lax.rsqrt(spread + EPS) * gain_vec + shift_vec


def dot(a, b):
    return jnp.dot(a, b, preferred_element_type=F32)


def dot_tn(a, b):
    return lax.dot_general(a, b, (((0,), (0,)), ((), ())), preferred_element_type=F32)


def dot_nt(a, b):
    return lax.dot_general(a, b, (((1,), (1,)), ((), ())), preferred_element_type=F32)


def half(a, h):
    a = a[:, (h // 2) * 2 * HD : (h // 2 + 1) * 2 * HD]
    lane = lax.broadcasted_iota(jnp.int32, a.shape, 1)
    zero = jnp.zeros_like(a)
    return jnp.where(lane < HD, a, zero) if h % 2 == 0 else jnp.where(lane < HD, zero, a)


def pair(a, h):
    return a[:, (h // 2) * 2 * HD : (h // 2 + 1) * 2 * HD]


def fwd_kernel(T, HG, lst, cnt, base, q_ref, k_ref, v_ref, lo_ref, hi_ref, ctx_ref, lse_ref):
    nq = q_ref.shape[0] // T
    row = lax.broadcasted_iota(jnp.int32, (T, T), 0)

    @pl.loop(0, nq)
    def _(qt):
        at = pl.ds(pl.multiple_of(qt * T, T), T)
        q = q_ref[at, :]
        qh = [half(q, h) for h in range(HG)]
        lo, hi = lo_ref[:, at], hi_ref[:, at]

        def body(n, carry):
            t = lst[qt, n]
            ks = pl.ds(pl.multiple_of(t * T, T), T)
            k, v = k_ref[ks, :], v_ref[ks, :].T
            vis = (row >= lo - base[t]) & (row < hi - base[t])
            raw = [dot_nt(pair(k, h), qh[h]) for h in range(HG)]
            out = []
            for h in range(HG):
                m, l, acc = carry[h]
                s = jnp.where(vis, raw[h], NEG)
                mn = jnp.maximum(m, jnp.max(s, axis=0, keepdims=True))
                a = jnp.exp(m - mn)
                p = jnp.exp(s - mn)
                l = a * l + jnp.sum(p, axis=0, keepdims=True)
                acc = acc * a + dot(v[h * HD : (h + 1) * HD, :], p.astype(BF))
                out.append((mn, l, acc))
            return tuple(out)

        one = (jnp.full((1, T), NEG, F32), jnp.zeros((1, T), F32), jnp.zeros((HD, T), F32))
        res = lax.fori_loop(0, cnt[qt], body, (one,) * HG)
        ctx_ref[at, :] = jnp.concatenate([r[2] / r[1] for r in res], axis=0).T.astype(BF)
        lse_ref[:, at] = jnp.concatenate([r[0] + jnp.log(r[1]) for r in res], axis=0)


def bwd_kernel(T, HG, lst, cnt, base, q_ref, k_ref, v_ref, ctx_ref, do_ref, lse_ref, lo_ref, hi_ref, out_ref, dqt, dl):
    n_tiles = q_ref.shape[0] // T
    W = HG * HD
    row = lax.broadcasted_iota(jnp.int32, (T, T), 0)
    lane = lax.broadcasted_iota(jnp.int32, (T, 2 * HD), 1)
    dqt[...] = jnp.zeros_like(dqt)

    @pl.loop(0, n_tiles)
    def _(t):
        at = pl.ds(pl.multiple_of(t * T, T), T)
        prod = (do_ref[at, :].astype(F32) * ctx_ref[at, :].astype(F32)).T
        dl[:, at] = jnp.concatenate([jnp.sum(prod[h * HD : (h + 1) * HD], axis=0, keepdims=True) for h in range(HG)], axis=0)

    @pl.loop(0, n_tiles)
    def _(kt):
        ks = pl.ds(pl.multiple_of(kt * T, T), T)
        k, v = k_ref[ks, :], v_ref[ks, :]
        kT = k.T
        kh, vh = [half(k, h) for h in range(HG)], [half(v, h) for h in range(HG)]

        def body(n, carry):
            at = pl.ds(pl.multiple_of(lst[kt, n] * T, T), T)
            q, do = q_ref[at, :], do_ref[at, :]
            vis = (row >= lo_ref[:, at] - base[kt]) & (row < hi_ref[:, at] - base[kt])
            raw = [dot_nt(kh[h], pair(q, h)) for h in range(HG)]
            dps = [dot_nt(vh[h], pair(do, h)) for h in range(HG)]
            out = []
            for h in range(HG):
                p = jnp.exp(jnp.where(vis, raw[h], NEG) - lse_ref[h : h + 1, at])
                ds = (p * (dps[h] - dl[h : h + 1, at])).astype(BF)
                out.append((carry[h][0] + dot(ds, pair(q, h)), carry[h][1] + dot(p.astype(BF), pair(do, h))))
                dqt[h * HD : (h + 1) * HD, at] += dot(kT[h * HD : (h + 1) * HD, :], ds)
            return tuple(out)

        one = (jnp.zeros((T, 2 * HD), F32), jnp.zeros((T, 2 * HD), F32))
        res = lax.fori_loop(0, cnt[kt], body, (one,) * HG)
        for p in range(HG // 2):
            cols = slice(p * 2 * HD, (p + 1) * 2 * HD)
            a, b = res[2 * p], res[2 * p + 1]
            out_ref[ks, W + cols.start : W + cols.stop] = jnp.where(lane < HD, a[0], b[0]).astype(BF)
            out_ref[ks, 2 * W + cols.start : 2 * W + cols.stop] = jnp.where(lane < HD, a[1], b[1]).astype(BF)

    @pl.loop(0, n_tiles)
    def _(t):
        at = pl.ds(pl.multiple_of(t * T, T), T)
        out_ref[at, :W] = (dqt[:, at].T * HD**-0.5).astype(BF)


def attend(kernel, scalars, ins, outs, scratch, flops):
    def spec(shape, cols):
        if cols is None:
            return pl.BlockSpec(shape, lambda i, *_: (0,) * len(shape))
        return pl.BlockSpec((shape[0], cols[0]), lambda i, *_: (0, cols[1]))

    size = sum(a.size * a.dtype.itemsize for a, _ in ins) + sum(o.size * o.dtype.itemsize for o in outs)
    return pl.pallas_call(
        kernel,
        out_shape=outs,
        grid_spec=pltpu.PrefetchScalarGridSpec(
            num_scalar_prefetch=len(scalars),
            grid=(1,),
            in_specs=[spec(a.shape, cols) for a, cols in ins],
            out_specs=[spec(o.shape, None) for o in outs],
            scratch_shapes=scratch,
        ),
        compiler_params=pltpu.CompilerParams(vmem_limit_bytes=AV << 20),
        cost_estimate=pl.CostEstimate(flops=flops, bytes_accessed=size, transcendentals=0),
    )(*scalars, *[a for a, _ in ins])


def grid_call(kernel, grid, scalars, ins, outs, flops, scratch=(), aliases=None, vmem=VM, light=1):
    def spec(block, index):
        return pl.BlockSpec(memory_space=pl.ANY) if block is None else pl.BlockSpec(block, index)

    size = sum(a.size * a.dtype.itemsize for a, b, _ in ins if b is not None)
    size += sum(o.size * o.dtype.itemsize for o, _, _ in outs)
    return pl.pallas_call(
        kernel,
        out_shape=[o for o, _, _ in outs],
        grid_spec=pltpu.PrefetchScalarGridSpec(
            num_scalar_prefetch=len(scalars),
            grid=grid,
            in_specs=[spec(b, m) for _, b, m in ins],
            out_specs=[spec(b, m) for _, b, m in outs],
            scratch_shapes=list(scratch),
        ),
        input_output_aliases=aliases or {},
        compiler_params=pltpu.CompilerParams(vmem_limit_bytes=vmem << 20),
        cost_estimate=pl.CostEstimate(flops=flops // light, bytes_accessed=size // light, transcendentals=0),
    )(*scalars, *[a for a, _, _ in ins])


def whole(a):
    return a.shape, lambda *_: (0,) * len(a.shape)


def centred(x):
    x = x.astype(F32)
    center = x - jnp.mean(x, axis=-1, keepdims=True)
    spread = jnp.mean(center * center, axis=-1, keepdims=True)
    return center * lax.rsqrt(spread + EPS)


def qkv_kernel(x_ref, g_ref, b_ref, w_ref, bias_ref, sc_ref, *refs):
    h_ref, o_ref = refs[-2:]
    h = (centred(x_ref[...]) * g_ref[...] + b_ref[...]).astype(BF)
    h_ref[...] = h
    o = (dot(h, w_ref[...]) + bias_ref[...]).astype(BF)
    o_ref[...] = (o.astype(F32) * sc_ref[...]).astype(BF)


def qkv_call(x, g, b, w, bias, sc, r, blocks, held):
    F, n = x.shape[0], w.shape[1]
    TR = min(128, F)
    per = F // TR
    row = lambda i: (i, 0)
    to = lambda i: (r * per + i, 0)
    ins = [(x, (TR, D), row)] + [(v, *whole(v)) for v in (g, b, w, bias, sc)]
    shapes = [jax.ShapeDtypeStruct((blocks * F, D), BF), jax.ShapeDtypeStruct((blocks * F, n), BF)]
    aliases = {}
    if held is not None:
        ins += [(held[0], None, None), (held[1], None, None)]
        aliases = {6: 0, 7: 1}
    return grid_call(qkv_kernel, (per,), (), ins, [(shapes[0], (TR, D), to), (shapes[1], (TR, n), to)],
                     2 * F * D * n, aliases=aliases)


def out_kernel(n, group_ref, *refs):
    x_ref, bias_ref, g_ref, b_ref, mid_ref, h_ref = refs[2 * n :]
    mid = sum(dot(refs[i][...], refs[n + i][...]) for i in range(n)) + bias_ref[...]
    mid = x_ref[...].astype(F32) + mid
    mid_ref[...] = mid
    h_ref[...] = (centred(mid) * g_ref[...] + b_ref[...]).astype(BF)


def out_call(mine, groups, w_out, x, bias, g, b):
    F, n = x.shape[0], len(mine)
    W = mine[0].shape[1]
    TR = min(256, F)
    row = lambda i, gr: (i, 0)
    ins = [(m, (TR, W), row) for m in mine]
    ins += [(w_out, (W, D), lambda i, gr, r=r: (gr[r], 0)) for r in range(n)]
    ins += [(x, (TR, D), row)] + [(v, *whole(v)) for v in (bias, g, b)]
    return grid_call(functools.partial(out_kernel, n), (F // TR,), (groups,), ins,
                     [(jax.ShapeDtypeStruct((F, D), F32), (TR, D), row), (jax.ShapeDtypeStruct((F, D), BF), (TR, D), row)],
                     2 * F * D * D)


def ln2_kernel(dh_ref, mid_ref, up_ref, g_ref, w_ref, dy_ref, da_ref, dctx_ref, sum_ref):
    @pl.when(pl.program_id(0) == 0)
    def _():
        sum_ref[...] = jnp.zeros_like(sum_ref)

    mid, dh, up = mid_ref[...], dh_ref[...], up_ref[...].astype(F32)
    center = mid - jnp.mean(mid, axis=-1, keepdims=True)
    rstd = lax.rsqrt(jnp.mean(center * center, axis=-1, keepdims=True) + EPS)
    xh = center * rstd
    t = dh * g_ref[...]
    d = rstd * (t - jnp.mean(t, axis=-1, keepdims=True) - xh * jnp.mean(t * xh, axis=-1, keepdims=True))
    dy = up + d
    dy_ref[...] = dy
    da = dy.astype(BF)
    da_ref[...] = da
    dctx_ref[...] = dot_nt(da, w_ref[...]).astype(BF)
    for k, v in enumerate((dh * xh, dh, da.astype(F32), up)):
        sum_ref[k : k + 1, :] += jnp.sum(v, axis=0, keepdims=True)


def ln2_call(dh2, middle, up, g, w_out):
    F = up.shape[0]
    TR = min(256, F)
    row = lambda i: (i, 0)
    sds = jax.ShapeDtypeStruct
    return grid_call(
        ln2_kernel, (F // TR,), (),
        [(dh2, (TR, D), row), (middle, (TR, D), row), (up, (TR, D), row), (g, *whole(g)), (w_out, *whole(w_out))],
        [(sds((F, D), F32), (TR, D), row), (sds((F, D), BF), (TR, D), row), (sds((F, D), BF), (TR, D), row),
         (sds((4, D), F32), (4, D), lambda i: (0, 0))], 2 * F * D * D)


def mlp_kernel(sub, h_ref, w_ref, b_ref, dg_ref, act_ref, du_ref, dh_ref, bu_ref):
    rows = h_ref.shape[0]

    @pl.when(pl.program_id(0) == 0)
    def _():
        dh_ref[...] = jnp.zeros_like(dh_ref)

    bu = jnp.zeros(bu_ref.shape, F32)
    for r in range(0, rows, sub):
        at = slice(r, r + sub)
        u = dot(h_ref[at, :], w_ref[...]) + b_ref[...]
        cdf = 0.5 + 0.5 * lax.erf(u * 0.7071067811865476)
        pdf = jnp.exp(-0.5 * u * u) * 0.3989422804014327
        act_ref[at, :] = (u * cdf).astype(BF)
        du = (dg_ref[at, :].astype(F32) * (cdf + u * pdf)).astype(BF)
        du_ref[at, :] = du
        bu = bu + jnp.sum(du.astype(F32), axis=0, keepdims=True)
        dh_ref[at, :] += dot_nt(du, w_ref[...])
    bu_ref[...] = bu


def dg_kernel(c_ref, w_ref, o_ref):
    o_ref[...] = dot_nt(c_ref[...], w_ref[...]).astype(BF)


def dg_call(c, w_down):
    F, FF = c.shape[0], w_down.shape[0]
    N = 512
    (out,) = grid_call(dg_kernel, (FF // N,), (), [(c, *whole(c)), (w_down, (N, D), lambda i: (i, 0))],
                       [(jax.ShapeDtypeStruct((F, FF), BF), (F, N), lambda i: (0, i))], 2 * F * D * FF)
    return out


def down_kernel(a_ref, w_ref, mid_ref, bias_ref, o_ref, acc):
    k = pl.program_id(0)

    @pl.when(k == 0)
    def _():
        acc[...] = mid_ref[...] + bias_ref[...]

    acc[...] += dot(a_ref[...], w_ref[...])

    @pl.when(k == pl.num_programs(0) - 1)
    def _():
        o_ref[...] = acc[...].astype(BF)


def down_call(act, w_down, middle, bias):
    F, FF = act.shape
    N = 1024
    (out,) = grid_call(
        down_kernel, (FF // N,), (),
        [(act, (F, N), lambda k: (0, k)), (w_down, (N, D), lambda k: (k, 0)), (middle, *whole(middle)), (bias, *whole(bias))],
        [(jax.ShapeDtypeStruct((F, D), BF), (F, D), lambda k: (0, 0))], 2 * F * D * FF,
        scratch=[pltpu.VMEM((F, D), F32)], light=8)
    return out


def mlp_call(h2, w_up, bias_up, dg):
    F, FF = dg.shape
    N = 1024
    sds = jax.ShapeDtypeStruct
    col = lambda i: (0, i)
    return grid_call(
        functools.partial(mlp_kernel, min(256, F)), (FF // N,), (),
        [(h2, *whole(h2)), (w_up, (D, N), col), (bias_up, (1, N), col), (dg, (F, N), col)],
        [(sds((F, FF), BF), (F, N), col), (sds((F, FF), BF), (F, N), col), (sds((F, D), F32), (F, D), lambda i: (0, 0)),
         (sds((1, FF), F32), (1, N), col)], 4 * F * D * FF, vmem=28)


def wgrad_kernel(put, n, half_ref, *refs):
    put([dot_tn(refs[2 * i][...], refs[2 * i + 1][...]) for i in range(n)], refs[2 * n :])


def wgrad_rows(a, b, side, Y, B, add=None, splits=()):
    k, M = a.shape
    N = b.shape[1] // 2
    W, R = N // Y, M // B
    per = min(B, max(1, 1024 // R))
    idx = lambda i, h: (i, 0, 0, 0)
    ends = list(splits) + [R]

    def put(prods, refs):
        (o,) = prods
        for p in range(per):
            for q in range(Y):
                v = o[p * R : (p + 1) * R, q * W : (q + 1) * W]
                if add is not None:
                    v = v + refs[0][p, q].astype(F32)
                v = v.astype(BF)
                for ref, lo, hi in zip(refs[-len(ends) :], [0] + ends, ends):
                    ref[p, q] = v[lo:hi]

    ins = [(a, (k, per * R), lambda i, h: (0, i)), (b, (k, N), lambda i, h: (0, h[0]))]
    if add is not None:
        ins.append((add, (per, Y, R, W), idx))
    sizes = [hi - lo for lo, hi in zip([0] + ends, ends)]
    return grid_call(functools.partial(wgrad_kernel, put, 1), (B // per,), (side.reshape(1),), ins,
                     [(jax.ShapeDtypeStruct((B, Y, r, W), BF), (per, Y, r, W), idx) for r in sizes], 2 * k * M * N)


def wgrad_cols(a, b, side, Y, B, W, add=None, splits=(), lead=None):
    k, M = a.shape
    R, cut = M // B, b.shape[1] // (2 * Y * W)
    before = 0 if lead is None else lead.shape[2]
    rows = R * cut
    idx = lambda j, h: (0, j, 0, 0)
    ends = [before + e for e in splits] + [before + rows]

    def put(prods, refs):
        (o,) = prods
        if lead is not None:
            refs[-1][:, 0, :before] = refs[-2][:, 0]
        for p in range(cut):
            v = o[:, p * W : (p + 1) * W].reshape(B, R, W)
            if add is not None:
                v = v + refs[0][:, 0, p * R : (p + 1) * R].astype(F32)
            v = v.astype(BF)
            for ref, lo, hi in zip(refs[-len(ends) :], [0] + ends, ends):
                a0, a1 = max(lo, before + p * R), min(hi, before + (p + 1) * R)
                if a0 < a1:
                    ref[:, 0, a0 - lo : a1 - lo] = v[:, a0 - before - p * R : a1 - before - p * R]

    ins = [(a, *whole(a)), (b, (k, cut * W), lambda j, h: (0, h[0] * Y + j))]
    if add is not None:
        ins.append((add, (B, 1, rows, W), idx))
    if lead is not None:
        ins.append((lead, (B, 1, before, W), idx))
    sizes = [hi - lo for lo, hi in zip([0] + ends, ends)]
    return grid_call(functools.partial(wgrad_kernel, put, 1), (Y,), (side.reshape(1),), ins,
                     [(jax.ShapeDtypeStruct((B, Y, r, W), BF), (B, 1, r, W), idx) for r in sizes],
                     2 * k * M * b.shape[1] // 2)


def qgrad_kernel(a_ref, b_ref, o_ref):
    o_ref[...] = dot_tn(a_ref[...], b_ref[...]).reshape(o_ref.shape).astype(BF)


def qgrad(h_all, dqkv, B):
    S, n = dqkv.shape
    W = n // 3
    (out,) = grid_call(
        qgrad_kernel, (3,), (), [(h_all, *whole(h_all)), (dqkv, (S, W), lambda p: (0, p))],
        [(jax.ShapeDtypeStruct((B, 3 * D // B, W), BF), (B, D // B, W), lambda p: (0, p, 0))], 2 * S * D * n, light=8)
    return out


def dh_kernel(n_far, dq_ref, got_ref, w_ref, wm_ref, x_ref, far_ref, own_ref, sum_ref):
    i = pl.program_id(0)

    @pl.when(i == 0)
    def _():
        sum_ref[...] = jnp.zeros_like(sum_ref)

    part = dot_nt(dq_ref[...], w_ref[...]) + dot_nt(got_ref[...], wm_ref[...])
    low = part.astype(BF)

    @pl.when(i < n_far)
    def _():
        far_ref[...] = low

    @pl.when(i >= n_far)
    def _():
        own_ref[...] = low

    sum_ref[0:1, :] += jnp.sum(part * centred(x_ref[...]), axis=0, keepdims=True)
    sum_ref[1:2, :] += jnp.sum(part, axis=0, keepdims=True)


def dh_call(dqkv, got, w_g, w_m, x_all, Y):
    S, n = dqkv.shape
    F = S // (2 * Y)
    TR = min(256, F)
    per = F // TR
    n_far = (Y - 1) * per
    block = lambda i: (i // per + 1) % Y
    full = lambda i: (2 * block(i) * per + i % per, 0)
    sds = jax.ShapeDtypeStruct
    return grid_call(
        functools.partial(dh_kernel, n_far), (Y * per,), (),
        [(dqkv, (TR, n), full), (got, (TR, n), lambda i: (block(i) * per + i % per, 0)), (w_g, *whole(w_g)),
         (w_m, *whole(w_m)), (x_all, (TR, D), full)],
        [(sds(((Y - 1) * F, D), BF), (TR, D), lambda i: (jnp.minimum(i, n_far - 1), 0)),
         (sds((F, D), BF), (TR, D), lambda i: (jnp.maximum(i - n_far, 0), 0)),
         (sds((2, D), F32), (2, D), lambda i: (0, 0))],
        2 * S * D * n, light=8)


def tile_list(active):
    m = active.shape[1]
    hit = active.astype(jnp.int32)
    upto = jnp.tril(jnp.ones((m, m), jnp.int32))
    rank = jnp.sum(hit[:, None, :] * upto[None], axis=2) - 1
    ids = jnp.arange(m, dtype=jnp.int32)
    here = (rank[:, :, None] == ids[None, None, :]) & active[:, :, None]
    return jnp.sum(jnp.where(here, ids[None, :, None], 0), axis=1), jnp.sum(hit, axis=1)


def after(vals, deps):
    return lax.optimization_barrier((vals, deps))[0]


def shards(Z, X, Y, inputs, ln1_gain, ln1_bias, w_qkv, bias_q, bias_v, w_out, bias_out, ln2_gain, ln2_bias,
           w_up, bias_up, w_down, bias_down, lengths, cotangent):
    F = inputs.shape[1]
    K = 2 * Y
    S = F * K
    T = min(256, F)
    W = D // K
    HG = H // K
    B = Z * X
    zi, xi, y, c = (lax.axis_index(n) for n in ("z", "x", "y", "c"))
    group = y * 2 + c
    sds = jax.ShapeDtypeStruct

    def shift(v, axis, n, s):
        return lax.ppermute(v, axis, [(i, (i + s) % n) for i in range(n)])

    def mate(v):
        return lax.ppermute(v, "c", [(0, 1), (1, 0)])

    rel = [(s, d) for s in range(Y) for d in range(2)]

    def hop(v, s, d):
        pairs = [(yy * 2 + cc, ((yy + s) % Y) * 2 + (cc ^ d)) for yy in range(Y) for cc in range(2)]
        return lax.ppermute(v, ("y", "c"), pairs)

    def flip(d):
        return c if d == 0 else 1 - c

    blocks = jnp.stack([((y - s) % Y) * 2 + flip(d) for s, d in rel])
    ends = jnp.cumsum(lengths.reshape(-1))
    pos = (blocks[:, None] * F + jnp.arange(F, dtype=jnp.int32)[None]).reshape(1, S)
    piece = jnp.sum((pos >= ends[:, None]).astype(jnp.int32), axis=0, keepdims=True)
    pieces = ends.shape[0]
    starts = jnp.concatenate([jnp.zeros((1,), ends.dtype), ends[:-1]])

    def look(table, idx):
        return jnp.sum(jnp.where(idx == jnp.arange(pieces)[:, None], table[:, None], 0), axis=0, keepdims=True)

    pad = piece >= pieces
    lo = jnp.where(pad, pos, look(starts, (piece // 3) * 3)).astype(jnp.int32)
    hi = jnp.where(pad | (piece % 3 == 2), pos + 1, look(ends, piece)).astype(jnp.int32)
    base = pos[0, ::T].astype(jnp.int32)
    qlo = jnp.min(lo.reshape(S // T, T), axis=1)
    qhi = jnp.max(hi.reshape(S // T, T), axis=1)
    active = (base[None, :] < qhi[:, None]) & (base[None, :] + T > qlo[:, None])
    lst_q, cnt_q = tile_list(active)
    lst_k, cnt_k = tile_list(active.T)

    x_own = inputs.reshape(F, D)
    up = cotangent.reshape(F, D)
    flat_in = x_own.astype(F32)

    def cols_of(w, g):
        return [lax.dynamic_slice_in_dim(w, part * D + g * W, W, w.ndim - 1) for part in range(3)]

    far = [shift(x_own, "y", Y, s) for s in range(1, Y)]
    near = mate(x_own)
    w_g = jnp.concatenate(cols_of(w_qkv, group), axis=1)
    w_m = jnp.concatenate(cols_of(w_qkv, y * 2 + 1 - c), axis=1)
    b_g = jnp.concatenate([lax.dynamic_slice_in_dim(bias_q, group * W, W, 0), jnp.zeros((W,), F32),
                           lax.dynamic_slice_in_dim(bias_v, group * W, W, 0)])[None]
    sc_g = jnp.where(jnp.arange(3 * W) < W, HD**-0.5, 1.0).astype(F32)[None]
    ln1 = (ln1_gain[None], ln1_bias[None])
    held = qkv_call(x_own, *ln1, w_g, b_g, sc_g, 0, K, None)
    held = qkv_call(near, *ln1, w_g, b_g, sc_g, 1, K, held)
    dg = dg_call(after(up, (held[1], w_m)), w_down)
    xs = [x_own, near]
    for i, r in enumerate(far):
        r = after(r, dg) if i == 0 else r
        xs += [r, mate(r)]
        held = qkv_call(xs[-2], *ln1, w_g, b_g, sc_g, 2 * i + 2, K, held)
        held = qkv_call(xs[-1], *ln1, w_g, b_g, sc_g, 2 * i + 3, K, held)
    h_all, qkv = held
    lse_shape = sds((HG, S), F32)
    ctx_g, lse = attend(
        functools.partial(fwd_kernel, T, HG), (lst_q, cnt_q, base),
        [(qkv, (W, 0)), (qkv, (W, 1)), (qkv, (W, 2)), (lo, None), (hi, None)],
        [sds((S, W), BF), lse_shape], [], 12 * 10**9)

    mine = [ctx_g[:F]] + [hop(ctx_g[(2 * s + d) * F : (2 * s + d + 1) * F], -s, d) for s, d in rel[1:]]
    x_all = jnp.concatenate(after(xs, ctx_g), axis=0)
    mine[1:] = after(mine[1:], x_all)
    groups = jnp.stack([((y + s) % Y) * 2 + flip(d) for s, d in rel]).astype(jnp.int32)
    middle, h2 = out_call([ctx_g] + mine[1:], groups, w_out, x_own, bias_out[None], ln2_gain[None], ln2_bias[None])
    act, du, dh2, g_bu = mlp_call(h2, w_up, bias_up[None], dg)
    mine = jnp.stack(after(mine, dh2))
    ctx = jnp.concatenate(
        [lax.dynamic_index_in_dim(mine, ((yy - y) % Y) * 2 + (cc ^ c), 0, keepdims=False)
         for yy in range(Y) for cc in range(2)], axis=1)

    def shaped(g):
        return g.reshape(Z, X, Y, g.shape[2], W)

    def begin(items, n, me, send, dep=None):
        def cut(g, axis, i):
            return lax.dynamic_index_in_dim(g, i, axis, keepdims=False)

        def piece(terms, axis, i):
            return settle([cut(g, axis, i) for g in terms]).reshape(-1, W)

        bufs = [jnp.concatenate([piece(g, ax, (me + s) % n) for g, ax in items]) for s in range(1, n)]
        if dep is not None:
            bufs = after(bufs, dep)
        return [[cut(g, ax, me) for g in terms] for terms, ax in items], [send(b, s + 1) for s, b in enumerate(bufs)], bufs

    def settle(terms):
        return sum((g.astype(F32) for g in terms[1:]), terms[0].astype(F32)).astype(BF)

    def finish(state):
        own, sent, _ = state
        out, at = [], 0
        for terms in own:
            rows = terms[0].size // W
            out.append(terms + [r[at : at + rows].reshape(terms[0].shape) for r in sent])
            at += rows
        return out

    def hold(states, others):
        sent, others = lax.optimization_barrier(([st[1] for st in states], others))
        return [(st[0], r, st[2]) for st, r in zip(states, sent)], others

    def head(terms):
        return [g[0] for g in terms]

    def over_y(items):
        return begin(items, Y, y, lambda v, s: shift(v, "y", Y, s))

    def over_x(items):
        return begin(items, X, xi, lambda v, s: shift(v, "x", X, s))

    def over_z(items, bit, dep=None):
        bits = [([g.reshape((g.shape[0] // 2, 2) + g.shape[1:]) for g in terms], 1) for terms in items]
        return begin(bits, 2, (zi // bit) % 2, lambda v, s: lax.ppermute(v, "z", [(i, i ^ bit) for i in range(Z)]), dep)

    assert Z & (Z - 1) == 0
    zbits = [1 << i for i in range(Z.bit_length() - 1)]

    def total(v):
        return jnp.sum(v.astype(F32), axis=0)

    def rows_of(vecs):
        return jnp.concatenate([v.reshape(B, -1) for v in vecs], axis=1).astype(BF).reshape(B, -1, W)

    hr = w_down.shape[0] // B // 2
    pr = qr = 11 * hr // 16 // 16 * 16
    n_ot = D // B
    ur = hr + n_ot // 2

    (dn_give,) = wgrad_rows(act, up, 1 - c, Y, B)
    dn_got = mate(dn_give)
    (up_give,) = wgrad_cols(h2, after(du, dn_give), 1 - c, Y, B, W)
    up_got = mate(up_give)
    dy1, da, dctx, sums = ln2_call(after(dh2, up_give), middle, up, ln2_gain[None], w_out)

    def heads_of(s, d):
        return lax.dynamic_slice_in_dim(dctx, (((y + s) % Y) * 2 + flip(d)) * W, W, 1)

    def both(s):
        return jnp.concatenate([heads_of(s, 0), heads_of(s, 1)])

    do_y = [both(0)] + [shift(both(s), "y", Y, s) for s in range(1, Y)]

    (ot_give,) = wgrad_cols(ctx, after(da, do_y[0]), 1 - c, Y, B, W)
    ot_got = mate(ot_give)
    dnP, dnQ, dnR = wgrad_rows(act, after(up, ot_give), c, Y, B, dn_got, (pr, pr + qr))
    (dnP, dnQ, dnR), ot_got = lax.optimization_barrier(((dnP, dnQ, dnR), ot_got))
    t_y, t_x, t_r = over_y([([shaped(dnP)], 2)]), over_x([([shaped(dnQ)], 1)]), over_z([[shaped(dnR)]], 1)
    h2_, ctx_, da_ = after((h2, ctx, da), (t_y[2], t_x[2], t_r[2]))
    upQ, upP = wgrad_cols(h2_, du, c, Y, B, W, up_got, (ur,))
    do_y = after(do_y, (t_y[2], t_x[2], t_r[2]))
    do_c = mate(jnp.concatenate([v[F:] for v in do_y]))
    do_g = jnp.concatenate([b for s in range(Y) for b in (do_y[s][:F], do_c[s * F : (s + 1) * F])])
    (upP,) = wgrad_cols(ctx_, da_, c, Y, B, W, ot_got, (), upP)
    n_y, n_x = over_y([([shaped(upP)], 2)]), over_x([([shaped(upQ)], 1)])
    (t_y, t_x, t_r), (n_bufs, do_g) = hold([t_y, t_x, t_r], ((n_y[2], n_x[2]), do_g))
    (dnP,), (dnQ,), (dnR,) = finish(t_y), finish(t_x), finish(t_r)

    t_y, t_x, t_z, t_r = n_y, n_x, over_z([dnQ], 1), over_z([dnR], zbits[1])
    dnP = settle(dnP)
    early = rows_of([sums[2], sums[0], sums[1], sums[3], g_bu[0]])
    do_g = after(do_g, (n_bufs, t_z[2], t_r[2], early, dnP))
    (dqkv,) = attend(
        functools.partial(bwd_kernel, T, HG), (lst_k, cnt_k, base),
        [(qkv, (W, 0)), (qkv, (W, 1)), (qkv, (W, 2)), (ctx_g, None), (do_g, None), (lse, None), (lo, None), (hi, None)],
        [sds((S, 3 * W), BF)], [pltpu.VMEM((W, S), F32), pltpu.VMEM((HG, S), F32)], 20 * 10**9)
    (t_y, t_x, t_z, t_r), (dqkv, dnP) = hold([t_y, t_x, t_z, t_r], (dqkv, dnP))
    def rest(items, k):
        for bit in zbits[k:]:
            items = finish(over_z(items, bit))
        return items

    (upP,), (upQ,), (dnQ,), (dnR,) = finish(t_y), finish(t_x), finish(t_z), rest(finish(t_r), 2)

    def of_x(i):
        return jnp.concatenate([settle([lax.dynamic_index_in_dim(g, i, 1, keepdims=False) for g in terms])
                                for terms in ([dnP], upP)], axis=1)

    p_bufs, p_own = [of_x((xi + s) % X) for s in range(1, X)], of_x(xi)
    t_x = ([[p_own]], [shift(b, "x", X, s + 1) for s, b in enumerate(p_bufs)], p_bufs)
    t_a, t_b = over_z([upQ], 1), over_z([dnQ], zbits[1])
    dq_got = mate(dqkv.reshape(Y, 2, F, 3 * W)[:, 1].reshape(Y * F, 3 * W))
    qv = qgrad(h_all, after(dqkv, (p_bufs, t_a[2])), B)
    dh_far, dh_own, g_ln1 = dh_call(dqkv, after(dq_got, qv), w_g, w_m, x_all, Y)
    far = [shift(dh_far[s * F : (s + 1) * F], "y", Y, -s - 1) for s in range(Y - 1)]
    cols = total(dqkv)
    mine_only = jnp.arange(D) // W == group
    late = rows_of([g_ln1[0], g_ln1[1]] + [jnp.where(mine_only, jnp.tile(v, K), 0.0) for v in (cols[:W], cols[2 * W :])])
    vec = jnp.concatenate([late, early], axis=1)
    vec = jnp.pad(vec, ((0, 0), (0, -vec.shape[1] % 16), (0, 0)))
    qv = jnp.concatenate([qv, vec], axis=1).reshape(Z, X, -1, W)
    n_x = over_x([([qv], 1), (dnR, 1)])
    (t_x, t_a, t_b), n_bufs = hold([t_x, t_a, t_b], n_x[2])
    parts, upQ, dnQ = [p_own] + t_x[1], finish(t_a)[0], finish(t_b)[0]

    t_x = n_x
    t_a, t_b = over_z([parts], 1), over_z([upQ], zbits[1])
    result = down_call(after(act, (n_bufs, t_a[2], t_b[2])), w_down, middle, bias_down[None])
    (t_x, t_a, t_b), (far, result) = hold([t_x, t_a, t_b], (far, result))

    (qv, dnR), (parts,), (upQ,), (dnQ,) = finish(t_x), finish(t_a), rest(finish(t_b), 2), rest([dnQ], 2)

    t_a, t_b = over_z([qv], 1), over_z([parts], zbits[1])
    t_y = over_y([(head(dnQ), 0), (head(upQ), 0), (head(dnR), 0)])
    far, dh_own = after((far, dh_own), (t_a[2], t_b[2], t_y[2]))
    dh1 = sum((r.astype(F32) for r in far), dh_own.astype(F32))
    _, norm_back_one = jax.vjp(lambda v: layer_norm(v, ln1_gain, ln1_bias), flat_in)
    (dx,) = norm_back_one(dh1)
    grad_inputs = (dy1 + dx).reshape(1, F, D)
    (t_a, t_b, t_y), grad_inputs = hold([t_a, t_b, t_y], grad_inputs)
    (qv,), (parts,), (dnQ, upQ, dnR) = finish(t_a), rest(finish(t_b), 2), finish(t_y)

    t_b = over_z([qv], zbits[1])
    parts, dnQ, upQ, dnR = after((head(parts), dnQ, upQ, dnR), t_b[2])
    parts = settle(parts)
    first = jnp.concatenate([parts[:pr], settle(dnQ), settle(dnR), settle(upQ), parts[pr:]])

    def share_y(g):
        return [g] + [shift(g, "y", Y, s) for s in range(1, Y)]

    first_y = share_y(first)
    (t_b,), first_y = hold([t_b], first_y)
    (qv,) = rest(finish(t_b), 2)
    tail_y = share_y(settle(head(qv)))

    def share_c(got):
        got = jnp.stack(got)
        other = mate(got)

        def piece(yy, cc):
            i = (y - yy) % Y
            return jnp.where(cc == c, lax.dynamic_index_in_dim(got, i, 0, keepdims=False),
                             lax.dynamic_index_in_dim(other, i, 0, keepdims=False))

        return [[piece(yy, cc) for cc in range(2)] for yy in range(Y)]

    def by_columns(e, at, rows, chunks):
        return jnp.concatenate([e[yy][cc][at + k * rows : at + (k + 1) * rows] for cc in range(2) for yy in range(Y)
                                for k in range(chunks)], axis=1).astype(F32)

    first_e = share_c(first_y)
    n_dn = 2 * hr
    g_w_down = by_columns(first_e, 0, n_dn, 1)
    g_w_up = by_columns(first_e, n_dn, n_ot, 2 * ur // n_ot - 1)
    g_w_out = by_columns(first_e, n_dn + 2 * ur - n_ot, n_ot, 1)
    tail_y, g_w_down, g_w_up, g_w_out = lax.optimization_barrier((tail_y, g_w_down, g_w_up, g_w_out))
    tail_e = share_c(tail_y)
    g_w_qkv = jnp.concatenate([tail_e[yy][cc][p * n_ot : (p + 1) * n_ot] for p in range(3) for yy in range(Y)
                               for cc in range(2)], axis=1).astype(F32)
    at = 3 * n_ot
    flat = sum(tail_e[yy][cc][at:].astype(F32) for yy in range(Y) for cc in range(2)).reshape(-1)
    out, at = [], 0
    for n in (D, D, D, D, D, D, D, D, w_up.shape[1]):
        out.append(flat[at : at + n // B])
        at += n // B
    g_ln1g, g_ln1b, g_bq, g_bv, g_bo, g_ln2g, g_ln2b, g_bd, g_bu = out
    return (result.reshape(1, F, D), grad_inputs, g_ln1g, g_ln1b, g_w_qkv, g_bq, g_bv, g_w_out, g_bo, g_ln2g, g_ln2b,
            g_w_up, g_bu, g_w_down, g_bd)


def solution(mesh):
    batch, blk = mesh.shape["batch"], mesh.shape["blk"]
    Y = blk // 2
    X = Y if batch % Y == 0 else 1
    Z = batch // X
    fine = Mesh(mesh.devices.reshape(Z, X, Y, 2), ("z", "x", "y", "c"))
    rows, slots = ("z", "x"), ("y", "c")
    act = P(rows, slots, None)
    flat, mat = P(rows), P(rows, None)
    return jax.shard_map(
        functools.partial(shards, Z, X, Y),
        mesh=fine,
        in_specs=(act,) + (P(),) * 13 + (P(rows, None, None), act),
        out_specs=(act, act, flat, flat, mat, flat, flat, mat, flat, flat, flat, mat, flat, mat, flat),
        check_vma=False,
    )
```
